32 devices in a mesh: kpt: 2 (over y), dom: 8 (over z, x), band: 2 (over core).
Axes of the slice: x: 2, y: 2, z: 4, core: 2. Of those that a mesh axis runs over, the one named last changes fastest.
Arguments:
- wavefunctions: bfloat16 [65536, 256], P(('kpt', 'dom'), 'band'), parts along dimension 0, may hold values from -40 to 40
- bounds: float32 [4], P('kpt'), parts along dimension 0, may hold values from 0.5 to 23, as said below
- cell_matrix: bfloat16 [512, 512], replicated, may hold values from -1 to 4, as said below
- cell_scale: float32 [128], P('dom'), may hold values from 0.5 to 6
- potential: float32 [32768], P('dom'), may hold values from 0.5 to 3
- cell_nodes: int32 [128, 512], P('dom'), may hold values from 0 to 5119, as said below
- face_nodes: int32 [32, 256], P('dom'), may hold values from -1 to 4095, as said below
Outputs:
- rotated: float32 [65536, 256], P(('kpt', 'dom'), 'band'), parts along dimension 0
The draws below stay inside these ranges and needn't reach their ends.
There are 2 independent parts, one for each index of `kpt`. The reference program is written for one: setup_inputs(seed, part) draws one part's arguments, and reference() takes and returns one part's arrays. A program takes and returns all parts, laid end to end along the dimension named above; an argument that names none is the same for every part. Nothing has to cross between parts.
Inputs may be any that keep to these rules, and one draw needn't show every extreme that they name: `face_nodes`: row 4 d + o lists in its first slots the own nodes (0 to 4095 of block d) sent to block d + (1, -1, 2, -2)[o]; the remaining slots hold -1; at least one row whose neighbour block exists is full. `cell_nodes`: entries below 4096 are own nodes of the cell's block, the others ghost rows of its extended block. bounds[1] exceeds bounds[0] by 8 or more. `cell_matrix`: symmetric.
All inputs are finite; a program needn't handle non-finite values.
Results may differ from the reference program's by a relative error of at most 0.0054.
Values may be sent and summed in bfloat16 or wider, within the bound.
No kernel may reach another device: no remote copies, remote signals or barrier semaphores. Data moves between devices by JAX's collectives and lax.ppermute only.
A program may use at most 64 MiB of HBM per device.

```python
import math
import jax
import jax.numpy as jnp
from jax import lax

NC = 512
BANDS = 256
NODE_DEV = 4096
CELLS = 16
SLOT = 256
NODES = 32768
CELLS_ALL = 128
FACE_ROWS = 32


def draw_wavefunctions(key, part):
    key_one, key_two, key_three = jax.random.split(jax.random.fold_in(key, 5), 3)
    col_scale = jnp.exp(jax.random.uniform(key_two, (BANDS,), jnp.float32, math.log(0.3), math.log(3.0)))
    row_scale = jnp.exp(jax.random.uniform(key_three, (NODES,), jnp.float32, math.log(0.3), math.log(3.0)))
    values = jax.random.truncated_normal(key_one, -4.0, 4.0, (NODES, BANDS), jnp.float32)
    return (values * row_scale[:, None] * col_scale[None, :]).astype(jnp.bfloat16)


def draw_bounds(key, part):
    draws = jax.random.uniform(jax.random.fold_in(key, 21), (2,), jnp.float32)
    low_end = 0.5 + 2.5 * draws[0]
    high_end = low_end + 8.0 + 12.0 * draws[1]
    return jnp.stack([low_end, high_end]).astype(jnp.float32)


def draw_cell_matrix(key, part):
    inner = jax.random.fold_in(key, 31)
    values = jax.random.truncated_normal(inner, -4.0, 4.0, (NC, NC), jnp.float32)
    matrix = (values + values.T) / math.sqrt(2.0 * NC) + 2.5 * jnp.eye(NC, dtype=jnp.float32)
    return matrix.astype(jnp.bfloat16)


def draw_cell_scale(key, part):
    inner = jax.random.fold_in(key, 41)
    position = jnp.arange(CELLS_ALL).astype(jnp.float32)
    rising = jnp.exp(math.log(3.0) * position / max(CELLS_ALL - 1, 1))
    factor = jnp.exp(jax.random.uniform(inner, (CELLS_ALL,), jnp.float32, math.log(0.5), math.log(2.0)))
    return (rising * factor).astype(jnp.float32)


def draw_cell_nodes(key, part):
    key_one, key_two, key_three, key_four, key_five = jax.random.split(jax.random.fold_in(key, 51), 5)
    cell_keys = jax.random.split(key_one, CELLS_ALL)
    orders = jax.vmap(lambda single: jax.random.permutation(single, NC))(cell_keys).astype(jnp.int32)
    base = jnp.arange(CELLS_ALL, dtype=jnp.int32) % CELLS * (NC // 2)
    owned = (base[:, None] + orders) % NODE_DEV
    chosen = jax.random.randint(key_two, (CELLS_ALL, NC), 0, 4) == 0
    ghost_rows = NODE_DEV + jax.random.randint(key_three, (CELLS_ALL, NC), 0, 4 * SLOT)
    result = jnp.where(chosen, ghost_rows, owned).astype(jnp.int32).reshape(-1)
    total = CELLS_ALL * NC
    low_spot = jax.random.randint(key_four, (), 0, total // 2)
    high_spot = jax.random.randint(key_five, (), total // 2, total)
    result = result.at[low_spot].set(0)
    result = result.at[high_spot].set(NODE_DEV + 4 * SLOT - 1)
    return result.reshape(CELLS_ALL, NC).astype(jnp.int32)


def draw_face_nodes(key, part):
    key_one, key_two, key_three, key_four = jax.random.split(jax.random.fold_in(key, 61), 4)
    lengths = jax.random.randint(key_one, (FACE_ROWS,), SLOT // 4, SLOT)
    block_pick = jax.random.randint(key_two, (), 2, FACE_ROWS // 4 - 2)
    offset_pick = jax.random.randint(key_three, (), 0, 4)
    full_row = 4 * block_pick + offset_pick
    lengths = jnp.where(jnp.arange(FACE_ROWS, dtype=jnp.int32) == full_row, SLOT, lengths)
    entries = jax.random.randint(key_four, (FACE_ROWS, SLOT), 0, NODE_DEV)
    entries = entries.at[full_row, 0].set(NODE_DEV - 1)
    slot_ids = jnp.arange(SLOT, dtype=jnp.int32)[None, :]
    return jnp.where(slot_ids < lengths[:, None], entries, -1).astype(jnp.int32)


def block_scale(key, shape, cuts, low, top_value):
    def one(axis_at, parts):
        steps = jax.random.uniform(jax.random.fold_in(jax.random.fold_in(key, 6), axis_at), (parts,), jnp.float32, low / len(cuts), top_value / len(cuts))
        return jnp.repeat(jnp.exp(steps), shape[axis_at] // parts).reshape((-1,) + (1,) * (len(shape) - axis_at - 1))

    gain = one(*cuts[0])
    for cut in cuts[1:]:
        gain = gain * one(*cut)
    return gain


def setup_inputs(seed: int = 0, part: int = 0) -> dict:
    seeds = jax.random.split(jax.random.key(seed), 8)
    own_keys = jax.random.split(jax.random.fold_in(seeds[7], part), 8)
    return {
        "wavefunctions": draw_wavefunctions(jax.random.fold_in(jax.random.fold_in(seeds[7], part), 71), part),
        "bounds": draw_bounds(jax.random.fold_in(jax.random.fold_in(seeds[7], part), 71), part),
        "cell_matrix": draw_cell_matrix(jax.random.fold_in(seeds[7], 71), part),
        "cell_scale": draw_cell_scale(jax.random.fold_in(seeds[7], 71), part),
        "potential": jnp.clip(0.5 + 2.5 * jax.random.uniform(seeds[4], (NODES,), jnp.float32) ** block_scale(seeds[4], (NODES,), ((0, 8),), -0.2, 0.2), 0.5, 3.0),
        "cell_nodes": draw_cell_nodes(jax.random.fold_in(seeds[7], 71), part),
        "face_nodes": draw_face_nodes(jax.random.fold_in(seeds[7], 71), part),
    }


peer_offsets = (1, -1, 2, -2)

def shift_devices(blocks, offset):
    padding = jnp.zeros_like(blocks[:abs(offset)])
    if offset > 0:
        return jnp.concatenate([padding, blocks[:-offset]], 0)
    return jnp.concatenate([blocks[-offset:], padding], 0)

def apply_operator(vectors, cell_matrix, cell_scale, potential, cell_nodes, face_nodes):
    node_blocks = NODES // NODE_DEV
    blocks = vectors.reshape(node_blocks, NODE_DEV, BANDS)
    faces = face_nodes.reshape(node_blocks, 4, SLOT)
    filled = faces >= 0
    safe_index = jnp.maximum(faces, 0)
    outgoing = jax.vmap(lambda block_rows, picks: block_rows[picks])(blocks, safe_index)
    outgoing = jnp.where(filled[..., None], outgoing, jnp.zeros((), vectors.dtype))
    ghosts = jnp.stack([shift_devices(outgoing[:, idx], peer_offsets[idx]) for idx in range(4)], 1)
    extended = jnp.concatenate([blocks, ghosts.reshape(node_blocks, 4 * SLOT, BANDS)], 1)
    cell_maps = cell_nodes.reshape(node_blocks, CELLS, NC)
    scales = cell_scale.reshape(node_blocks, CELLS)
    stiffness = cell_matrix.astype(jnp.float32)

    def cell_pass(device_items):
        ext_rows, maps, scale_row = device_items
        gathered = ext_rows[maps].astype(jnp.float32)
        products = jnp.einsum('ij,cjk->cik', stiffness, gathered) * scale_row[:, None, None]
        return jax.ops.segment_sum(products.reshape(-1, BANDS), maps.reshape(-1), num_segments=NODE_DEV + 4 * SLOT)
    summed = lax.map(cell_pass, (extended, cell_maps, scales))
    owned = summed[:, :NODE_DEV]
    ghost_acc = summed[:, NODE_DEV:].reshape(node_blocks, 4, SLOT, BANDS)
    returned = jnp.stack([shift_devices(ghost_acc[:, idx], -peer_offsets[idx]) for idx in range(4)], 1)
    targets = jnp.where(filled, faces, NODE_DEV).astype(jnp.int32)

    def add_back(owned_rows, returned_rows, target_rows):
        extra = jax.ops.segment_sum(returned_rows.reshape(-1, BANDS), target_rows.reshape(-1), num_segments=NODE_DEV + 1)
        return owned_rows + extra[:NODE_DEV]
    owned = jax.vmap(add_back)(owned, returned, targets)
    return owned.reshape(NODES, BANDS) + potential[:, None] * vectors.astype(jnp.float32)

def reference(wavefunctions, bounds, cell_matrix, cell_scale, potential, cell_nodes, face_nodes):
    center = (bounds[0] + bounds[1]) / 2.0
    half_width = (bounds[1] - bounds[0]) / 2.0
    wave_wide = wavefunctions.astype(jnp.float32)
    image_one = apply_operator(wavefunctions, cell_matrix, cell_scale, potential, cell_nodes, face_nodes)
    degree_one = ((image_one - center * wave_wide) / half_width).astype(jnp.bfloat16)
    image_two = apply_operator(degree_one, cell_matrix, cell_scale, potential, cell_nodes, face_nodes)
    degree_two = (2.0 * (image_two - center * degree_one.astype(jnp.float32)) / half_width - wave_wide).astype(jnp.bfloat16)
    margin = jnp.dot(degree_two.T.astype(jnp.float32), degree_two.astype(jnp.float32), preferred_element_type=jnp.float32) / NODES
    factor = jnp.linalg.cholesky(margin)
    inverse = lax.linalg.triangular_solve(factor, jnp.eye(BANDS, dtype=factor.dtype), left_side=True, lower=True)
    return jnp.dot(degree_two.astype(jnp.float32), inverse.T, precision=lax.Precision.HIGHEST)
```

```python
import functools

import jax
import jax.numpy as jnp
from jax import lax
from jax.experimental import pallas as pl
from jax.experimental.pallas import tpu as pltpu
from jax.sharding import PartitionSpec as P

peer_offsets = (1, -1, 2, -2)
f32, bf16 = jnp.float32, jnp.bfloat16
LANES, GROUP, PANEL = 128, 8, 8
vmem = pl.BlockSpec(memory_space=pltpu.VMEM)
smem = pl.BlockSpec(memory_space=pltpu.SMEM)
params = pltpu.CompilerParams(vmem_limit_bytes=58 * 2**20)


def passed_along(value, axis, by):
    size = lax.axis_size(axis)
    pairs = [(i, i + by) for i in range(size) if 0 <= i + by < size]
    return lax.ppermute(value, axis, pairs)


def gather_faces(faces_ref, table_ref, rows_ref, out_refs):
    spare = table_ref.shape[0] - 8
    slots = out_refs[0].shape[0]

    def body(step, _):
        base = step * 16
        for u in range(16):
            face = faces_ref[base + u]
            face = jnp.where(face < 0, spare, face)
            rows_ref[pl.ds(base + u, 1), :] = table_ref[pl.ds(face, 1), :]
        return 0

    lax.fori_loop(0, 4 * slots // 16, body, 0)
    for o in range(4):
        out_refs[o][...] = rows_ref[o * slots : (o + 1) * slots, :].astype(bf16)


def face_kernel(faces_ref, vec_ref, o0, o1, o2, o3, table_ref, rows_ref):
    nodes = vec_ref.shape[0]
    table_ref[0:nodes, :] = vec_ref[...].astype(f32)
    table_ref[nodes : nodes + 8, :] = jnp.zeros((8, LANES), f32)
    gather_faces(faces_ref, table_ref, rows_ref, (o0, o1, o2, o3))


def send_faces(faces, vectors):
    nodes, slots = vectors.shape[0], faces.shape[0] // 4
    return pl.pallas_call(
        face_kernel,
        out_shape=[jax.ShapeDtypeStruct((slots, LANES), bf16)] * 4,
        in_specs=[smem, vmem],
        out_specs=[vmem] * 4,
        scratch_shapes=[
            pltpu.VMEM((nodes + 8, LANES), f32),
            pltpu.VMEM((4 * slots, LANES), f32),
        ],
        compiler_params=params,
    )(faces, vectors)


def cells_kernel(
    maps_ref, scale_ref, matrix_ref, vec_ref, h0, h1, h2, h3, own_ref, g0, g1, g2, g3,
    ext_ref, in_ref, out_ref, *acc
):
    nodes, slots = vec_ref.shape[0], h0.shape[0]
    size = matrix_ref.shape[0]
    ext = nodes + 4 * slots
    ext_ref[0:nodes, :] = vec_ref[...].astype(f32)
    for o, ghost in enumerate((h0, h1, h2, h3)):
        ext_ref[nodes + o * slots : nodes + (o + 1) * slots, :] = ghost[...].astype(f32)

    def clear(step, _):
        rows = pl.ds(pl.multiple_of(step * 64, 64), 64)
        for a in acc:
            a[rows, :] = jnp.zeros((64, LANES), f32)
        return 0

    lax.fori_loop(0, ext // 64, clear, 0)
    cells = scale_ref.shape[0]
    for first in range(0, cells, GROUP):

        def gather(step, _):
            base = step * 8
            for u in range(8):
                for k in range(GROUP):
                    row = maps_ref[(first + k) * size + base + u]
                    in_ref[k, pl.ds(base + u, 1), :] = ext_ref[pl.ds(row, 1), :]
            return 0

        lax.fori_loop(0, size // 8, gather, 0)
        for k in range(0, GROUP, 2):
            pair = jnp.concatenate([in_ref[k].astype(bf16), in_ref[k + 1].astype(bf16)], 1)
            product = jnp.dot(matrix_ref[...], pair, preferred_element_type=f32)
            out_ref[k] = product[:, :LANES] * scale_ref[first + k]
            out_ref[k + 1] = product[:, LANES:] * scale_ref[first + k + 1]

        def scatter(step, _):
            base = step * 8
            for u in range(8):
                rows = [maps_ref[(first + k) * size + base + u] for k in range(GROUP)]
                sums = [
                    acc[k][pl.ds(rows[k], 1), :] + out_ref[k, pl.ds(base + u, 1), :]
                    for k in range(GROUP)
                ]
                for k in range(GROUP):
                    acc[k][pl.ds(rows[k], 1), :] = sums[k]
            return 0

        lax.fori_loop(0, size // 8, scatter, 0)

    def total(start):
        rows = pl.ds(start, 64)
        parts = [a[rows, :] for a in acc]
        while len(parts) > 1:
            parts = [parts[i] + parts[i + 1] for i in range(0, len(parts), 2)]
        return parts[0]

    def reduce_own(step, _):
        start = pl.multiple_of(step * 64, 64)
        own_ref[pl.ds(start, 64), :] = total(start)
        return 0

    lax.fori_loop(0, nodes // 64, reduce_own, 0)
    for o, ghost in enumerate((g0, g1, g2, g3)):
        for r in range(0, slots, 64):
            ghost[r : r + 64, :] = total(nodes + o * slots + r)


def apply_cells(maps, scale, matrix, vectors, ghosts):
    nodes, slots, size = vectors.shape[0], ghosts[0].shape[0], matrix.shape[0]
    ext = nodes + 4 * slots
    return pl.pallas_call(
        cells_kernel,
        out_shape=[jax.ShapeDtypeStruct((nodes, LANES), f32)]
        + [jax.ShapeDtypeStruct((slots, LANES), f32)] * 4,
        in_specs=[smem, smem] + [vmem] * 6,
        out_specs=[vmem] * 5,
        scratch_shapes=[
            pltpu.VMEM((ext, LANES), f32),
            pltpu.VMEM((GROUP, size, LANES), f32),
            pltpu.VMEM((GROUP, size, LANES), f32),
        ]
        + [pltpu.VMEM((ext, LANES), f32)] * GROUP,
        compiler_params=params,
    )(maps, scale, matrix, vectors, *ghosts)


def add_returned(faces_ref, returned, acc):
    spare = acc[0].shape[0] - 8
    slots = returned[0].shape[0]
    for a in acc:
        a[...] = jnp.zeros(a.shape, f32)

    def body(step, _):
        base = step * 4
        for u in range(4):
            rows = [faces_ref[o * slots + base + u] for o in range(4)]
            rows = [jnp.where(row < 0, spare, row) for row in rows]
            sums = [
                acc[o][pl.ds(rows[o], 1), :] + returned[o][pl.ds(base + u, 1), :]
                for o in range(4)
            ]
            for o in range(4):
                acc[o][pl.ds(rows[o], 1), :] = sums[o]
        return 0

    lax.fori_loop(0, slots // 4, body, 0)


def first_kernel(
    faces_ref, inv_ref, own_ref, coef_ref, vec_ref, r0, r1, r2, r3,
    out_ref, o0, o1, o2, o3, table_ref, rows_ref, *acc
):
    nodes = vec_ref.shape[0]
    add_returned(faces_ref, (r0, r1, r2, r3), acc)

    def combine(step, _):
        rows = pl.ds(pl.multiple_of(step * 64, 64), 64)
        image = own_ref[rows, :] + (
            (acc[0][rows, :] + acc[1][rows, :]) + (acc[2][rows, :] + acc[3][rows, :])
        )
        value = image * inv_ref[0] + coef_ref[rows, :] * vec_ref[rows, :].astype(f32)
        value = value.astype(bf16)
        out_ref[rows, :] = value
        table_ref[rows, :] = value.astype(f32)
        return 0

    lax.fori_loop(0, nodes // 64, combine, 0)
    table_ref[nodes : nodes + 8, :] = jnp.zeros((8, LANES), f32)
    gather_faces(faces_ref, table_ref, rows_ref, (o0, o1, o2, o3))


def second_kernel(
    faces_ref, inv_ref, own_ref, coef_ref, vec_ref, old_ref, r0, r1, r2, r3, out_ref, *acc
):
    nodes = vec_ref.shape[0]
    add_returned(faces_ref, (r0, r1, r2, r3), acc)

    def combine(step, _):
        rows = pl.ds(pl.multiple_of(step * 64, 64), 64)
        image = own_ref[rows, :] + (
            (acc[0][rows, :] + acc[1][rows, :]) + (acc[2][rows, :] + acc[3][rows, :])
        )
        value = image * inv_ref[0] + coef_ref[rows, :] * vec_ref[rows, :].astype(f32)
        out_ref[rows, :] = (2.0 * value - old_ref[rows, :].astype(f32)).astype(bf16)
        return 0

    lax.fori_loop(0, nodes // 64, combine, 0)


def finish_first(faces, inv, own, coef, vectors, returned):
    nodes, slots = vectors.shape[0], faces.shape[0] // 4
    return pl.pallas_call(
        first_kernel,
        out_shape=[jax.ShapeDtypeStruct((nodes, LANES), bf16)]
        + [jax.ShapeDtypeStruct((slots, LANES), bf16)] * 4,
        in_specs=[smem, smem] + [vmem] * 7,
        out_specs=[vmem] * 5,
        scratch_shapes=[
            pltpu.VMEM((nodes + 8, LANES), f32),
            pltpu.VMEM((4 * slots, LANES), f32),
        ]
        + [pltpu.VMEM((nodes + 8, LANES), f32)] * 4,
        compiler_params=params,
    )(faces, inv, own, coef, vectors, *returned)


def finish_second(faces, inv, own, coef, vectors, old, returned):
    nodes = vectors.shape[0]
    return pl.pallas_call(
        second_kernel,
        out_shape=jax.ShapeDtypeStruct((nodes, LANES), bf16),
        in_specs=[smem, smem] + [vmem] * 8,
        out_specs=vmem,
        scratch_shapes=[pltpu.VMEM((nodes + 8, LANES), f32)] * 4,
        compiler_params=params,
    )(faces, inv, own, coef, vectors, old, *returned)


def margin_kernel(band_ref, own_ref, other_ref, out_ref):
    half = LANES // 2
    nt = functools.partial(
        lax.dot_general,
        dimension_numbers=(((0,), (0,)), ((), ())),
        preferred_element_type=f32,
    )

    def write(low, high, band):
        low_rows = low[:, band * half : (band + 1) * half]
        high_rows = high[:, band * half : (band + 1) * half]
        block = nt(low_rows, low)
        cross = nt(low_rows, high)
        tail = nt(high_rows, high)
        row = lax.broadcasted_iota(jnp.int32, (half, LANES), 0) + band * half
        col = lax.broadcasted_iota(jnp.int32, (half, LANES), 1)
        out_ref[0:half, :] = jnp.where(col >= row, block, tail)
        out_ref[half : 2 * half, :] = cross
        diag = jnp.sum(jnp.where(col == row, tail, 0.0), 0, keepdims=True)
        out_ref[2 * half : 2 * half + 8, :] = jnp.broadcast_to(diag, (8, LANES))

    @pl.when(band_ref[0] == 0)
    def _():
        write(own_ref[...], other_ref[...], 0)

    @pl.when(band_ref[0] != 0)
    def _():
        write(other_ref[...], own_ref[...], 1)


def margin_rows(band, own, other):
    return pl.pallas_call(
        margin_kernel,
        out_shape=jax.ShapeDtypeStruct((LANES + 8, LANES), f32),
        in_specs=[smem, vmem, vmem],
        out_specs=vmem,
        compiler_params=params,
    )(band, own, other)


def split_three(x):
    high = x.astype(bf16)
    rest = x - high.astype(f32)
    mid = rest.astype(bf16)
    return high, mid, (rest - mid.astype(f32)).astype(bf16)


def invert_factor(work_ref, panel_ref):
    total = work_ref.shape[0]
    col = lax.broadcasted_iota(jnp.int32, (PANEL, total), 1)
    row = lax.broadcasted_iota(jnp.int32, (PANEL, total), 0)

    def step(p, start_row):
        first = pl.multiple_of(p * PANEL, PANEL)
        rows = work_ref[pl.ds(first, PANEL), :]
        halves = [rows[:, h * LANES : (h + 1) * LANES] for h in range(total // LANES)]
        block = halves[start_row // LANES]
        block = pltpu.roll(block, lax.rem(total - first, LANES), 1)
        columns = [
            jnp.broadcast_to(block[:, k : k + 1], (PANEL, LANES)) for k in range(PANEL)
        ]
        entry = {
            (i, k): columns[k][i : i + 1, :] for i in range(PANEL) for k in range(i + 1)
        }
        panel = jnp.where((col >= first) & (col < first + PANEL), 0.0, rows)
        panel = jnp.where(col == row + first, 1.0, panel)
        done = []
        for k in range(PANEL):
            pivot = entry[k, k]
            scale = lax.rsqrt(pivot)
            scale = scale * (1.5 - 0.5 * pivot * scale * scale)
            for i in range(k + 1, PANEL):
                entry[i, k] = entry[i, k] * scale
            for i in range(k + 1, PANEL):
                for m in range(k + 1, i + 1):
                    entry[i, m] = entry[i, m] - entry[i, k] * entry[m, k]
            line = panel[k : k + 1, :]
            wide = lambda x: jnp.concatenate([x] * (total // LANES), 1)
            for m in range(k):
                line = line - wide(entry[k, m]) * done[m]
            line = line * wide(scale)
            done.append(line)
            panel_ref[k : k + 1, :] = line
        panel = panel_ref[...]
        right = jnp.where(col >= first + PANEL, panel, 0.0)
        ah, am, al = split_three(right)
        bh, bm, bl = split_three(panel)
        lhs = jnp.concatenate([x.astype(f32) for x in (ah, ah, am, am, ah, al)], 0).astype(bf16)
        rhs = jnp.concatenate([x.astype(f32) for x in (bh, bm, bh, bm, bl, bh)], 0).astype(bf16)
        update = lax.dot_general(
            lhs[:, start_row:], rhs, (((0,), (0,)), ((), ())), preferred_element_type=f32
        )
        below = work_ref[start_row:, :]
        big = lax.broadcasted_iota(jnp.int32, below.shape, 1)
        inside = (big >= first) & (big < first + PANEL)
        work_ref[start_row:, :] = jnp.where(inside, 0.0, below) - update
        work_ref[pl.ds(first, PANEL), :] = panel

    per = LANES // PANEL
    for h in range(total // LANES):
        lax.fori_loop(h * per, (h + 1) * per, lambda p, _: (step(p, h * LANES), 0)[1], 0)


def rotate_kernel(
    band_ref, count_ref, mine_ref, theirs_ref, own_ref, other_ref, out_ref, work_ref, panel_ref
):
    half = LANES // 2
    band = band_ref[0]
    mine, theirs = mine_ref[...] * count_ref[0], theirs_ref[...] * count_ref[0]
    top = jnp.where(band == 0, mine, theirs)
    bottom = jnp.where(band == 0, theirs, mine)
    packed = jnp.concatenate([top[0:half], bottom[0:half]], 0)
    cross = jnp.concatenate([top[half:LANES], bottom[half:LANES]], 0)
    diag = top[LANES : LANES + 1] + bottom[LANES : LANES + 1]
    flipped = packed.T
    row = lax.broadcasted_iota(jnp.int32, (LANES, LANES), 0)
    col = lax.broadcasted_iota(jnp.int32, (LANES, LANES), 1)
    work_ref[0:LANES, 0:LANES] = jnp.where(col >= row, packed, flipped)
    work_ref[0:LANES, LANES:] = cross
    work_ref[LANES:, 0:LANES] = cross.T
    tail = jnp.where(col < row, packed, flipped)
    work_ref[LANES:, LANES:] = jnp.where(col == row, jnp.broadcast_to(diag, tail.shape), tail)
    invert_factor(work_ref, panel_ref)
    lower = jnp.where(col <= row, 1.0, 0.0)
    first = work_ref[0:LANES, 0:LANES] * lower
    last = work_ref[LANES:, LANES:] * lower
    corner = work_ref[LANES:, 0:LANES]
    from_own = jnp.where(band == 0, first, last)
    from_other = jnp.where(band == 0, jnp.zeros_like(corner), corner)
    weights = jnp.concatenate([from_own, from_other], 1)
    high = weights.astype(bf16)
    low = (weights - high.astype(f32)).astype(bf16)
    weights = jnp.concatenate([high, low], 0)
    chunk = 512

    def body(step, _):
        rows = pl.ds(pl.multiple_of(step * chunk, chunk), chunk)
        both = jnp.concatenate([own_ref[rows, :], other_ref[rows, :]], 1)
        product = lax.dot_general(
            both, weights, (((1,), (1,)), ((), ())), preferred_element_type=f32
        )
        out_ref[rows, :] = product[:, :LANES] + product[:, LANES:]
        return 0

    lax.fori_loop(0, own_ref.shape[0] // chunk, body, 0)


def rotate(band, inv_count, mine, theirs, own, other):
    return pl.pallas_call(
        rotate_kernel,
        out_shape=jax.ShapeDtypeStruct(own.shape, f32),
        in_specs=[smem, smem] + [vmem] * 4,
        out_specs=vmem,
        scratch_shapes=[pltpu.VMEM((2 * LANES, 2 * LANES), f32), pltpu.VMEM((PANEL, 2 * LANES), f32)],
        compiler_params=params,
    )(band, inv_count, mine, theirs, own, other)


def summed_over(value, axis):
    size = lax.axis_size(axis)
    if size & (size - 1):
        return lax.psum(value, axis)
    stride = 1
    while stride < size:
        value = value + lax.ppermute(value, axis, [(i, i ^ stride) for i in range(size)])
        stride *= 2
    return value


def swapped(value):
    return lax.ppermute(value, "band", [(0, 1), (1, 0)])


def on_device(wavefunctions, bounds, cell_matrix, cell_scale, potential, cell_nodes, face_nodes):
    nodes, columns = wavefunctions.shape
    maps = cell_nodes.reshape(-1)
    faces = face_nodes.reshape(-1)
    center = (bounds[0] + bounds[1]) / 2.0
    half_width = (bounds[1] - bounds[0]) / 2.0
    inv = (1.0 / half_width).reshape(1)
    coef = jnp.broadcast_to(((potential - center) / half_width)[:, None], (nodes, columns))

    def forward(blocks):
        return [passed_along(blocks[o], "dom", peer_offsets[o]) for o in range(4)]

    def backward(blocks):
        return [passed_along(blocks[o], "dom", -peer_offsets[o]) for o in range(4)]

    ghosts = forward(send_faces(faces, wavefunctions))
    own, *sums = apply_cells(maps, cell_scale, cell_matrix, wavefunctions, ghosts)
    degree_one, *blocks = finish_first(faces, inv, own, coef, wavefunctions, backward(sums))
    own, *sums = apply_cells(maps, cell_scale, cell_matrix, degree_one, forward(blocks))
    degree_two = finish_second(
        faces, inv, own, coef, degree_one, wavefunctions, backward(sums)
    )
    other = swapped(degree_two)
    band = lax.axis_index("band").astype(jnp.int32).reshape(1)
    mine = summed_over(margin_rows(band, degree_two, other), "dom")
    inv_count = jnp.full((1,), 1.0 / (nodes * lax.axis_size("dom")), f32)
    return rotate(band, inv_count, mine, swapped(mine), degree_two, other)


def solution(mesh):
    return jax.shard_map(
        on_device,
        mesh=mesh,
        in_specs=(
            P(("kpt", "dom"), "band"),
            P("kpt"),
            P(),
            P("dom"),
            P("dom"),
            P("dom", None),
            P("dom", None),
        ),
        out_specs=P(("kpt", "dom"), "band"),
        check_vma=False,
    )
```

```python
import functools

import jax
import jax.numpy as jnp
from jax import lax
from jax.experimental import pallas as pl
from jax.experimental.pallas import tpu as pltpu
from jax.sharding import PartitionSpec as P

peer_offsets = (1, -1, 2, -2)
f32, bf16 = jnp.float32, jnp.bfloat16
LANES, GROUP, PANEL = 128, 8, 16
vmem = pl.BlockSpec(memory_space=pltpu.VMEM)
smem = pl.BlockSpec(memory_space=pltpu.SMEM)
hbm = pl.BlockSpec(memory_space=pltpu.HBM)


def grant(mib):
    return pltpu.CompilerParams(vmem_limit_bytes=mib * 2**20)


def exchange_pairs(size):
    first = ([i for i in range(size) if i % 2 == 0], 1)
    second = ([i for i in range(size) if i % 2 == 1], 1)
    third = ([i for i in range(size) if i % 4 < 2], 2)
    fourth = ([i for i in range(size) if i % 4 >= 2], 2)
    return [
        [pair for i in starts if i + by < size for pair in ((i, i + by), (i + by, i))]
        for starts, by in (first, second, third, fourth)
    ]


def face_of(side_ref, q):
    side = side_ref[q // 2]
    return (q // 2) * 2 + (side if q % 2 == 0 else 1 - side)


def gather_faces(side_ref, faces_ref, table_ref, rows_ref, out_refs):
    slots = out_refs[0].shape[0]
    for q in range(4):
        offset = face_of(side_ref, q) * slots

        def body(step, _):
            base = step * 64
            for u in range(64):
                face = faces_ref[offset + base + u]
                rows_ref[pl.ds(base + u, 1), :] = table_ref[pl.ds(face, 1), :]
            return 0

        lax.fori_loop(0, slots // 64, body, 0)
        out_refs[q][...] = rows_ref[...].astype(bf16)


def face_kernel(side_ref, faces_ref, vec_ref, o0, o1, o2, o3, table_ref, rows_ref):
    nodes = vec_ref.shape[0]
    table_ref[0:nodes, :] = vec_ref[...].astype(f32)
    table_ref[nodes : nodes + 8, :] = jnp.zeros((8, LANES), f32)
    gather_faces(side_ref, faces_ref, table_ref, rows_ref, (o0, o1, o2, o3))


def send_faces(side, faces, vectors):
    nodes, slots = vectors.shape[0], faces.shape[0] // 4
    return pl.pallas_call(
        face_kernel,
        out_shape=[jax.ShapeDtypeStruct((slots, LANES), bf16)] * 4,
        in_specs=[smem, smem, vmem],
        out_specs=[vmem] * 4,
        scratch_shapes=[
            pltpu.VMEM((nodes + 8, LANES), f32),
            pltpu.VMEM((slots, LANES), f32),
        ],
        compiler_params=grant(8),
    )(side, faces, vectors)


def cells_kernel(
    outer, side_ref, maps_ref, scale_ref, whole_ref, given_ref, h0, h1, h2, h3,
    own_ref, g0, g1, g2, g3, matrix_ref, ext_ref, in_ref, out_ref, sems, *rest
):
    acc = rest[:GROUP]
    nodes, slots = given_ref.shape[0], h0.shape[0]
    size = matrix_ref.shape[0]
    ext = nodes + 4 * slots
    fetch = pltpu.make_async_copy(whole_ref, matrix_ref, sems.at[0])
    if outer:
        vec_ref = rest[GROUP]
        load = pltpu.make_async_copy(given_ref, vec_ref, sems.at[1])
        load.start()
    else:
        vec_ref = given_ref
    fetch.start()
    for q, ghost in enumerate((h0, h1, h2, h3)):
        start = pl.multiple_of(nodes + (face_of(side_ref, q) ^ 1) * slots, slots)
        ext_ref[pl.ds(start, slots), :] = ghost[...].astype(f32)

    def clear(step, _):
        rows = pl.ds(pl.multiple_of(step * 64, 64), 64)
        for a in acc:
            a[rows, :] = jnp.zeros((64, LANES), f32)
        return 0

    lax.fori_loop(0, ext // 64, clear, 0)
    if outer:
        load.wait()
    ext_ref[0:nodes, :] = vec_ref[...].astype(f32)
    cells = scale_ref.shape[0]
    for first in range(0, cells, GROUP):

        def gather(step, _):
            base = step * 8
            for u in range(8):
                for k in range(GROUP):
                    row = maps_ref[(first + k) * size + base + u]
                    in_ref[k, pl.ds(base + u, 1), :] = ext_ref[pl.ds(row, 1), :]
            return 0

        lax.fori_loop(0, size // 8, gather, 0)
        if first == 0:
            fetch.wait()
        for k in range(0, GROUP, 2):
            pair = jnp.concatenate([in_ref[k].astype(bf16), in_ref[k + 1].astype(bf16)], 1)
            product = jnp.dot(matrix_ref[...], pair, preferred_element_type=f32)
            out_ref[k] = product[:, :LANES] * scale_ref[first + k]
            out_ref[k + 1] = product[:, LANES:] * scale_ref[first + k + 1]

        def scatter(step, _):
            base = step * 8
            for u in range(8):
                rows = [maps_ref[(first + k) * size + base + u] for k in range(GROUP)]
                sums = [
                    acc[k][pl.ds(rows[k], 1), :] + out_ref[k, pl.ds(base + u, 1), :]
                    for k in range(GROUP)
                ]
                for k in range(GROUP):
                    acc[k][pl.ds(rows[k], 1), :] = sums[k]
            return 0

        lax.fori_loop(0, size // 8, scatter, 0)

    def total(start):
        rows = pl.ds(start, 64)
        parts = [a[rows, :] for a in acc]
        while len(parts) > 1:
            parts = [parts[i] + parts[i + 1] for i in range(0, len(parts), 2)]
        return parts[0]

    def reduce_own(step, _):
        start = pl.multiple_of(step * 64, 64)
        own_ref[pl.ds(start, 64), :] = total(start)
        return 0

    lax.fori_loop(0, nodes // 64, reduce_own, 0)
    for q, ghost in enumerate((g0, g1, g2, g3)):
        start = pl.multiple_of(nodes + (face_of(side_ref, q) ^ 1) * slots, slots)
        for r in range(0, slots, 64):
            ghost[r : r + 64, :] = total(pl.multiple_of(start + r, 64))


def apply_cells(side, maps, scale, matrix, vectors, ghosts, outer):
    nodes, slots, size = vectors.shape[0], ghosts[0].shape[0], matrix.shape[0]
    ext = nodes + 4 * slots
    return pl.pallas_call(
        functools.partial(cells_kernel, outer),
        out_shape=[jax.ShapeDtypeStruct((nodes, LANES), f32)]
        + [jax.ShapeDtypeStruct((slots, LANES), f32)] * 4,
        in_specs=[smem, smem, smem, hbm, hbm if outer else vmem] + [vmem] * 4,
        out_specs=[vmem] * 5,
        scratch_shapes=[
            pltpu.VMEM((size, size), bf16),
            pltpu.VMEM((ext, LANES), f32),
            pltpu.VMEM((GROUP, size, LANES), f32),
            pltpu.VMEM((GROUP, size, LANES), f32),
            pltpu.SemaphoreType.DMA((2,)),
        ]
        + [pltpu.VMEM((ext, LANES), f32)] * GROUP
        + [pltpu.VMEM((nodes, LANES), bf16)] * outer,
        compiler_params=grant(36),
    )(side, maps, scale, matrix, vectors, *ghosts)


def add_returned(side_ref, faces_ref, returned, acc):
    slots = returned[0].shape[0]
    for a in acc:
        a[...] = jnp.zeros(a.shape, f32)
    offsets = [face_of(side_ref, q) * slots for q in range(4)]

    def body(step, _):
        base = step * 16
        for u in range(16):
            rows = [faces_ref[offsets[q] + base + u] for q in range(4)]
            sums = [
                acc[q][pl.ds(rows[q], 1), :] + returned[q][pl.ds(base + u, 1), :]
                for q in range(4)
            ]
            for q in range(4):
                acc[q][pl.ds(rows[q], 1), :] = sums[q]
        return 0

    lax.fori_loop(0, slots // 16, body, 0)


def filtered(interval_ref, own_ref, pot_ref, vec_ref, acc, write):
    low = jnp.full((1, LANES), interval_ref[0])
    high = jnp.full((1, LANES), interval_ref[1])
    center, half_width = (low + high) / 2.0, (high - low) / 2.0
    inverse = 1.0 / half_width
    shifts = ((pot_ref[...] - center) * inverse).T
    for step in range(shifts.shape[1]):
        rows = slice(step * LANES, (step + 1) * LANES)
        image = own_ref[rows, :] + (
            (acc[0][rows, :] + acc[1][rows, :]) + (acc[2][rows, :] + acc[3][rows, :])
        )
        shift = jnp.broadcast_to(shifts[:, step : step + 1], (LANES, LANES))
        write(rows, image * inverse + shift * vec_ref[rows, :].astype(f32))


def first_kernel(
    side_ref, faces_ref, interval_ref, own_ref, pot_ref, vec_ref, r0, r1, r2, r3,
    out_ref, o0, o1, o2, o3, table_ref, rows_ref, *acc
):
    nodes = vec_ref.shape[0]
    add_returned(side_ref, faces_ref, (r0, r1, r2, r3), acc)

    def write(rows, value):
        value = value.astype(bf16)
        out_ref[rows, :] = value
        table_ref[rows, :] = value.astype(f32)

    filtered(interval_ref, own_ref, pot_ref, vec_ref, acc, write)
    table_ref[nodes : nodes + 8, :] = jnp.zeros((8, LANES), f32)
    gather_faces(side_ref, faces_ref, table_ref, rows_ref, (o0, o1, o2, o3))


def second_kernel(
    side_ref, faces_ref, interval_ref, own_ref, pot_ref, vec_ref, r0, r1, r2, r3, old_ref,
    out_ref, *acc
):
    add_returned(side_ref, faces_ref, (r0, r1, r2, r3), acc)

    def write(rows, value):
        out_ref[rows, :] = (2.0 * value - old_ref[rows, :].astype(f32)).astype(bf16)

    filtered(interval_ref, own_ref, pot_ref, vec_ref, acc, write)


def finish_first(side, faces, interval, own, potential, vectors, returned):
    nodes, slots = vectors.shape[0], returned[0].shape[0]
    return pl.pallas_call(
        first_kernel,
        out_shape=[jax.ShapeDtypeStruct((nodes, LANES), bf16)]
        + [jax.ShapeDtypeStruct((slots, LANES), bf16)] * 4,
        in_specs=[smem] * 3 + [vmem] * 7,
        out_specs=[vmem] * 5,
        scratch_shapes=[
            pltpu.VMEM((nodes + 8, LANES), f32),
            pltpu.VMEM((slots, LANES), f32),
        ]
        + [pltpu.VMEM((nodes + 8, LANES), f32)] * 4,
        compiler_params=grant(20),
    )(side, faces, interval, own, potential, vectors, *returned)


def finish_second(side, faces, interval, own, potential, vectors, returned, old):
    nodes = vectors.shape[0]
    return pl.pallas_call(
        second_kernel,
        out_shape=jax.ShapeDtypeStruct((nodes, LANES), bf16),
        in_specs=[smem] * 3 + [vmem] * 8,
        out_specs=vmem,
        scratch_shapes=[pltpu.VMEM((nodes + 8, LANES), f32)] * 4,
        compiler_params=grant(20),
    )(side, faces, interval, own, potential, vectors, *returned, old)


def margin_kernel(band_ref, own_ref, other_ref, out_ref):
    half = LANES // 2
    nt = functools.partial(
        lax.dot_general,
        dimension_numbers=(((0,), (0,)), ((), ())),
        preferred_element_type=f32,
    )

    def write(low, high, band):
        low_rows = low[:, band * half : (band + 1) * half]
        high_rows = high[:, band * half : (band + 1) * half]
        block = nt(low_rows, low)
        cross = nt(low_rows, high)
        tail = nt(high_rows, high)
        row = lax.broadcasted_iota(jnp.int32, (half, LANES), 0) + band * half
        col = lax.broadcasted_iota(jnp.int32, (half, LANES), 1)
        out_ref[0:half, :] = jnp.where(col >= row, block, tail)
        out_ref[half : 2 * half, :] = cross
        diag = jnp.sum(jnp.where(col == row, tail, 0.0), 0, keepdims=True)
        out_ref[2 * half : 2 * half + 8, :] = jnp.broadcast_to(diag, (8, LANES))

    @pl.when(band_ref[0] == 0)
    def _():
        write(own_ref[...], other_ref[...], 0)

    @pl.when(band_ref[0] != 0)
    def _():
        write(other_ref[...], own_ref[...], 1)


def margin_rows(band, own, other):
    return pl.pallas_call(
        margin_kernel,
        out_shape=jax.ShapeDtypeStruct((LANES + 8, LANES), f32),
        in_specs=[smem, vmem, vmem],
        out_specs=vmem,
        compiler_params=grant(12),
    )(band, own, other)


def split_three(x):
    high = x.astype(bf16)
    rest = x - high.astype(f32)
    mid = rest.astype(bf16)
    return high, mid, (rest - mid.astype(f32)).astype(bf16)


def invert_factor(work_ref, block_ref, panel_ref):
    total = work_ref.shape[0]
    halves = total // LANES
    col = lax.broadcasted_iota(jnp.int32, (PANEL, total), 1)
    row = lax.broadcasted_iota(jnp.int32, (PANEL, total), 0)

    def step(p, start_row):
        first = pl.multiple_of(p * PANEL, PANEL)
        rows = work_ref[pl.ds(first, PANEL), :]
        block = rows[:, start_row : start_row + LANES]
        block = pltpu.roll(block, lax.rem(total - first, LANES), 1)
        for k in range(PANEL):
            block_ref[k] = jnp.broadcast_to(block[:, k : k + 1], (PANEL, LANES))
        panel = jnp.where((col >= first) & (col < first + PANEL), 0.0, rows)
        panel = jnp.where(col == row + first, 1.0, panel)
        for h in range(halves):
            panel_ref[h] = panel[:, h * LANES : (h + 1) * LANES]
        entry = {
            (i, k): block_ref[k, pl.ds(i, 8, stride=0), :]
            for k in range(PANEL)
            for i in range(k, PANEL)
        }
        done = []
        for k in range(PANEL):
            scale = lax.rsqrt(entry[k, k])
            lines = [panel_ref[h, pl.ds(k, 8, stride=0), :] for h in range(halves)]
            for i in range(k + 1, PANEL):
                entry[i, k] = entry[i, k] * scale
            for i in range(k + 1, PANEL):
                for m in range(k + 1, i + 1):
                    entry[i, m] = entry[i, m] - entry[i, k] * entry[m, k]
            for m in range(k):
                lines = [line - entry[k, m] * old for line, old in zip(lines, done[m])]
            lines = [line * scale for line in lines]
            done.append(lines)
            for h in range(halves):
                panel_ref[h, k : k + 1, :] = lines[h][k % 8 : k % 8 + 1, :]
        panel = jnp.concatenate([panel_ref[h] for h in range(halves)], 1)
        right = jnp.where(col >= first + PANEL, panel, 0.0)
        ah, am, al = split_three(right)
        bh, bm, bl = split_three(panel)
        lhs = jnp.concatenate([ah, ah, am, am, ah, al], 0)
        rhs = jnp.concatenate([bh, bm, bh, bm, bl, bh], 0)
        update = lax.dot_general(
            lhs[:, start_row:], rhs, (((0,), (0,)), ((), ())), preferred_element_type=f32
        )
        below = work_ref[start_row:, :]
        big = lax.broadcasted_iota(jnp.int32, below.shape, 1)
        inside = (big >= first) & (big < first + PANEL)
        work_ref[start_row:, :] = jnp.where(inside, 0.0, below) - update
        work_ref[pl.ds(first, PANEL), :] = panel

    per = LANES // PANEL
    for h in range(halves):
        lax.fori_loop(h * per, (h + 1) * per, lambda p, _: (step(p, h * LANES), 0)[1], 0)


def rotate_kernel(
    band_ref, count_ref, mine_ref, theirs_ref, own_ref, other_ref, out_ref, work_ref,
    block_ref, panel_ref
):
    half = LANES // 2
    band = band_ref[0]
    mine, theirs = mine_ref[...] * count_ref[0], theirs_ref[...] * count_ref[0]
    top = jnp.where(band == 0, mine, theirs)
    bottom = jnp.where(band == 0, theirs, mine)
    packed = jnp.concatenate([top[0:half], bottom[0:half]], 0)
    cross = jnp.concatenate([top[half:LANES], bottom[half:LANES]], 0)
    diag = top[LANES : LANES + 1] + bottom[LANES : LANES + 1]
    flipped = packed.T
    row = lax.broadcasted_iota(jnp.int32, (LANES, LANES), 0)
    col = lax.broadcasted_iota(jnp.int32, (LANES, LANES), 1)
    work_ref[0:LANES, 0:LANES] = jnp.where(col >= row, packed, flipped)
    work_ref[0:LANES, LANES:] = cross
    work_ref[LANES:, 0:LANES] = cross.T
    tail = jnp.where(col < row, packed, flipped)
    work_ref[LANES:, LANES:] = jnp.where(col == row, jnp.broadcast_to(diag, tail.shape), tail)
    invert_factor(work_ref, block_ref, panel_ref)
    lower = jnp.where(col <= row, 1.0, 0.0)
    first = work_ref[0:LANES, 0:LANES] * lower
    last = work_ref[LANES:, LANES:] * lower
    corner = work_ref[LANES:, 0:LANES]
    from_own = jnp.where(band == 0, first, last)
    from_other = jnp.where(band == 0, jnp.zeros_like(corner), corner)
    weights = jnp.concatenate([from_own, from_other], 1)
    high = weights.astype(bf16)
    low = (weights - high.astype(f32)).astype(bf16)
    weights = jnp.concatenate([high, low], 0)
    chunk = 512

    def body(step, _):
        rows = pl.ds(pl.multiple_of(step * chunk, chunk), chunk)
        both = jnp.concatenate([own_ref[rows, :], other_ref[rows, :]], 1)
        product = lax.dot_general(
            both, weights, (((1,), (1,)), ((), ())), preferred_element_type=f32
        )
        out_ref[rows, :] = product[:, :LANES] + product[:, LANES:]
        return 0

    lax.fori_loop(0, own_ref.shape[0] // chunk, body, 0)


def rotate(band, inv_count, mine, theirs, own, other):
    return pl.pallas_call(
        rotate_kernel,
        out_shape=jax.ShapeDtypeStruct(own.shape, f32),
        in_specs=[smem, smem] + [vmem] * 4,
        out_specs=vmem,
        scratch_shapes=[
            pltpu.VMEM((2 * LANES, 2 * LANES), f32),
            pltpu.VMEM((PANEL, PANEL, LANES), f32),
            pltpu.VMEM((2, PANEL, LANES), f32),
        ],
        compiler_params=grant(12),
    )(band, inv_count, mine, theirs, own, other)


def summed_over(value, axis):
    size = lax.axis_size(axis)
    if size & (size - 1):
        return lax.psum(value, axis)
    stride = 1
    while stride < size:
        count = min(4, size // stride)
        parts = [
            lax.ppermute(value, axis, [(i, i ^ (k * stride)) for i in range(size)])
            for k in range(1, count)
        ]
        value = value + sum(parts[1:], parts[0])
        stride *= count
    return value


def swapped(value):
    return lax.ppermute(value, "band", [(0, 1), (1, 0)])


def on_device(wavefunctions, bounds, cell_matrix, cell_scale, potential, cell_nodes, face_nodes):
    nodes = wavefunctions.shape[0]
    faces = jnp.where(face_nodes < 0, nodes, face_nodes).reshape(-1)
    potential = potential.reshape(-1, LANES)
    at = lax.axis_index("dom").astype(jnp.int32)
    side = jnp.stack([at % 2, at // 2 % 2])
    pairs = exchange_pairs(lax.axis_size("dom"))

    def exchanged(blocks):
        return [lax.ppermute(block, "dom", pair) for block, pair in zip(blocks, pairs)]

    cells = functools.partial(apply_cells, side, cell_nodes.reshape(-1), cell_scale, cell_matrix)
    ghosts = exchanged(send_faces(side, faces, wavefunctions))
    own, *sums = cells(wavefunctions, ghosts, True)
    degree_one, *blocks = finish_first(
        side, faces, bounds, own, potential, wavefunctions, exchanged(sums)
    )
    own, *sums = cells(degree_one, exchanged(blocks), False)
    degree_two = finish_second(
        side, faces, bounds, own, potential, degree_one, exchanged(sums), wavefunctions
    )
    other = swapped(degree_two)
    band = lax.axis_index("band").astype(jnp.int32).reshape(1)
    mine = summed_over(margin_rows(band, degree_two, other), "dom")
    inv_count = jnp.full((1,), 1.0 / (nodes * lax.axis_size("dom")), f32)
    return rotate(band, inv_count, mine, swapped(mine), degree_two, other)


def solution(mesh):
    return jax.shard_map(
        on_device,
        mesh=mesh,
        in_specs=(
            P(("kpt", "dom"), "band"),
            P("kpt"),
            P(),
            P("dom"),
            P("dom"),
            P("dom", None),
            P("dom", None),
        ),
        out_specs=P(("kpt", "dom"), "band"),
        check_vma=False,
    )
```

```python
import functools

import jax
import jax.numpy as jnp
from jax import lax
from jax.experimental import pallas as pl
from jax.experimental.pallas import tpu as pltpu
from jax.sharding import PartitionSpec as P

peer_offsets = (1, -1, 2, -2)
f32, bf16 = jnp.float32, jnp.bfloat16
LANES, GROUP, PANEL = 128, 8, 16
vmem = pl.BlockSpec(memory_space=pltpu.VMEM)
smem = pl.BlockSpec(memory_space=pltpu.SMEM)
hbm = pl.BlockSpec(memory_space=pltpu.HBM)


def grant(mib):
    return pltpu.CompilerParams(vmem_limit_bytes=mib * 2**20)


def exchange_pairs(size):
    first = ([i for i in range(size) if i % 2 == 0], 1)
    second = ([i for i in range(size) if i % 2 == 1], 1)
    third = ([i for i in range(size) if i % 4 < 2], 2)
    fourth = ([i for i in range(size) if i % 4 >= 2], 2)
    return [
        [pair for i in starts if i + by < size for pair in ((i, i + by), (i + by, i))]
        for starts, by in (first, second, third, fourth)
    ]


def gather_faces(order_ref, faces_ref, table_ref, rows_ref, out_refs):
    slots = out_refs[0].shape[0]
    for q in range(4):
        offset = order_ref[q] * slots

        def body(step, _):
            base = step * 64
            for u in range(64):
                face = faces_ref[offset + base + u]
                rows_ref[pl.ds(base + u, 1), :] = table_ref[pl.ds(face, 1), :]
            return 0

        lax.fori_loop(0, slots // 64, body, 0)
        out_refs[q][...] = rows_ref[...].astype(bf16)


def face_kernel(order_ref, faces_ref, vec_ref, o0, o1, o2, o3, table_ref, rows_ref):
    nodes = vec_ref.shape[0]
    table_ref[0:nodes, :] = vec_ref[...].astype(f32)
    table_ref[nodes : nodes + 8, :] = jnp.zeros((8, LANES), f32)
    gather_faces(order_ref, faces_ref, table_ref, rows_ref, (o0, o1, o2, o3))


def send_faces(side, faces, vectors):
    nodes, slots = vectors.shape[0], faces.shape[0] // 4
    return pl.pallas_call(
        face_kernel,
        out_shape=[jax.ShapeDtypeStruct((slots, LANES), bf16)] * 4,
        in_specs=[smem, smem, vmem],
        out_specs=[vmem] * 4,
        scratch_shapes=[
            pltpu.VMEM((nodes + 8, LANES), f32),
            pltpu.VMEM((slots, LANES), f32),
        ],
        compiler_params=grant(8),
    )(side, faces, vectors)


def cells_kernel(
    outer, order_ref, maps_ref, scale_ref, whole_ref, given_ref, h0, h1, h2, h3,
    own_ref, g0, g1, g2, g3, matrix_ref, ext_ref, in_ref, out_ref, sems, *rest
):
    acc = rest[:GROUP]
    nodes, slots = given_ref.shape[0], h0.shape[0]
    size = matrix_ref.shape[0]
    ext = nodes + 4 * slots
    fetch = pltpu.make_async_copy(whole_ref, matrix_ref, sems.at[0])
    if outer:
        vec_ref = rest[GROUP]
        load = pltpu.make_async_copy(given_ref, vec_ref, sems.at[1])
        load.start()
    else:
        vec_ref = given_ref
    fetch.start()
    for q, ghost in enumerate((h0, h1, h2, h3)):
        start = pl.multiple_of(nodes + (order_ref[q] ^ 1) * slots, slots)
        ext_ref[pl.ds(start, slots), :] = ghost[...].astype(f32)

    def clear(step, _):
        rows = pl.ds(pl.multiple_of(step * 64, 64), 64)
        for a in acc:
            a[rows, :] = jnp.zeros((64, LANES), f32)
        return 0

    lax.fori_loop(0, ext // 64, clear, 0)
    if outer:
        load.wait()
    ext_ref[0:nodes, :] = vec_ref[...].astype(f32)
    cells = scale_ref.shape[0]
    for first in range(0, cells, GROUP):

        def gather(step, _):
            base = step * 8
            for u in range(8):
                for k in range(GROUP):
                    row = maps_ref[(first + k) * size + base + u]
                    in_ref[k, pl.ds(base + u, 1), :] = ext_ref[pl.ds(row, 1), :]
            return 0

        lax.fori_loop(0, size // 8, gather, 0)
        if first == 0:
            fetch.wait()
        for k in range(0, GROUP, 2):
            pair = jnp.concatenate([in_ref[k].astype(bf16), in_ref[k + 1].astype(bf16)], 1)
            product = jnp.dot(matrix_ref[...], pair, preferred_element_type=f32)
            out_ref[k] = product[:, :LANES] * scale_ref[first + k]
            out_ref[k + 1] = product[:, LANES:] * scale_ref[first + k + 1]

        def scatter(step, _):
            base = step * 8
            for u in range(8):
                rows = [maps_ref[(first + k) * size + base + u] for k in range(GROUP)]
                sums = [
                    acc[k][pl.ds(rows[k], 1), :] + out_ref[k, pl.ds(base + u, 1), :]
                    for k in range(GROUP)
                ]
                for k in range(GROUP):
                    acc[k][pl.ds(rows[k], 1), :] = sums[k]
            return 0

        lax.fori_loop(0, size // 8, scatter, 0)

    def total(start):
        rows = pl.ds(start, 64)
        parts = [a[rows, :] for a in acc]
        while len(parts) > 1:
            parts = [parts[i] + parts[i + 1] for i in range(0, len(parts), 2)]
        return parts[0]

    def reduce_own(step, _):
        start = pl.multiple_of(step * 64, 64)
        own_ref[pl.ds(start, 64), :] = total(start)
        return 0

    lax.fori_loop(0, nodes // 64, reduce_own, 0)
    for q, ghost in enumerate((g0, g1, g2, g3)):
        start = pl.multiple_of(nodes + (order_ref[q] ^ 1) * slots, slots)
        for r in range(0, slots, 64):
            ghost[r : r + 64, :] = total(pl.multiple_of(start + r, 64))


def apply_cells(side, maps, scale, matrix, vectors, ghosts, outer):
    nodes, slots, size = vectors.shape[0], ghosts[0].shape[0], matrix.shape[0]
    ext = nodes + 4 * slots
    return pl.pallas_call(
        functools.partial(cells_kernel, outer),
        out_shape=[jax.ShapeDtypeStruct((nodes, LANES), f32)]
        + [jax.ShapeDtypeStruct((slots, LANES), f32)] * 4,
        in_specs=[smem, smem, smem, hbm, hbm if outer else vmem] + [vmem] * 4,
        out_specs=[vmem] * 5,
        scratch_shapes=[
            pltpu.VMEM((size, size), bf16),
            pltpu.VMEM((ext, LANES), f32),
            pltpu.VMEM((GROUP, size, LANES), f32),
            pltpu.VMEM((GROUP, size, LANES), f32),
            pltpu.SemaphoreType.DMA((2,)),
        ]
        + [pltpu.VMEM((ext, LANES), f32)] * GROUP
        + [pltpu.VMEM((nodes, LANES), bf16)] * outer,
        compiler_params=grant(36),
    )(side, maps, scale, matrix, vectors, *ghosts)


def add_returned(order_ref, faces_ref, returned, acc):
    slots = returned[0].shape[0]
    for a in acc:
        a[...] = jnp.zeros(a.shape, f32)
    offsets = [order_ref[q] * slots for q in range(4)]

    def body(step, _):
        base = step * 16
        for u in range(16):
            rows = [faces_ref[offsets[q] + base + u] for q in range(4)]
            sums = [
                acc[q][pl.ds(rows[q], 1), :] + returned[q][pl.ds(base + u, 1), :]
                for q in range(4)
            ]
            for q in range(4):
                acc[q][pl.ds(rows[q], 1), :] = sums[q]
        return 0

    lax.fori_loop(0, slots // 16, body, 0)


def filtered(interval_ref, own_ref, pot_ref, vec_ref, acc, write):
    low = jnp.full((1, LANES), interval_ref[0])
    high = jnp.full((1, LANES), interval_ref[1])
    center, half_width = (low + high) / 2.0, (high - low) / 2.0
    inverse = 1.0 / half_width
    shifts = ((pot_ref[...] - center) * inverse).T
    for step in range(shifts.shape[1]):
        rows = slice(step * LANES, (step + 1) * LANES)
        image = own_ref[rows, :] + (
            (acc[0][rows, :] + acc[1][rows, :]) + (acc[2][rows, :] + acc[3][rows, :])
        )
        shift = jnp.broadcast_to(shifts[:, step : step + 1], (LANES, LANES))
        write(rows, image * inverse + shift * vec_ref[rows, :].astype(f32))


def first_kernel(
    order_ref, faces_ref, interval_ref, own_ref, pot_ref, vec_ref, r0, r1, r2, r3,
    out_ref, o0, o1, o2, o3, table_ref, rows_ref, *acc
):
    nodes = vec_ref.shape[0]
    add_returned(order_ref, faces_ref, (r0, r1, r2, r3), acc)

    def write(rows, value):
        value = value.astype(bf16)
        out_ref[rows, :] = value
        table_ref[rows, :] = value.astype(f32)

    filtered(interval_ref, own_ref, pot_ref, vec_ref, acc, write)
    table_ref[nodes : nodes + 8, :] = jnp.zeros((8, LANES), f32)
    gather_faces(order_ref, faces_ref, table_ref, rows_ref, (o0, o1, o2, o3))


def second_kernel(
    order_ref, faces_ref, interval_ref, own_ref, pot_ref, vec_ref, r0, r1, r2, r3, old_ref,
    out_ref, *acc
):
    add_returned(order_ref, faces_ref, (r0, r1, r2, r3), acc)

    def write(rows, value):
        out_ref[rows, :] = (2.0 * value - old_ref[rows, :].astype(f32)).astype(bf16)

    filtered(interval_ref, own_ref, pot_ref, vec_ref, acc, write)


def finish_first(side, faces, interval, own, potential, vectors, returned):
    nodes, slots = vectors.shape[0], returned[0].shape[0]
    return pl.pallas_call(
        first_kernel,
        out_shape=[jax.ShapeDtypeStruct((nodes, LANES), bf16)]
        + [jax.ShapeDtypeStruct((slots, LANES), bf16)] * 4,
        in_specs=[smem] * 3 + [vmem] * 7,
        out_specs=[vmem] * 5,
        scratch_shapes=[
            pltpu.VMEM((nodes + 8, LANES), f32),
            pltpu.VMEM((slots, LANES), f32),
        ]
        + [pltpu.VMEM((nodes + 8, LANES), f32)] * 4,
        compiler_params=grant(20),
    )(side, faces, interval, own, potential, vectors, *returned)


def finish_second(side, faces, interval, own, potential, vectors, returned, old):
    nodes = vectors.shape[0]
    return pl.pallas_call(
        second_kernel,
        out_shape=jax.ShapeDtypeStruct((nodes, LANES), bf16),
        in_specs=[smem] * 3 + [vmem] * 8,
        out_specs=vmem,
        scratch_shapes=[pltpu.VMEM((nodes + 8, LANES), f32)] * 4,
        compiler_params=grant(20),
    )(side, faces, interval, own, potential, vectors, *returned, old)


def margin_kernel(band_ref, own_ref, other_ref, out_ref):
    half = LANES // 2
    nt = functools.partial(
        lax.dot_general,
        dimension_numbers=(((0,), (0,)), ((), ())),
        preferred_element_type=f32,
    )

    def write(low, high, band):
        low_rows = low[:, band * half : (band + 1) * half]
        high_rows = high[:, band * half : (band + 1) * half]
        block = nt(low_rows, low)
        cross = nt(low_rows, high)
        tail = nt(high_rows, high)
        row = lax.broadcasted_iota(jnp.int32, (half, LANES), 0) + band * half
        col = lax.broadcasted_iota(jnp.int32, (half, LANES), 1)
        out_ref[0:half, :] = jnp.where(col >= row, block, tail)
        out_ref[half : 2 * half, :] = cross
        diag = jnp.sum(jnp.where(col == row, tail, 0.0), 0, keepdims=True)
        out_ref[2 * half : 2 * half + 8, :] = jnp.broadcast_to(diag, (8, LANES))

    @pl.when(band_ref[0] == 0)
    def _():
        write(own_ref[...], other_ref[...], 0)

    @pl.when(band_ref[0] != 0)
    def _():
        write(other_ref[...], own_ref[...], 1)


def margin_rows(band, own, other):
    return pl.pallas_call(
        margin_kernel,
        out_shape=jax.ShapeDtypeStruct((LANES + 8, LANES), f32),
        in_specs=[smem, vmem, vmem],
        out_specs=vmem,
        compiler_params=grant(12),
    )(band, own, other)


def split_three(x):
    high = x.astype(bf16)
    rest = x - high.astype(f32)
    mid = rest.astype(bf16)
    return high, mid, (rest - mid.astype(f32)).astype(bf16)


def invert_factor(work_ref, block_ref, panel_ref):
    total = work_ref.shape[0]
    halves = total // LANES
    col = lax.broadcasted_iota(jnp.int32, (PANEL, total), 1)
    row = lax.broadcasted_iota(jnp.int32, (PANEL, total), 0)

    def step(p, start_row):
        first = pl.multiple_of(p * PANEL, PANEL)
        rows = work_ref[pl.ds(first, PANEL), :]
        block = rows[:, start_row : start_row + LANES]
        block = pltpu.roll(block, lax.rem(total - first, LANES), 1)
        for k in range(PANEL):
            block_ref[k] = jnp.broadcast_to(block[:, k : k + 1], (PANEL, LANES))
        panel = jnp.where((col >= first) & (col < first + PANEL), 0.0, rows)
        panel = jnp.where(col == row + first, 1.0, panel)
        for h in range(halves):
            panel_ref[h] = panel[:, h * LANES : (h + 1) * LANES]
        entry = {
            (i, k): block_ref[k, pl.ds(i, 8, stride=0), :]
            for k in range(PANEL)
            for i in range(k, PANEL)
        }
        done = []
        for k in range(PANEL):
            scale = lax.rsqrt(entry[k, k])
            lines = [panel_ref[h, pl.ds(k, 8, stride=0), :] for h in range(halves)]
            for i in range(k + 1, PANEL):
                entry[i, k] = entry[i, k] * scale
            for i in range(k + 1, PANEL):
                for m in range(k + 1, i + 1):
                    entry[i, m] = entry[i, m] - entry[i, k] * entry[m, k]
            for m in range(k):
                lines = [line - entry[k, m] * old for line, old in zip(lines, done[m])]
            lines = [line * scale for line in lines]
            done.append(lines)
            for h in range(halves):
                panel_ref[h, k : k + 1, :] = lines[h][k % 8 : k % 8 + 1, :]
        panel = jnp.concatenate([panel_ref[h] for h in range(halves)], 1)
        right = jnp.where(col >= first + PANEL, panel, 0.0)
        ah, am, al = split_three(right)
        bh, bm, bl = split_three(panel)
        lhs = jnp.concatenate([ah, ah, am, am, ah, al], 0)
        rhs = jnp.concatenate([bh, bm, bh, bm, bl, bh], 0)
        update = lax.dot_general(
            lhs[:, start_row:], rhs, (((0,), (0,)), ((), ())), preferred_element_type=f32
        )
        below = work_ref[start_row:, :]
        big = lax.broadcasted_iota(jnp.int32, below.shape, 1)
        inside = (big >= first) & (big < first + PANEL)
        work_ref[start_row:, :] = jnp.where(inside, 0.0, below) - update
        work_ref[pl.ds(first, PANEL), :] = panel

    per = LANES // PANEL
    for h in range(halves):
        lax.fori_loop(h * per, (h + 1) * per, lambda p, _: (step(p, h * LANES), 0)[1], 0)


def rotate_kernel(
    band_ref, count_ref, mine_ref, theirs_ref, own_ref, other_ref, out_ref, work_ref,
    block_ref, panel_ref
):
    half = LANES // 2
    band = band_ref[0]
    mine, theirs = mine_ref[...] * count_ref[0], theirs_ref[...] * count_ref[0]
    top = jnp.where(band == 0, mine, theirs)
    bottom = jnp.where(band == 0, theirs, mine)
    packed = jnp.concatenate([top[0:half], bottom[0:half]], 0)
    cross = jnp.concatenate([top[half:LANES], bottom[half:LANES]], 0)
    diag = top[LANES : LANES + 1] + bottom[LANES : LANES + 1]
    flipped = packed.T
    row = lax.broadcasted_iota(jnp.int32, (LANES, LANES), 0)
    col = lax.broadcasted_iota(jnp.int32, (LANES, LANES), 1)
    work_ref[0:LANES, 0:LANES] = jnp.where(col >= row, packed, flipped)
    work_ref[0:LANES, LANES:] = cross
    work_ref[LANES:, 0:LANES] = cross.T
    tail = jnp.where(col < row, packed, flipped)
    work_ref[LANES:, LANES:] = jnp.where(col == row, jnp.broadcast_to(diag, tail.shape), tail)
    invert_factor(work_ref, block_ref, panel_ref)
    lower = jnp.where(col <= row, 1.0, 0.0)
    first = work_ref[0:LANES, 0:LANES] * lower
    last = work_ref[LANES:, LANES:] * lower
    corner = work_ref[LANES:, 0:LANES]
    from_own = jnp.where(band == 0, first, last)
    from_other = jnp.where(band == 0, jnp.zeros_like(corner), corner)
    weights = jnp.concatenate([from_own, from_other], 1)
    high = weights.astype(bf16)
    low = (weights - high.astype(f32)).astype(bf16)
    weights = jnp.concatenate([high, low], 0)
    chunk = 512

    def body(step, _):
        rows = pl.ds(pl.multiple_of(step * chunk, chunk), chunk)
        both = jnp.concatenate([own_ref[rows, :], other_ref[rows, :]], 1)
        product = lax.dot_general(
            both, weights, (((1,), (1,)), ((), ())), preferred_element_type=f32
        )
        out_ref[rows, :] = product[:, :LANES] + product[:, LANES:]
        return 0

    lax.fori_loop(0, own_ref.shape[0] // chunk, body, 0)


def rotate(band, inv_count, mine, theirs, own, other):
    return pl.pallas_call(
        rotate_kernel,
        out_shape=jax.ShapeDtypeStruct(own.shape, f32),
        in_specs=[smem, smem] + [vmem] * 4,
        out_specs=vmem,
        scratch_shapes=[
            pltpu.VMEM((2 * LANES, 2 * LANES), f32),
            pltpu.VMEM((PANEL, PANEL, LANES), f32),
            pltpu.VMEM((2, PANEL, LANES), f32),
        ],
        compiler_params=grant(12),
    )(band, inv_count, mine, theirs, own, other)


def summed_over(value, axis):
    size = lax.axis_size(axis)
    if size & (size - 1):
        return lax.psum(value, axis)
    stride = 1
    while stride < size:
        count = min(4, size // stride)
        parts = [
            lax.ppermute(value, axis, [(i, i ^ (k * stride)) for i in range(size)])
            for k in range(1, count)
        ]
        value = value + sum(parts[1:], parts[0])
        stride *= count
    return value


def swapped(value):
    return lax.ppermute(value, "band", [(0, 1), (1, 0)])


def on_device(wavefunctions, bounds, cell_matrix, cell_scale, potential, cell_nodes, face_nodes):
    nodes = wavefunctions.shape[0]
    faces = jnp.where(face_nodes < 0, nodes, face_nodes).reshape(-1)
    potential = potential.reshape(-1, LANES)
    at = lax.axis_index("dom").astype(jnp.int32)
    band = lax.axis_index("band").astype(jnp.int32)
    kind = jnp.arange(4, dtype=jnp.int32) ^ (2 * band)
    flip = jnp.where(kind < 2, at % 2, at // 2 % 2)
    side = kind // 2 * 2 + ((kind % 2) ^ flip)
    pairs = exchange_pairs(lax.axis_size("dom"))

    def exchanged(blocks):
        return [
            lax.ppermute(
                block,
                ("dom", "band"),
                [(2 * i + b, 2 * j + b) for b in range(2) for i, j in pairs[q ^ (2 * b)]],
            )
            for q, block in enumerate(blocks)
        ]

    cells = functools.partial(apply_cells, side, cell_nodes.reshape(-1), cell_scale, cell_matrix)
    ghosts = exchanged(send_faces(side, faces, wavefunctions))
    own, *sums = cells(wavefunctions, ghosts, True)
    degree_one, *blocks = finish_first(
        side, faces, bounds, own, potential, wavefunctions, exchanged(sums)
    )
    own, *sums = cells(degree_one, exchanged(blocks), False)
    degree_two = finish_second(
        side, faces, bounds, own, potential, degree_one, exchanged(sums), wavefunctions
    )
    other = swapped(degree_two)
    band = band.reshape(1)
    mine = summed_over(margin_rows(band, degree_two, other), "dom")
    inv_count = jnp.full((1,), 1.0 / (nodes * lax.axis_size("dom")), f32)
    return rotate(band, inv_count, mine, swapped(mine), degree_two, other)


def solution(mesh):
    return jax.shard_map(
        on_device,
        mesh=mesh,
        in_specs=(
            P(("kpt", "dom"), "band"),
            P("kpt"),
            P(),
            P("dom"),
            P("dom"),
            P("dom", None),
            P("dom", None),
        ),
        out_specs=P(("kpt", "dom"), "band"),
        check_vma=False,
    )
```

```python
import functools

import jax
import jax.numpy as jnp
from jax import lax
from jax.experimental import pallas as pl
from jax.experimental.pallas import tpu as pltpu
from jax.sharding import PartitionSpec as P

peer_offsets = (1, -1, 2, -2)
f32, bf16 = jnp.float32, jnp.bfloat16
LANES, GROUP, PANEL = 128, 8, 16
vmem = pl.BlockSpec(memory_space=pltpu.VMEM)
smem = pl.BlockSpec(memory_space=pltpu.SMEM)
hbm = pl.BlockSpec(memory_space=pltpu.HBM)


def grant(mib):
    return pltpu.CompilerParams(vmem_limit_bytes=mib * 2**20)


def exchange_pairs(size):
    first = ([i for i in range(size) if i % 2 == 0], 1)
    second = ([i for i in range(size) if i % 2 == 1], 1)
    third = ([i for i in range(size) if i % 4 < 2], 2)
    fourth = ([i for i in range(size) if i % 4 >= 2], 2)
    return [
        [pair for i in starts if i + by < size for pair in ((i, i + by), (i + by, i))]
        for starts, by in (first, second, third, fourth)
    ]


def gather_faces(order_ref, faces_ref, table_ref, rows_ref, out_refs):
    slots = out_refs[0].shape[0]
    for q in range(4):
        offset = order_ref[q] * slots

        def body(step, _):
            base = step * 64
            for u in range(64):
                face = faces_ref[offset + base + u]
                rows_ref[pl.ds(base + u, 1), :] = table_ref[pl.ds(face, 1), :]
            return 0

        lax.fori_loop(0, slots // 64, body, 0)
        out_refs[q][...] = rows_ref[...].astype(bf16)


def face_kernel(
    order_ref, faces_ref, given_ref, o0, o1, o2, o3, vec_ref, table_ref, rows_ref, sems
):
    nodes, chunk = vec_ref.shape[0], vec_ref.shape[0] // sems.shape[0]
    copies = []
    for c in range(sems.shape[0]):
        rows = pl.ds(c * chunk, chunk)
        copies.append(pltpu.make_async_copy(given_ref.at[rows], vec_ref.at[rows], sems.at[c]))
        copies[-1].start()
    table_ref[nodes : nodes + 8, :] = jnp.zeros((8, LANES), f32)
    for c, copy in enumerate(copies):
        rows = pl.ds(c * chunk, chunk)
        copy.wait()
        table_ref[rows, :] = vec_ref[rows, :].astype(f32)
    gather_faces(order_ref, faces_ref, table_ref, rows_ref, (o0, o1, o2, o3))


def send_faces(side, faces, vectors):
    nodes, slots = vectors.shape[0], faces.shape[0] // 4
    *blocks, vectors = pl.pallas_call(
        face_kernel,
        out_shape=[jax.ShapeDtypeStruct((slots, LANES), bf16)] * 4
        + [jax.ShapeDtypeStruct((nodes, LANES), bf16)],
        in_specs=[smem, smem, hbm],
        out_specs=[vmem] * 5,
        scratch_shapes=[
            pltpu.VMEM((nodes + 8, LANES), f32),
            pltpu.VMEM((slots, LANES), f32),
            pltpu.SemaphoreType.DMA((4,)),
        ],
        compiler_params=grant(8),
    )(side, faces, vectors)
    return blocks, vectors


def cells_kernel(
    order_ref, names_ref, scales_ref, whole_ref, vec_ref, h0, h1, h2, h3,
    own_ref, g0, g1, g2, g3, maps_ref, scale_ref, matrix_ref, ext_ref, in_ref, out_ref, sems, *acc
):
    nodes, slots = vec_ref.shape[0], h0.shape[0]
    size = matrix_ref.shape[0]
    ext = nodes + 4 * slots
    fetch = pltpu.make_async_copy(whole_ref, matrix_ref, sems.at[0])
    name = pltpu.make_async_copy(names_ref, maps_ref, sems.at[1])
    scale = pltpu.make_async_copy(scales_ref, scale_ref, sems.at[2])
    name.start()
    scale.start()
    fetch.start()
    for q, ghost in enumerate((h0, h1, h2, h3)):
        start = pl.multiple_of(nodes + (order_ref[q] ^ 1) * slots, slots)
        ext_ref[pl.ds(start, slots), :] = ghost[...].astype(f32)
    share = ext // (size // 8)
    ext_ref[0:nodes, :] = vec_ref[...].astype(f32)
    name.wait()
    scale.wait()
    cells = scale_ref.shape[0]
    for first in range(0, cells, GROUP):

        def gather(step, _):
            base = step * 8
            if first == 0:
                cleared = pl.ds(pl.multiple_of(step * share, 8), share)
                for a in acc:
                    a[cleared, :] = jnp.zeros((share, LANES), f32)
            for u in range(8):
                for k in range(GROUP):
                    row = maps_ref[(first + k) * size + base + u]
                    in_ref[k, pl.ds(base + u, 1), :] = ext_ref[pl.ds(row, 1), :]
            return 0

        lax.fori_loop(0, size // 8, gather, 0)
        if first == 0:
            fetch.wait()
        for k in range(0, GROUP, 2):
            pair = jnp.concatenate([in_ref[k].astype(bf16), in_ref[k + 1].astype(bf16)], 1)
            product = jnp.dot(matrix_ref[...], pair, preferred_element_type=f32)
            out_ref[k] = product[:, :LANES] * scale_ref[first + k]
            out_ref[k + 1] = product[:, LANES:] * scale_ref[first + k + 1]

        def scatter(step, _):
            base = step * 8
            for u in range(8):
                rows = [maps_ref[(first + k) * size + base + u] for k in range(GROUP)]
                sums = [
                    acc[k][pl.ds(rows[k], 1), :] + out_ref[k, pl.ds(base + u, 1), :]
                    for k in range(GROUP)
                ]
                for k in range(GROUP):
                    acc[k][pl.ds(rows[k], 1), :] = sums[k]
            return 0

        lax.fori_loop(0, size // 8, scatter, 0)

    def total(start):
        rows = pl.ds(start, 64)
        parts = [a[rows, :] for a in acc]
        while len(parts) > 1:
            parts = [parts[i] + parts[i + 1] for i in range(0, len(parts), 2)]
        return parts[0]

    def reduce_own(step, _):
        start = pl.multiple_of(step * 64, 64)
        own_ref[pl.ds(start, 64), :] = total(start)
        return 0

    lax.fori_loop(0, nodes // 64, reduce_own, 0)
    for q, ghost in enumerate((g0, g1, g2, g3)):
        start = pl.multiple_of(nodes + (order_ref[q] ^ 1) * slots, slots)
        for r in range(0, slots, 64):
            ghost[r : r + 64, :] = total(pl.multiple_of(start + r, 64))


def apply_cells(side, maps, scale, matrix, vectors, ghosts):
    nodes, slots, size = vectors.shape[0], ghosts[0].shape[0], matrix.shape[0]
    ext = nodes + 4 * slots
    return pl.pallas_call(
        cells_kernel,
        out_shape=[jax.ShapeDtypeStruct((nodes, LANES), f32)]
        + [jax.ShapeDtypeStruct((slots, LANES), f32)] * 4,
        in_specs=[smem, hbm, hbm, hbm] + [vmem] * 5,
        out_specs=[vmem] * 5,
        scratch_shapes=[
            pltpu.SMEM(maps.shape, jnp.int32),
            pltpu.SMEM(scale.shape, f32),
            pltpu.VMEM((size, size), bf16),
            pltpu.VMEM((ext, LANES), f32),
            pltpu.VMEM((GROUP, size, LANES), f32),
            pltpu.VMEM((GROUP, size, LANES), f32),
            pltpu.SemaphoreType.DMA((3,)),
        ]
        + [pltpu.VMEM((ext, LANES), f32)] * GROUP,
        compiler_params=grant(36),
    )(side, maps, scale, matrix, vectors, *ghosts)


def add_returned(order_ref, faces_ref, returned, acc):
    slots = returned[0].shape[0]
    for a in acc:
        a[...] = jnp.zeros(a.shape, f32)
    offsets = [order_ref[q] * slots for q in range(4)]

    def body(step, _):
        base = step * 16
        for u in range(16):
            rows = [faces_ref[offsets[q] + base + u] for q in range(4)]
            sums = [
                acc[q][pl.ds(rows[q], 1), :] + returned[q][pl.ds(base + u, 1), :]
                for q in range(4)
            ]
            for q in range(4):
                acc[q][pl.ds(rows[q], 1), :] = sums[q]
        return 0

    lax.fori_loop(0, slots // 16, body, 0)


def filtered(interval_ref, own_ref, pot_ref, vec_ref, acc, write):
    low = jnp.full((1, LANES), interval_ref[0])
    high = jnp.full((1, LANES), interval_ref[1])
    center, half_width = (low + high) / 2.0, (high - low) / 2.0
    inverse = 1.0 / half_width
    shifts = ((pot_ref[...] - center) * inverse).T
    for step in range(shifts.shape[1]):
        rows = slice(step * LANES, (step + 1) * LANES)
        image = own_ref[rows, :] + (
            (acc[0][rows, :] + acc[1][rows, :]) + (acc[2][rows, :] + acc[3][rows, :])
        )
        shift = jnp.broadcast_to(shifts[:, step : step + 1], (LANES, LANES))
        write(rows, image * inverse + shift * vec_ref[rows, :].astype(f32))


def first_kernel(
    order_ref, faces_ref, interval_ref, own_ref, pot_ref, vec_ref, r0, r1, r2, r3,
    out_ref, o0, o1, o2, o3, table_ref, rows_ref, *acc
):
    nodes = vec_ref.shape[0]
    add_returned(order_ref, faces_ref, (r0, r1, r2, r3), acc)

    def write(rows, value):
        value = value.astype(bf16)
        out_ref[rows, :] = value
        table_ref[rows, :] = value.astype(f32)

    filtered(interval_ref, own_ref, pot_ref, vec_ref, acc, write)
    table_ref[nodes : nodes + 8, :] = jnp.zeros((8, LANES), f32)
    gather_faces(order_ref, faces_ref, table_ref, rows_ref, (o0, o1, o2, o3))


def second_kernel(
    order_ref, faces_ref, interval_ref, own_ref, pot_ref, vec_ref, r0, r1, r2, r3, old_ref,
    out_ref, *acc
):
    add_returned(order_ref, faces_ref, (r0, r1, r2, r3), acc)

    def write(rows, value):
        out_ref[rows, :] = (2.0 * value - old_ref[rows, :].astype(f32)).astype(bf16)

    filtered(interval_ref, own_ref, pot_ref, vec_ref, acc, write)


def finish_first(side, faces, interval, own, potential, vectors, returned):
    nodes, slots = vectors.shape[0], returned[0].shape[0]
    return pl.pallas_call(
        first_kernel,
        out_shape=[jax.ShapeDtypeStruct((nodes, LANES), bf16)]
        + [jax.ShapeDtypeStruct((slots, LANES), bf16)] * 4,
        in_specs=[smem] * 3 + [vmem] * 7,
        out_specs=[vmem] * 5,
        scratch_shapes=[
            pltpu.VMEM((nodes + 8, LANES), f32),
            pltpu.VMEM((slots, LANES), f32),
        ]
        + [pltpu.VMEM((nodes + 8, LANES), f32)] * 4,
        compiler_params=grant(20),
    )(side, faces, interval, own, potential, vectors, *returned)


def finish_second(side, faces, interval, own, potential, vectors, returned, old):
    nodes = vectors.shape[0]
    return pl.pallas_call(
        second_kernel,
        out_shape=jax.ShapeDtypeStruct((nodes, LANES), bf16),
        in_specs=[smem] * 3 + [vmem] * 8,
        out_specs=vmem,
        scratch_shapes=[pltpu.VMEM((nodes + 8, LANES), f32)] * 4,
        compiler_params=grant(20),
    )(side, faces, interval, own, potential, vectors, *returned, old)


def margin_kernel(band_ref, own_ref, other_ref, out_ref):
    half = LANES // 2
    nt = functools.partial(
        lax.dot_general,
        dimension_numbers=(((0,), (0,)), ((), ())),
        preferred_element_type=f32,
    )

    def write(low, high, band):
        low_rows = low[:, band * half : (band + 1) * half]
        high_rows = high[:, band * half : (band + 1) * half]
        block = nt(low_rows, low)
        cross = nt(low_rows, high)
        tail = nt(high_rows, high)
        row = lax.broadcasted_iota(jnp.int32, (half, LANES), 0) + band * half
        col = lax.broadcasted_iota(jnp.int32, (half, LANES), 1)
        out_ref[0:half, :] = jnp.where(col >= row, block, tail)
        out_ref[half : 2 * half, :] = cross
        diag = jnp.sum(jnp.where(col == row, tail, 0.0), 0, keepdims=True)
        out_ref[2 * half : 2 * half + 8, :] = jnp.broadcast_to(diag, (8, LANES))

    @pl.when(band_ref[0] == 0)
    def _():
        write(own_ref[...], other_ref[...], 0)

    @pl.when(band_ref[0] != 0)
    def _():
        write(other_ref[...], own_ref[...], 1)


def margin_rows(band, own, other):
    return pl.pallas_call(
        margin_kernel,
        out_shape=jax.ShapeDtypeStruct((LANES + 8, LANES), f32),
        in_specs=[smem, vmem, vmem],
        out_specs=vmem,
        compiler_params=grant(12),
    )(band, own, other)


def split_three(x):
    high = x.astype(bf16)
    rest = x - high.astype(f32)
    mid = rest.astype(bf16)
    return high, mid, (rest - mid.astype(f32)).astype(bf16)


def invert_factor(work_ref, block_ref, panel_ref):
    total = work_ref.shape[0]
    halves = total // LANES
    col = lax.broadcasted_iota(jnp.int32, (PANEL, total), 1)
    row = lax.broadcasted_iota(jnp.int32, (PANEL, total), 0)

    def step(p, start_row):
        first = pl.multiple_of(p * PANEL, PANEL)
        rows = work_ref[pl.ds(first, PANEL), :]
        block = rows[:, start_row : start_row + LANES]
        block = pltpu.roll(block, lax.rem(total - first, LANES), 1)
        for k in range(PANEL):
            block_ref[k] = jnp.broadcast_to(block[:, k : k + 1], (PANEL, LANES))
        panel = jnp.where((col >= first) & (col < first + PANEL), 0.0, rows)
        panel = jnp.where(col == row + first, 1.0, panel)
        for h in range(halves):
            panel_ref[h] = panel[:, h * LANES : (h + 1) * LANES]
        entry = {
            (i, k): block_ref[k, pl.ds(i, 8, stride=0), :]
            for k in range(PANEL)
            for i in range(k, PANEL)
        }
        done = []
        for k in range(PANEL):
            scale = lax.rsqrt(entry[k, k])
            lines = [panel_ref[h, pl.ds(k, 8, stride=0), :] for h in range(halves)]
            for i in range(k + 1, PANEL):
                entry[i, k] = entry[i, k] * scale
            for i in range(k + 1, PANEL):
                for m in range(k + 1, i + 1):
                    entry[i, m] = entry[i, m] - entry[i, k] * entry[m, k]
            for m in range(k):
                lines = [line - entry[k, m] * old for line, old in zip(lines, done[m])]
            lines = [line * scale for line in lines]
            done.append(lines)
            for h in range(halves):
                panel_ref[h, k : k + 1, :] = lines[h][k % 8 : k % 8 + 1, :]
        panel = jnp.concatenate([panel_ref[h] for h in range(halves)], 1)
        right = jnp.where(col >= first + PANEL, panel, 0.0)
        ah, am, al = split_three(right)
        bh, bm, bl = split_three(panel)
        lhs = jnp.concatenate([ah, ah, am, am, ah, al], 0)
        rhs = jnp.concatenate([bh, bm, bh, bm, bl, bh], 0)
        update = lax.dot_general(
            lhs[:, start_row:], rhs, (((0,), (0,)), ((), ())), preferred_element_type=f32
        )
        below = work_ref[start_row:, :]
        big = lax.broadcasted_iota(jnp.int32, below.shape, 1)
        inside = (big >= first) & (big < first + PANEL)
        work_ref[start_row:, :] = jnp.where(inside, 0.0, below) - update
        work_ref[pl.ds(first, PANEL), :] = panel

    per = LANES // PANEL
    for h in range(halves):
        lax.fori_loop(h * per, (h + 1) * per, lambda p, _: (step(p, h * LANES), 0)[1], 0)


def rotate_kernel(
    band_ref, count_ref, mine_ref, theirs_ref, own_ref, other_ref, out_ref, work_ref,
    block_ref, panel_ref, result_ref, sems
):
    half = LANES // 2
    band = band_ref[0]
    mine, theirs = mine_ref[...] * count_ref[0], theirs_ref[...] * count_ref[0]
    top = jnp.where(band == 0, mine, theirs)
    bottom = jnp.where(band == 0, theirs, mine)
    packed = jnp.concatenate([top[0:half], bottom[0:half]], 0)
    cross = jnp.concatenate([top[half:LANES], bottom[half:LANES]], 0)
    diag = top[LANES : LANES + 1] + bottom[LANES : LANES + 1]
    flipped = packed.T
    row = lax.broadcasted_iota(jnp.int32, (LANES, LANES), 0)
    col = lax.broadcasted_iota(jnp.int32, (LANES, LANES), 1)
    work_ref[0:LANES, 0:LANES] = jnp.where(col >= row, packed, flipped)
    work_ref[0:LANES, LANES:] = cross
    work_ref[LANES:, 0:LANES] = cross.T
    tail = jnp.where(col < row, packed, flipped)
    work_ref[LANES:, LANES:] = jnp.where(col == row, jnp.broadcast_to(diag, tail.shape), tail)
    invert_factor(work_ref, block_ref, panel_ref)
    lower = jnp.where(col <= row, 1.0, 0.0)
    first = work_ref[0:LANES, 0:LANES] * lower
    last = work_ref[LANES:, LANES:] * lower
    corner = work_ref[LANES:, 0:LANES]
    from_own = jnp.where(band == 0, first, last)
    from_other = jnp.where(band == 0, jnp.zeros_like(corner), corner)
    weights = jnp.concatenate([from_own, from_other], 1)
    high = weights.astype(bf16)
    low = (weights - high.astype(f32)).astype(bf16)
    weights = jnp.concatenate([high, low], 0)
    chunk = own_ref.shape[0] // sems.shape[0]
    copies = []
    for c in range(sems.shape[0]):
        rows = pl.ds(c * chunk, chunk)
        both = jnp.concatenate([own_ref[rows, :], other_ref[rows, :]], 1)
        product = lax.dot_general(
            both, weights, (((1,), (1,)), ((), ())), preferred_element_type=f32
        )
        result_ref[rows, :] = product[:, :LANES] + product[:, LANES:]
        copies.append(pltpu.make_async_copy(result_ref.at[rows], out_ref.at[rows], sems.at[c]))
        copies[-1].start()
    for copy in copies:
        copy.wait()


def rotate(band, inv_count, mine, theirs, own, other):
    return pl.pallas_call(
        rotate_kernel,
        out_shape=jax.ShapeDtypeStruct(own.shape, f32),
        in_specs=[smem, smem] + [vmem] * 4,
        out_specs=hbm,
        scratch_shapes=[
            pltpu.VMEM((2 * LANES, 2 * LANES), f32),
            pltpu.VMEM((PANEL, PANEL, LANES), f32),
            pltpu.VMEM((2, PANEL, LANES), f32),
            pltpu.VMEM(own.shape, f32),
            pltpu.SemaphoreType.DMA((8,)),
        ],
        compiler_params=grant(12),
    )(band, inv_count, mine, theirs, own, other)


def summed_over(value, axis):
    size = lax.axis_size(axis)
    if size & (size - 1):
        return lax.psum(value, axis)
    stride = 1
    while stride < size:
        count = min(4, size // stride)
        parts = [
            lax.ppermute(value, axis, [(i, i ^ (k * stride)) for i in range(size)])
            for k in range(1, count)
        ]
        value = value + sum(parts[1:], parts[0])
        stride *= count
    return value


def swapped(value):
    return lax.ppermute(value, "band", [(0, 1), (1, 0)])


def on_device(wavefunctions, bounds, cell_matrix, cell_scale, potential, cell_nodes, face_nodes):
    nodes = wavefunctions.shape[0]
    cell_matrix = pltpu.with_memory_space_constraint(cell_matrix, pltpu.HBM)
    cell_scale = pltpu.with_memory_space_constraint(cell_scale, pltpu.HBM)
    held = pltpu.with_memory_space_constraint(wavefunctions, pltpu.HBM)
    faces = jnp.where(face_nodes < 0, nodes, face_nodes).reshape(-1)
    potential = potential.reshape(-1, LANES)
    at = lax.axis_index("dom").astype(jnp.int32)
    band = lax.axis_index("band").astype(jnp.int32)
    kind = jnp.arange(4, dtype=jnp.int32) ^ (2 * band)
    flip = jnp.where(kind < 2, at % 2, at // 2 % 2)
    side = kind // 2 * 2 + ((kind % 2) ^ flip)
    pairs = exchange_pairs(lax.axis_size("dom"))

    def exchanged(blocks):
        return [
            lax.ppermute(
                block,
                ("dom", "band"),
                [(2 * i + b, 2 * j + b) for b in range(2) for i, j in pairs[q ^ (2 * b)]],
            )
            for q, block in enumerate(blocks)
        ]

    cells = functools.partial(apply_cells, side, cell_nodes.reshape(-1), cell_scale, cell_matrix)
    blocks, vectors = send_faces(side, faces, held)
    own, *sums = cells(vectors, exchanged(blocks))
    degree_one, *blocks = finish_first(
        side, faces, bounds, own, potential, vectors, exchanged(sums)
    )
    own, *sums = cells(degree_one, exchanged(blocks))
    degree_two = finish_second(
        side, faces, bounds, own, potential, degree_one, exchanged(sums), wavefunctions
    )
    other = swapped(degree_two)
    band = band.reshape(1)
    mine = summed_over(margin_rows(band, degree_two, other), "dom")
    inv_count = jnp.full((1,), 1.0 / (nodes * lax.axis_size("dom")), f32)
    return rotate(band, inv_count, mine, swapped(mine), degree_two, other)


def solution(mesh):
    return jax.shard_map(
        on_device,
        mesh=mesh,
        in_specs=(
            P(("kpt", "dom"), "band"),
            P("kpt"),
            P(),
            P("dom"),
            P("dom"),
            P("dom", None),
            P("dom", None),
        ),
        out_specs=P(("kpt", "dom"), "band"),
        check_vma=False,
    )
```

```python
import functools

import jax
import jax.numpy as jnp
from jax import lax
from jax.experimental import pallas as pl
from jax.experimental.pallas import tpu as pltpu
from jax.sharding import PartitionSpec as P

peer_offsets = (1, -1, 2, -2)
f32, bf16 = jnp.float32, jnp.bfloat16
LANES, GROUP, PANEL, HALF = 128, 8, 16, 8
vmem = pl.BlockSpec(memory_space=pltpu.VMEM)
smem = pl.BlockSpec(memory_space=pltpu.SMEM)
hbm = pl.BlockSpec(memory_space=pltpu.HBM)


def grant(mib):
    return pltpu.CompilerParams(vmem_limit_bytes=mib * 2**20)


def exchange_pairs(size):
    first = ([i for i in range(size) if i % 2 == 0], 1)
    second = ([i for i in range(size) if i % 2 == 1], 1)
    third = ([i for i in range(size) if i % 4 < 2], 2)
    fourth = ([i for i in range(size) if i % 4 >= 2], 2)
    return [
        [pair for i in starts if i + by < size for pair in ((i, i + by), (i + by, i))]
        for starts, by in (first, second, third, fourth)
    ]


def gather_faces(order_ref, faces_ref, table_ref, rows_ref, out_refs):
    slots = out_refs[0].shape[0]
    for q in range(4):
        offset = order_ref[q] * slots

        def body(step, _):
            base = step * 64
            for u in range(64):
                face = faces_ref[offset + base + u]
                rows_ref[pl.ds(base + u, 1), :] = table_ref[pl.ds(face, 1), :]
            return 0

        lax.fori_loop(0, slots // 64, body, 0)
        out_refs[q][...] = rows_ref[...].astype(bf16)


def face_kernel(
    order_ref, faces_ref, given_ref, o0, o1, o2, o3, vec_ref, table_ref, rows_ref, sems
):
    nodes, chunk = vec_ref.shape[0], vec_ref.shape[0] // sems.shape[0]
    copies = []
    for c in range(sems.shape[0]):
        rows = pl.ds(c * chunk, chunk)
        copies.append(pltpu.make_async_copy(given_ref.at[rows], vec_ref.at[rows], sems.at[c]))
        copies[-1].start()
    table_ref[nodes : nodes + 8, :] = jnp.zeros((8, LANES), f32)
    for c, copy in enumerate(copies):
        rows = pl.ds(c * chunk, chunk)
        copy.wait()
        table_ref[rows, :] = vec_ref[rows, :].astype(f32)
    gather_faces(order_ref, faces_ref, table_ref, rows_ref, (o0, o1, o2, o3))


def send_faces(side, faces, vectors):
    nodes, slots = vectors.shape[0], faces.shape[0] // 4
    *blocks, vectors = pl.pallas_call(
        face_kernel,
        out_shape=[jax.ShapeDtypeStruct((slots, LANES), bf16)] * 4
        + [jax.ShapeDtypeStruct((nodes, LANES), bf16)],
        in_specs=[smem, smem, hbm],
        out_specs=[vmem] * 5,
        scratch_shapes=[
            pltpu.VMEM((nodes + 8, LANES), f32),
            pltpu.VMEM((slots, LANES), f32),
            pltpu.SemaphoreType.DMA((4,)),
        ],
        compiler_params=grant(8),
    )(side, faces, vectors)
    return blocks, vectors


def cells_kernel(
    order_ref, names_ref, scales_ref, whole_ref, vec_ref, h0, h1, h2, h3,
    own_ref, g0, g1, g2, g3, maps_ref, scale_ref, matrix_ref, ext_ref, in_ref, out_ref, sems, *acc
):
    nodes, slots = vec_ref.shape[0], h0.shape[0]
    size = matrix_ref.shape[0]
    ext = nodes + 4 * slots
    fetch = pltpu.make_async_copy(whole_ref, matrix_ref, sems.at[0])
    cells = scale_ref.shape[0]
    scale = pltpu.make_async_copy(scales_ref, scale_ref, sems.at[1])
    names = []
    for batch in range(cells // GROUP):
        part = pl.ds(batch * GROUP * size, GROUP * size)
        names.append(
            pltpu.make_async_copy(names_ref.at[part], maps_ref.at[part], sems.at[2 + batch])
        )
        names[-1].start()
    scale.start()
    fetch.start()
    for q, ghost in enumerate((h0, h1, h2, h3)):
        start = pl.multiple_of(nodes + (order_ref[q] ^ 1) * slots, slots)
        ext_ref[pl.ds(start, slots), :] = ghost[...].astype(f32)
    share = ext // (size // 8)
    ext_ref[0:nodes, :] = vec_ref[...].astype(f32)
    for first in range(0, cells, GROUP):
        names[first // GROUP].wait()

        def gather(step, _):
            base = step * 8
            if first == 0:
                cleared = pl.ds(pl.multiple_of(step * share, 8), share)
                for a in acc:
                    a[cleared, :] = jnp.zeros((share, LANES), f32)
            for u in range(8):
                for k in range(GROUP):
                    row = maps_ref[(first + k) * size + base + u]
                    in_ref[k, pl.ds(base + u, 1), :] = ext_ref[pl.ds(row, 1), :]
            return 0

        lax.fori_loop(0, size // 8, gather, 0)
        if first == 0:
            fetch.wait()
            scale.wait()
        for k in range(0, GROUP, 2):
            pair = jnp.concatenate([in_ref[k].astype(bf16), in_ref[k + 1].astype(bf16)], 1)
            product = jnp.dot(matrix_ref[...], pair, preferred_element_type=f32)
            out_ref[k] = product[:, :LANES] * scale_ref[first + k]
            out_ref[k + 1] = product[:, LANES:] * scale_ref[first + k + 1]

        def scatter(step, _):
            base = step * 8
            for u in range(8):
                rows = [maps_ref[(first + k) * size + base + u] for k in range(GROUP)]
                sums = [
                    acc[k][pl.ds(rows[k], 1), :] + out_ref[k, pl.ds(base + u, 1), :]
                    for k in range(GROUP)
                ]
                for k in range(GROUP):
                    acc[k][pl.ds(rows[k], 1), :] = sums[k]
            return 0

        lax.fori_loop(0, size // 8, scatter, 0)

    def total(start):
        rows = pl.ds(start, 64)
        parts = [a[rows, :] for a in acc]
        while len(parts) > 1:
            parts = [parts[i] + parts[i + 1] for i in range(0, len(parts), 2)]
        return parts[0]

    def reduce_own(step, _):
        start = pl.multiple_of(step * 64, 64)
        own_ref[pl.ds(start, 64), :] = total(start)
        return 0

    lax.fori_loop(0, nodes // 64, reduce_own, 0)
    for q, ghost in enumerate((g0, g1, g2, g3)):
        start = pl.multiple_of(nodes + (order_ref[q] ^ 1) * slots, slots)
        for r in range(0, slots, 64):
            ghost[r : r + 64, :] = total(pl.multiple_of(start + r, 64))


def apply_cells(side, maps, scale, matrix, vectors, ghosts):
    nodes, slots, size = vectors.shape[0], ghosts[0].shape[0], matrix.shape[0]
    ext = nodes + 4 * slots
    return pl.pallas_call(
        cells_kernel,
        out_shape=[jax.ShapeDtypeStruct((nodes, LANES), f32)]
        + [jax.ShapeDtypeStruct((slots, LANES), f32)] * 4,
        in_specs=[smem, hbm, hbm, hbm] + [vmem] * 5,
        out_specs=[vmem] * 5,
        scratch_shapes=[
            pltpu.SMEM(maps.shape, jnp.int32),
            pltpu.SMEM(scale.shape, f32),
            pltpu.VMEM((size, size), bf16),
            pltpu.VMEM((ext, LANES), f32),
            pltpu.VMEM((GROUP, size, LANES), f32),
            pltpu.VMEM((GROUP, size, LANES), f32),
            pltpu.SemaphoreType.DMA((2 + scale.shape[0] // GROUP,)),
        ]
        + [pltpu.VMEM((ext, LANES), f32)] * GROUP,
        compiler_params=grant(36),
    )(side, maps, scale, matrix, vectors, *ghosts)


def add_returned(order_ref, faces_ref, returned, acc):
    slots = returned[0].shape[0]
    for a in acc:
        a[...] = jnp.zeros(a.shape, f32)
    offsets = [order_ref[q] * slots for q in range(4)]

    def body(step, _):
        base = step * 16
        for u in range(16):
            rows = [faces_ref[offsets[q] + base + u] for q in range(4)]
            sums = [
                acc[q][pl.ds(rows[q], 1), :] + returned[q][pl.ds(base + u, 1), :]
                for q in range(4)
            ]
            for q in range(4):
                acc[q][pl.ds(rows[q], 1), :] = sums[q]
        return 0

    lax.fori_loop(0, slots // 16, body, 0)


def filtered(interval_ref, own_ref, pot_ref, vec_ref, acc, write):
    low = jnp.full((1, LANES), interval_ref[0])
    high = jnp.full((1, LANES), interval_ref[1])
    center, half_width = (low + high) / 2.0, (high - low) / 2.0
    inverse = 1.0 / half_width
    shifts = ((pot_ref[...] - center) * inverse).T
    for step in range(shifts.shape[1]):
        rows = slice(step * LANES, (step + 1) * LANES)
        image = own_ref[rows, :] + (
            (acc[0][rows, :] + acc[1][rows, :]) + (acc[2][rows, :] + acc[3][rows, :])
        )
        shift = jnp.broadcast_to(shifts[:, step : step + 1], (LANES, LANES))
        write(rows, image * inverse + shift * vec_ref[rows, :].astype(f32))


def first_kernel(
    order_ref, faces_ref, interval_ref, own_ref, pot_ref, vec_ref, r0, r1, r2, r3,
    out_ref, o0, o1, o2, o3, table_ref, rows_ref, *acc
):
    nodes = vec_ref.shape[0]
    add_returned(order_ref, faces_ref, (r0, r1, r2, r3), acc)

    def write(rows, value):
        value = value.astype(bf16)
        out_ref[rows, :] = value
        table_ref[rows, :] = value.astype(f32)

    filtered(interval_ref, own_ref, pot_ref, vec_ref, acc, write)
    table_ref[nodes : nodes + 8, :] = jnp.zeros((8, LANES), f32)
    gather_faces(order_ref, faces_ref, table_ref, rows_ref, (o0, o1, o2, o3))


def second_kernel(
    order_ref, faces_ref, interval_ref, own_ref, pot_ref, vec_ref, r0, r1, r2, r3, old_ref,
    out_ref, *acc
):
    add_returned(order_ref, faces_ref, (r0, r1, r2, r3), acc)

    def write(rows, value):
        out_ref[rows, :] = (2.0 * value - old_ref[rows, :].astype(f32)).astype(bf16)

    filtered(interval_ref, own_ref, pot_ref, vec_ref, acc, write)


def finish_first(side, faces, interval, own, potential, vectors, returned):
    nodes, slots = vectors.shape[0], returned[0].shape[0]
    return pl.pallas_call(
        first_kernel,
        out_shape=[jax.ShapeDtypeStruct((nodes, LANES), bf16)]
        + [jax.ShapeDtypeStruct((slots, LANES), bf16)] * 4,
        in_specs=[smem] * 3 + [vmem] * 7,
        out_specs=[vmem] * 5,
        scratch_shapes=[
            pltpu.VMEM((nodes + 8, LANES), f32),
            pltpu.VMEM((slots, LANES), f32),
        ]
        + [pltpu.VMEM((nodes + 8, LANES), f32)] * 4,
        compiler_params=grant(20),
    )(side, faces, interval, own, potential, vectors, *returned)


def finish_second(side, faces, interval, own, potential, vectors, returned, old):
    nodes = vectors.shape[0]
    return pl.pallas_call(
        second_kernel,
        out_shape=jax.ShapeDtypeStruct((nodes, LANES), bf16),
        in_specs=[smem] * 3 + [vmem] * 8,
        out_specs=vmem,
        scratch_shapes=[pltpu.VMEM((nodes + 8, LANES), f32)] * 4,
        compiler_params=grant(20),
    )(side, faces, interval, own, potential, vectors, *returned, old)


def margin_kernel(band_ref, own_ref, other_ref, out_ref):
    half = LANES // 2
    nt = functools.partial(
        lax.dot_general,
        dimension_numbers=(((0,), (0,)), ((), ())),
        preferred_element_type=f32,
    )

    def write(low, high, band):
        low_rows = low[:, band * half : (band + 1) * half]
        high_rows = high[:, band * half : (band + 1) * half]
        block = nt(low_rows, low)
        cross = nt(low_rows, high)
        tail = nt(high_rows, high)
        row = lax.broadcasted_iota(jnp.int32, (half, LANES), 0) + band * half
        col = lax.broadcasted_iota(jnp.int32, (half, LANES), 1)
        out_ref[0:half, :] = jnp.where(col >= row, block, tail)
        out_ref[half : 2 * half, :] = cross
        diag = jnp.sum(jnp.where(col == row, tail, 0.0), 0, keepdims=True)
        out_ref[2 * half : 2 * half + 8, :] = jnp.broadcast_to(diag, (8, LANES))

    @pl.when(band_ref[0] == 0)
    def _():
        write(own_ref[...], other_ref[...], 0)

    @pl.when(band_ref[0] != 0)
    def _():
        write(other_ref[...], own_ref[...], 1)


def margin_rows(band, own, other):
    return pl.pallas_call(
        margin_kernel,
        out_shape=jax.ShapeDtypeStruct((LANES + 8, LANES), f32),
        in_specs=[smem, vmem, vmem],
        out_specs=vmem,
        compiler_params=grant(12),
    )(band, own, other)


def split_three(x):
    high = x.astype(bf16)
    rest = x - high.astype(f32)
    mid = rest.astype(bf16)
    return high, mid, (rest - mid.astype(f32)).astype(bf16)


def invert_factor(work_ref, block_ref, panel_ref, lower_ref, second_ref):
    total = work_ref.shape[0]
    halves = total // LANES
    col = lax.broadcasted_iota(jnp.int32, (PANEL, total), 1)
    row = lax.broadcasted_iota(jnp.int32, (PANEL, total), 0)

    def step(p, start_row):
        first = pl.multiple_of(p * PANEL, PANEL)
        rows = work_ref[pl.ds(first, PANEL), :]
        block = rows[:, start_row : start_row + LANES]
        block = pltpu.roll(block, lax.rem(total - first, LANES), 1)
        for k in range(PANEL):
            block_ref[k] = jnp.broadcast_to(block[:, k : k + 1], (PANEL, LANES))
        panel = jnp.where((col >= first) & (col < first + PANEL), 0.0, rows)
        panel = jnp.where(col == row + first, 1.0, panel)
        for h in range(halves):
            panel_ref[h] = panel[:, h * LANES : (h + 1) * LANES]

        def repeated(ref, k, i):
            return ref[k, pl.ds(i, HALF, stride=0), :]

        def factor(entry, below):
            scales = []
            for k in range(HALF):
                scale = lax.rsqrt(entry[k, k])
                scales.append(scale)
                for i in range(k + 1, HALF):
                    entry[i, k] = entry[i, k] * scale
                for i in range(k + 1, HALF):
                    for m in range(k + 1, i + 1):
                        entry[i, m] = entry[i, m] - entry[i, k] * entry[m, k]
                if below:
                    below[k] = below[k] * scale
                    for m in range(k + 1, HALF):
                        below[m] = below[m] - below[k] * entry[m, k]
            return scales

        def corner(ref):
            return {(i, k): repeated(ref, k, i) for k in range(HALF) for i in range(k, HALF)}

        done = []

        def write_lines(k, weights, scale):
            lines = [panel_ref[h, pl.ds(k, HALF, stride=0), :] for h in range(halves)]
            for m, weight in enumerate(weights):
                lines = [line - weight * old for line, old in zip(lines, done[m])]
            lines = [line * scale for line in lines]
            done.append(lines)
            at = k % HALF
            for h in range(halves):
                panel_ref[h, k : k + 1, :] = lines[h][at : at + 1, :]

        entry = corner(block_ref)
        below = [block_ref[k, HALF:PANEL, :] for k in range(HALF)]
        scales = factor(entry, below)
        for k in range(HALF):
            write_lines(k, [entry[k, m] for m in range(k)], scales[k])
            lower_ref[k] = below[k]
        cross = {(m, k): repeated(lower_ref, k, m) for k in range(HALF) for m in range(HALF)}
        for m in range(HALF):
            column = block_ref[HALF + m, HALF:PANEL, :]
            for k in range(HALF):
                column = column - below[k] * cross[m, k]
            second_ref[m] = column
        entry = corner(second_ref)
        scales = factor(entry, None)
        for k in range(HALF):
            weights = [cross[k, m] for m in range(HALF)] + [entry[k, m] for m in range(k)]
            write_lines(HALF + k, weights, scales[k])
        panel = jnp.concatenate([panel_ref[h] for h in range(halves)], 1)
        right = jnp.where(col >= first + PANEL, panel, 0.0)
        ah, am, al = split_three(right)
        bh, bm, bl = split_three(panel)
        lhs = jnp.concatenate([ah, ah, am, am, ah, al], 0)
        rhs = jnp.concatenate([bh, bm, bh, bm, bl, bh], 0)
        update = lax.dot_general(
            lhs[:, start_row:], rhs, (((0,), (0,)), ((), ())), preferred_element_type=f32
        )
        below = work_ref[start_row:, :]
        big = lax.broadcasted_iota(jnp.int32, below.shape, 1)
        inside = (big >= first) & (big < first + PANEL)
        work_ref[start_row:, :] = jnp.where(inside, 0.0, below) - update
        work_ref[pl.ds(first, PANEL), :] = panel

    per = LANES // PANEL
    for h in range(halves):
        lax.fori_loop(h * per, (h + 1) * per, lambda p, _: (step(p, h * LANES), 0)[1], 0)


def rotate_kernel(
    band_ref, count_ref, mine_ref, theirs_ref, own_ref, other_ref, out_ref, work_ref,
    block_ref, panel_ref, lower_ref, second_ref, result_ref, sems
):
    half = LANES // 2
    band = band_ref[0]
    mine, theirs = mine_ref[...] * count_ref[0], theirs_ref[...] * count_ref[0]
    top = jnp.where(band == 0, mine, theirs)
    bottom = jnp.where(band == 0, theirs, mine)
    packed = jnp.concatenate([top[0:half], bottom[0:half]], 0)
    cross = jnp.concatenate([top[half:LANES], bottom[half:LANES]], 0)
    diag = top[LANES : LANES + 1] + bottom[LANES : LANES + 1]
    flipped = packed.T
    row = lax.broadcasted_iota(jnp.int32, (LANES, LANES), 0)
    col = lax.broadcasted_iota(jnp.int32, (LANES, LANES), 1)
    work_ref[0:LANES, 0:LANES] = jnp.where(col >= row, packed, flipped)
    work_ref[0:LANES, LANES:] = cross
    work_ref[LANES:, 0:LANES] = cross.T
    tail = jnp.where(col < row, packed, flipped)
    work_ref[LANES:, LANES:] = jnp.where(col == row, jnp.broadcast_to(diag, tail.shape), tail)
    invert_factor(work_ref, block_ref, panel_ref, lower_ref, second_ref)
    lower = jnp.where(col <= row, 1.0, 0.0)
    first = work_ref[0:LANES, 0:LANES] * lower
    last = work_ref[LANES:, LANES:] * lower
    corner = work_ref[LANES:, 0:LANES]
    from_own = jnp.where(band == 0, first, last)
    from_other = jnp.where(band == 0, jnp.zeros_like(corner), corner)
    weights = jnp.concatenate([from_own, from_other], 1)
    high = weights.astype(bf16)
    low = (weights - high.astype(f32)).astype(bf16)
    weights = jnp.concatenate([high, low], 0)
    chunk = own_ref.shape[0] // sems.shape[0]
    copies = []
    for c in range(sems.shape[0]):
        rows = pl.ds(c * chunk, chunk)
        both = jnp.concatenate([own_ref[rows, :], other_ref[rows, :]], 1)
        product = lax.dot_general(
            both, weights, (((1,), (1,)), ((), ())), preferred_element_type=f32
        )
        result_ref[rows, :] = product[:, :LANES] + product[:, LANES:]
        copies.append(pltpu.make_async_copy(result_ref.at[rows], out_ref.at[rows], sems.at[c]))
        copies[-1].start()
    for copy in copies:
        copy.wait()


def rotate(band, inv_count, mine, theirs, own, other):
    return pl.pallas_call(
        rotate_kernel,
        out_shape=jax.ShapeDtypeStruct(own.shape, f32),
        in_specs=[smem, smem] + [vmem] * 4,
        out_specs=hbm,
        scratch_shapes=[
            pltpu.VMEM((2 * LANES, 2 * LANES), f32),
            pltpu.VMEM((PANEL, PANEL, LANES), f32),
            pltpu.VMEM((2, PANEL, LANES), f32),
            pltpu.VMEM((HALF, HALF, LANES), f32),
            pltpu.VMEM((HALF, HALF, LANES), f32),
            pltpu.VMEM(own.shape, f32),
            pltpu.SemaphoreType.DMA((8,)),
        ],
        compiler_params=grant(12),
    )(band, inv_count, mine, theirs, own, other)


def summed_over(value, axis):
    size = lax.axis_size(axis)
    if size & (size - 1):
        return lax.psum(value, axis)
    stride = 1
    while stride < size:
        count = min(4, size // stride)
        parts = [
            lax.ppermute(value, axis, [(i, i ^ (k * stride)) for i in range(size)])
            for k in range(1, count)
        ]
        value = value + sum(parts[1:], parts[0])
        stride *= count
    return value


def swapped(value):
    return lax.ppermute(value, "band", [(0, 1), (1, 0)])


def on_device(wavefunctions, bounds, cell_matrix, cell_scale, potential, cell_nodes, face_nodes):
    nodes = wavefunctions.shape[0]
    cell_matrix = pltpu.with_memory_space_constraint(cell_matrix, pltpu.HBM)
    cell_scale = pltpu.with_memory_space_constraint(cell_scale, pltpu.HBM)
    held = pltpu.with_memory_space_constraint(wavefunctions, pltpu.HBM)
    faces = jnp.where(face_nodes < 0, nodes, face_nodes).reshape(-1)
    potential = potential.reshape(-1, LANES)
    at = lax.axis_index("dom").astype(jnp.int32)
    band = lax.axis_index("band").astype(jnp.int32)
    kind = jnp.arange(4, dtype=jnp.int32) ^ (2 * band)
    flip = jnp.where(kind < 2, at % 2, at // 2 % 2)
    side = kind // 2 * 2 + ((kind % 2) ^ flip)
    pairs = exchange_pairs(lax.axis_size("dom"))

    def exchanged(blocks):
        return [
            lax.ppermute(
                block,
                ("dom", "band"),
                [(2 * i + b, 2 * j + b) for b in range(2) for i, j in pairs[q ^ (2 * b)]],
            )
            for q, block in enumerate(blocks)
        ]

    cells = functools.partial(apply_cells, side, cell_nodes.reshape(-1), cell_scale, cell_matrix)
    blocks, vectors = send_faces(side, faces, held)
    own, *sums = cells(vectors, exchanged(blocks))
    degree_one, *blocks = finish_first(
        side, faces, bounds, own, potential, vectors, exchanged(sums)
    )
    own, *sums = cells(degree_one, exchanged(blocks))
    degree_two = finish_second(
        side, faces, bounds, own, potential, degree_one, exchanged(sums), wavefunctions
    )
    other = swapped(degree_two)
    band = band.reshape(1)
    mine = summed_over(margin_rows(band, degree_two, other), "dom")
    inv_count = jnp.full((1,), 1.0 / (nodes * lax.axis_size("dom")), f32)
    return rotate(band, inv_count, mine, swapped(mine), degree_two, other)


def solution(mesh):
    return jax.shard_map(
        on_device,
        mesh=mesh,
        in_specs=(
            P(("kpt", "dom"), "band"),
            P("kpt"),
            P(),
            P("dom"),
            P("dom"),
            P("dom", None),
            P("dom", None),
        ),
        out_specs=P(("kpt", "dom"), "band"),
        check_vma=False,
    )
```

```python
import functools

import jax
import jax.numpy as jnp
from jax import lax
from jax.experimental import pallas as pl
from jax.experimental.pallas import tpu as pltpu
from jax.sharding import PartitionSpec as P

peer_offsets = (1, -1, 2, -2)
f32, bf16 = jnp.float32, jnp.bfloat16
LANES, GROUP, PANEL, HALF = 128, 8, 16, 8
vmem = pl.BlockSpec(memory_space=pltpu.VMEM)
smem = pl.BlockSpec(memory_space=pltpu.SMEM)
hbm = pl.BlockSpec(memory_space=pltpu.HBM)


def grant(mib):
    return pltpu.CompilerParams(vmem_limit_bytes=mib * 2**20)


def exchange_pairs(size):
    first = ([i for i in range(size) if i % 2 == 0], 1)
    second = ([i for i in range(size) if i % 2 == 1], 1)
    third = ([i for i in range(size) if i % 4 < 2], 2)
    fourth = ([i for i in range(size) if i % 4 >= 2], 2)
    return [
        [pair for i in starts if i + by < size for pair in ((i, i + by), (i + by, i))]
        for starts, by in (first, second, third, fourth)
    ]


def gather_faces(named, table_ref, rows_ref, out_refs):
    slots = out_refs[0].shape[0]
    for q in range(4):
        row_of = named(q)

        def body(step, _):
            base = step * 64
            for u in range(64):
                rows_ref[pl.ds(base + u, 1), :] = table_ref[pl.ds(row_of(base + u), 1), :]
            return 0

        lax.fori_loop(0, slots // 64, body, 0)
        out_refs[q][...] = rows_ref[...].astype(bf16)


def face_kernel(
    order_ref, faces_ref, given_ref, o0, o1, o2, o3, vec_ref, table_ref, rows_ref, sems
):
    nodes, chunk = vec_ref.shape[0], vec_ref.shape[0] // sems.shape[0]
    copies = []
    for c in range(sems.shape[0]):
        rows = pl.ds(c * chunk, chunk)
        copies.append(pltpu.make_async_copy(given_ref.at[rows], vec_ref.at[rows], sems.at[c]))
        copies[-1].start()
    table_ref[0:8, :] = jnp.zeros((8, LANES), f32)
    for c, copy in enumerate(copies):
        copy.wait()
        table_ref[pl.ds(8 + c * chunk, chunk), :] = vec_ref[pl.ds(c * chunk, chunk), :].astype(f32)

    def named(q):
        face = order_ref[q]
        return lambda slot: faces_ref[face, slot] + 8

    gather_faces(named, table_ref, rows_ref, (o0, o1, o2, o3))


def send_faces(side, face_nodes, vectors):
    nodes, slots = vectors.shape[0], face_nodes.shape[1]
    *blocks, vectors = pl.pallas_call(
        face_kernel,
        out_shape=[jax.ShapeDtypeStruct((slots, LANES), bf16)] * 4
        + [jax.ShapeDtypeStruct((nodes, LANES), bf16)],
        in_specs=[smem, smem, hbm],
        out_specs=[vmem] * 5,
        scratch_shapes=[
            pltpu.VMEM((nodes + 8, LANES), f32),
            pltpu.VMEM((slots, LANES), f32),
            pltpu.SemaphoreType.DMA((4,)),
        ],
        compiler_params=grant(8),
    )(side, face_nodes, vectors)
    return blocks, vectors


def cells_kernel(
    order_ref, names_ref, scales_ref, whole_ref, vec_ref, h0, h1, h2, h3,
    own_ref, g0, g1, g2, g3, maps_ref, scale_ref, matrix_ref, ext_ref, in_ref, out_ref, sems, *acc
):
    nodes, slots = vec_ref.shape[0], h0.shape[0]
    size = matrix_ref.shape[0]
    ext = nodes + 4 * slots
    fetch = pltpu.make_async_copy(whole_ref, matrix_ref, sems.at[0])
    cells = scale_ref.shape[0]
    scale = pltpu.make_async_copy(scales_ref, scale_ref, sems.at[1])
    names = []
    for batch in range(cells // GROUP):
        part = pl.ds(batch * GROUP * size, GROUP * size)
        names.append(
            pltpu.make_async_copy(names_ref.at[part], maps_ref.at[part], sems.at[2 + batch])
        )
        names[-1].start()
    scale.start()
    fetch.start()
    for q, ghost in enumerate((h0, h1, h2, h3)):
        start = pl.multiple_of(nodes + (order_ref[q] ^ 1) * slots, slots)
        ext_ref[pl.ds(start, slots), :] = ghost[...].astype(f32)
    share = ext // (size // 32)
    ext_ref[0:nodes, :] = vec_ref[...].astype(f32)
    for first in range(0, cells, GROUP):
        names[first // GROUP].wait()

        def gather(step, _):
            base = step * 32
            if first == 0:
                cleared = pl.ds(pl.multiple_of(step * share, 8), share)
                for a in acc:
                    a[cleared, :] = jnp.zeros((share, LANES), f32)
            for u in range(32):
                for k in range(GROUP):
                    row = maps_ref[(first + k) * size + base + u]
                    in_ref[k, pl.ds(base + u, 1), :] = ext_ref[pl.ds(row, 1), :]
            return 0

        lax.fori_loop(0, size // 32, gather, 0)
        if first == 0:
            fetch.wait()
            scale.wait()
        for k in range(0, GROUP, 2):
            pair = jnp.concatenate([in_ref[k].astype(bf16), in_ref[k + 1].astype(bf16)], 1)
            product = jnp.dot(matrix_ref[...], pair, preferred_element_type=f32)
            out_ref[k] = product[:, :LANES] * scale_ref[first + k]
            out_ref[k + 1] = product[:, LANES:] * scale_ref[first + k + 1]

        def scatter(step, _):
            base = step * 32
            for u in range(32):
                rows = [maps_ref[(first + k) * size + base + u] for k in range(GROUP)]
                sums = [
                    acc[k][pl.ds(rows[k], 1), :] + out_ref[k, pl.ds(base + u, 1), :]
                    for k in range(GROUP)
                ]
                for k in range(GROUP):
                    acc[k][pl.ds(rows[k], 1), :] = sums[k]
            return 0

        lax.fori_loop(0, size // 32, scatter, 0)

    def total(start):
        rows = pl.ds(start, 64)
        parts = [a[rows, :] for a in acc]
        while len(parts) > 1:
            parts = [parts[i] + parts[i + 1] for i in range(0, len(parts), 2)]
        return parts[0]

    def reduce_own(step, _):
        start = pl.multiple_of(step * 64, 64)
        own_ref[pl.ds(start, 64), :] = total(start)
        return 0

    lax.fori_loop(0, nodes // 64, reduce_own, 0)
    for q, ghost in enumerate((g0, g1, g2, g3)):
        start = pl.multiple_of(nodes + (order_ref[q] ^ 1) * slots, slots)
        for r in range(0, slots, 64):
            ghost[r : r + 64, :] = total(pl.multiple_of(start + r, 64))


def apply_cells(side, maps, scale, matrix, vectors, ghosts):
    nodes, slots, size = vectors.shape[0], ghosts[0].shape[0], matrix.shape[0]
    ext = nodes + 4 * slots
    return pl.pallas_call(
        cells_kernel,
        out_shape=[jax.ShapeDtypeStruct((nodes, LANES), f32)]
        + [jax.ShapeDtypeStruct((slots, LANES), f32)] * 4,
        in_specs=[smem, hbm, hbm, hbm] + [vmem] * 5,
        out_specs=[vmem] * 5,
        scratch_shapes=[
            pltpu.SMEM(maps.shape, jnp.int32),
            pltpu.SMEM(scale.shape, f32),
            pltpu.VMEM((size, size), bf16),
            pltpu.VMEM((ext, LANES), f32),
            pltpu.VMEM((GROUP, size, LANES), f32),
            pltpu.VMEM((GROUP, size, LANES), f32),
            pltpu.SemaphoreType.DMA((2 + scale.shape[0] // GROUP,)),
        ]
        + [pltpu.VMEM((ext, LANES), f32)] * GROUP,
        compiler_params=grant(36),
    )(side, maps, scale, matrix, vectors, *ghosts)


def add_returned(order_ref, faces_ref, at, returned, acc):
    slots = returned[0].shape[0]
    for a in acc:
        a[...] = jnp.zeros(a.shape, f32)
    offsets = [order_ref[at + q] * slots for q in range(2)]

    def body(step, _):
        base = step * 32
        for u in range(32):
            rows = [faces_ref[offsets[q] + base + u] for q in range(2)]
            sums = [
                acc[q][pl.ds(rows[q], 1), :] + returned[q][pl.ds(base + u, 1), :]
                for q in range(2)
            ]
            for q in range(2):
                acc[q][pl.ds(rows[q], 1), :] = sums[q]
        return 0

    lax.fori_loop(0, slots // 32, body, 0)


def early_kernel(order_ref, faces_ref, own_ref, r0, r1, out_ref, *acc):
    add_returned(order_ref, faces_ref, 0, (r0, r1), acc)

    def combine(step, _):
        rows = pl.ds(pl.multiple_of(step * 64, 64), 64)
        out_ref[rows, :] = own_ref[rows, :] + (acc[0][rows, :] + acc[1][rows, :])
        return 0

    lax.fori_loop(0, own_ref.shape[0] // 64, combine, 0)


def add_early(side, faces, own, returned):
    nodes = own.shape[0]
    return pl.pallas_call(
        early_kernel,
        out_shape=jax.ShapeDtypeStruct((nodes, LANES), f32),
        in_specs=[smem] * 2 + [vmem] * 3,
        out_specs=vmem,
        scratch_shapes=[pltpu.VMEM((nodes + 8, LANES), f32)] * 2,
        compiler_params=grant(12),
        cost_estimate=pl.CostEstimate(flops=10**6, bytes_accessed=4 * 10**6, transcendentals=0),
    )(side, faces, own, *returned)


def filtered(interval_ref, own_ref, pot_ref, vec_ref, acc, write):
    low = jnp.full((1, LANES), interval_ref[0])
    high = jnp.full((1, LANES), interval_ref[1])
    center, half_width = (low + high) / 2.0, (high - low) / 2.0
    inverse = 1.0 / half_width
    shifts = ((pot_ref[...] - center) * inverse).T
    for step in range(shifts.shape[1]):
        rows = slice(step * LANES, (step + 1) * LANES)
        image = own_ref[rows, :] + (acc[0][rows, :] + acc[1][rows, :])
        shift = jnp.broadcast_to(shifts[:, step : step + 1], (LANES, LANES))
        write(rows, image * inverse + shift * vec_ref[rows, :].astype(f32))


def first_kernel(
    order_ref, faces_ref, interval_ref, own_ref, pot_ref, vec_ref, r2, r3,
    out_ref, o0, o1, o2, o3, table_ref, rows_ref, *acc
):
    nodes = vec_ref.shape[0]
    add_returned(order_ref, faces_ref, 2, (r2, r3), acc)

    def write(rows, value):
        value = value.astype(bf16)
        out_ref[rows, :] = value
        table_ref[rows, :] = value.astype(f32)

    filtered(interval_ref, own_ref, pot_ref, vec_ref, acc, write)
    table_ref[nodes : nodes + 8, :] = jnp.zeros((8, LANES), f32)

    def named(q):
        offset = order_ref[q] * rows_ref.shape[0]
        return lambda slot: faces_ref[offset + slot]

    gather_faces(named, table_ref, rows_ref, (o0, o1, o2, o3))


def second_kernel(
    order_ref, faces_ref, interval_ref, own_ref, pot_ref, vec_ref, r2, r3, old_ref,
    out_ref, *acc
):
    add_returned(order_ref, faces_ref, 2, (r2, r3), acc)

    def write(rows, value):
        out_ref[rows, :] = (2.0 * value - old_ref[rows, :].astype(f32)).astype(bf16)

    filtered(interval_ref, own_ref, pot_ref, vec_ref, acc, write)


def finish_first(side, faces, interval, own, potential, vectors, returned):
    nodes, slots = vectors.shape[0], returned[0].shape[0]
    own = add_early(side, faces, own, returned[:2])
    return pl.pallas_call(
        first_kernel,
        out_shape=[jax.ShapeDtypeStruct((nodes, LANES), bf16)]
        + [jax.ShapeDtypeStruct((slots, LANES), bf16)] * 4,
        in_specs=[smem] * 3 + [vmem] * 5,
        out_specs=[vmem] * 5,
        scratch_shapes=[
            pltpu.VMEM((nodes + 8, LANES), f32),
            pltpu.VMEM((slots, LANES), f32),
        ]
        + [pltpu.VMEM((nodes + 8, LANES), f32)] * 2,
        compiler_params=grant(20),
    )(side, faces, interval, own, potential, vectors, *returned[2:])


def finish_second(side, faces, interval, own, potential, vectors, returned, old):
    nodes = vectors.shape[0]
    own = add_early(side, faces, own, returned[:2])
    return pl.pallas_call(
        second_kernel,
        out_shape=jax.ShapeDtypeStruct((nodes, LANES), bf16),
        in_specs=[smem] * 3 + [vmem] * 6,
        out_specs=vmem,
        scratch_shapes=[pltpu.VMEM((nodes + 8, LANES), f32)] * 2,
        compiler_params=grant(20),
    )(side, faces, interval, own, potential, vectors, *returned[2:], old)


def margin_kernel(band_ref, own_ref, other_ref, out_ref):
    half = LANES // 2
    nt = functools.partial(
        lax.dot_general,
        dimension_numbers=(((0,), (0,)), ((), ())),
        preferred_element_type=f32,
    )

    def write(low, high, band):
        low_rows = low[:, band * half : (band + 1) * half]
        high_rows = high[:, band * half : (band + 1) * half]
        block = nt(low_rows, low)
        cross = nt(low_rows, high)
        tail = nt(high_rows, high)
        row = lax.broadcasted_iota(jnp.int32, (half, LANES), 0) + band * half
        col = lax.broadcasted_iota(jnp.int32, (half, LANES), 1)
        out_ref[0:half, :] = jnp.where(col >= row, block, tail)
        out_ref[half : 2 * half, :] = cross
        diag = jnp.sum(jnp.where(col == row, tail, 0.0), 0, keepdims=True)
        out_ref[2 * half : 2 * half + 8, :] = jnp.broadcast_to(diag, (8, LANES))

    @pl.when(band_ref[0] == 0)
    def _():
        write(own_ref[...], other_ref[...], 0)

    @pl.when(band_ref[0] != 0)
    def _():
        write(other_ref[...], own_ref[...], 1)


def margin_rows(band, own, other):
    return pl.pallas_call(
        margin_kernel,
        out_shape=jax.ShapeDtypeStruct((LANES + 8, LANES), f32),
        in_specs=[smem, vmem, vmem],
        out_specs=vmem,
        compiler_params=grant(12),
    )(band, own, other)


def split_three(x):
    high = x.astype(bf16)
    rest = x - high.astype(f32)
    mid = rest.astype(bf16)
    return high, mid, (rest - mid.astype(f32)).astype(bf16)


def invert_factor(work_ref, block_ref, panel_ref, lower_ref, second_ref):
    total = work_ref.shape[0]
    halves = total // LANES
    col = lax.broadcasted_iota(jnp.int32, (PANEL, total), 1)
    row = lax.broadcasted_iota(jnp.int32, (PANEL, total), 0)

    def step(p, start_row):
        first = pl.multiple_of(p * PANEL, PANEL)
        rows = work_ref[pl.ds(first, PANEL), :]
        block = rows[:, start_row : start_row + LANES]
        block = pltpu.roll(block, lax.rem(total - first, LANES), 1)
        for k in range(PANEL):
            block_ref[k] = jnp.broadcast_to(block[:, k : k + 1], (PANEL, LANES))
        panel = jnp.where((col >= first) & (col < first + PANEL), 0.0, rows)
        panel = jnp.where(col == row + first, 1.0, panel)
        for h in range(halves):
            panel_ref[h] = panel[:, h * LANES : (h + 1) * LANES]

        def repeated(ref, k, i):
            return ref[k, pl.ds(i, HALF, stride=0), :]

        def factor(entry, below):
            scales = []
            for k in range(HALF):
                scale = lax.rsqrt(entry[k, k])
                scales.append(scale)
                for i in range(k + 1, HALF):
                    entry[i, k] = entry[i, k] * scale
                for i in range(k + 1, HALF):
                    for m in range(k + 1, i + 1):
                        entry[i, m] = entry[i, m] - entry[i, k] * entry[m, k]
                if below:
                    below[k] = below[k] * scale
                    for m in range(k + 1, HALF):
                        below[m] = below[m] - below[k] * entry[m, k]
            return scales

        def corner(ref):
            return {(i, k): repeated(ref, k, i) for k in range(HALF) for i in range(k, HALF)}

        done = []

        def write_lines(k, weights, scale):
            lines = [panel_ref[h, pl.ds(k, HALF, stride=0), :] for h in range(halves)]
            for m, weight in enumerate(weights):
                lines = [line - weight * old for line, old in zip(lines, done[m])]
            lines = [line * scale for line in lines]
            done.append(lines)
            at = k % HALF
            for h in range(halves):
                panel_ref[h, k : k + 1, :] = lines[h][at : at + 1, :]

        entry = corner(block_ref)
        below = [block_ref[k, HALF:PANEL, :] for k in range(HALF)]
        scales = factor(entry, below)
        for k in range(HALF):
            write_lines(k, [entry[k, m] for m in range(k)], scales[k])
            lower_ref[k] = below[k]
        cross = {(m, k): repeated(lower_ref, k, m) for k in range(HALF) for m in range(HALF)}
        for m in range(HALF):
            column = block_ref[HALF + m, HALF:PANEL, :]
            for k in range(HALF):
                column = column - below[k] * cross[m, k]
            second_ref[m] = column
        entry = corner(second_ref)
        scales = factor(entry, None)
        for k in range(HALF):
            weights = [cross[k, m] for m in range(HALF)] + [entry[k, m] for m in range(k)]
            write_lines(HALF + k, weights, scales[k])
        panel = jnp.concatenate([panel_ref[h] for h in range(halves)], 1)
        right = jnp.where(col >= first + PANEL, panel, 0.0)
        ah, am, al = split_three(right)
        bh, bm, bl = split_three(panel)
        lhs = jnp.concatenate([ah, ah, am, am, ah, al], 0)
        rhs = jnp.concatenate([bh, bm, bh, bm, bl, bh], 0)
        update = lax.dot_general(
            lhs[:, start_row:], rhs, (((0,), (0,)), ((), ())), preferred_element_type=f32
        )
        below = work_ref[start_row:, :]
        big = lax.broadcasted_iota(jnp.int32, below.shape, 1)
        inside = (big >= first) & (big < first + PANEL)
        work_ref[start_row:, :] = jnp.where(inside, 0.0, below) - update
        work_ref[pl.ds(first, PANEL), :] = panel

    per = LANES // PANEL
    for h in range(halves):
        lax.fori_loop(h * per, (h + 1) * per, lambda p, _: (step(p, h * LANES), 0)[1], 0)


def rotate_kernel(
    band_ref, count_ref, mine_ref, theirs_ref, own_ref, other_ref, out_ref, work_ref,
    block_ref, panel_ref, lower_ref, second_ref, result_ref, sems
):
    half = LANES // 2
    band = band_ref[0]
    mine, theirs = mine_ref[...] * count_ref[0], theirs_ref[...] * count_ref[0]
    top = jnp.where(band == 0, mine, theirs)
    bottom = jnp.where(band == 0, theirs, mine)
    packed = jnp.concatenate([top[0:half], bottom[0:half]], 0)
    cross = jnp.concatenate([top[half:LANES], bottom[half:LANES]], 0)
    diag = top[LANES : LANES + 1] + bottom[LANES : LANES + 1]
    flipped = packed.T
    row = lax.broadcasted_iota(jnp.int32, (LANES, LANES), 0)
    col = lax.broadcasted_iota(jnp.int32, (LANES, LANES), 1)
    work_ref[0:LANES, 0:LANES] = jnp.where(col >= row, packed, flipped)
    work_ref[0:LANES, LANES:] = cross
    work_ref[LANES:, 0:LANES] = cross.T
    tail = jnp.where(col < row, packed, flipped)
    work_ref[LANES:, LANES:] = jnp.where(col == row, jnp.broadcast_to(diag, tail.shape), tail)
    invert_factor(work_ref, block_ref, panel_ref, lower_ref, second_ref)
    lower = jnp.where(col <= row, 1.0, 0.0)
    first = work_ref[0:LANES, 0:LANES] * lower
    last = work_ref[LANES:, LANES:] * lower
    corner = work_ref[LANES:, 0:LANES]
    from_own = jnp.where(band == 0, first, last)
    from_other = jnp.where(band == 0, jnp.zeros_like(corner), corner)
    weights = jnp.concatenate([from_own, from_other], 1)
    high = weights.astype(bf16)
    low = (weights - high.astype(f32)).astype(bf16)
    weights = jnp.concatenate([high, low], 0)
    chunk = own_ref.shape[0] // sems.shape[0]
    copies = []
    for c in range(sems.shape[0]):
        rows = pl.ds(c * chunk, chunk)
        both = jnp.concatenate([own_ref[rows, :], other_ref[rows, :]], 1)
        product = lax.dot_general(
            both, weights, (((1,), (1,)), ((), ())), preferred_element_type=f32
        )
        result_ref[rows, :] = product[:, :LANES] + product[:, LANES:]
        copies.append(pltpu.make_async_copy(result_ref.at[rows], out_ref.at[rows], sems.at[c]))
        copies[-1].start()
    for copy in copies:
        copy.wait()


def rotate(band, inv_count, mine, theirs, own, other):
    return pl.pallas_call(
        rotate_kernel,
        out_shape=jax.ShapeDtypeStruct(own.shape, f32),
        in_specs=[smem, smem] + [vmem] * 4,
        out_specs=hbm,
        scratch_shapes=[
            pltpu.VMEM((2 * LANES, 2 * LANES), f32),
            pltpu.VMEM((PANEL, PANEL, LANES), f32),
            pltpu.VMEM((2, PANEL, LANES), f32),
            pltpu.VMEM((HALF, HALF, LANES), f32),
            pltpu.VMEM((HALF, HALF, LANES), f32),
            pltpu.VMEM(own.shape, f32),
            pltpu.SemaphoreType.DMA((8,)),
        ],
        compiler_params=grant(12),
    )(band, inv_count, mine, theirs, own, other)


def summed_over(value, axis):
    size = lax.axis_size(axis)
    if size & (size - 1):
        return lax.psum(value, axis)
    stride = 1
    while stride < size:
        count = min(4, size // stride)
        parts = [
            lax.ppermute(value, axis, [(i, i ^ (k * stride)) for i in range(size)])
            for k in range(1, count)
        ]
        value = value + sum(parts[1:], parts[0])
        stride *= count
    return value


def swapped(value):
    return lax.ppermute(value, "band", [(0, 1), (1, 0)])


def on_device(wavefunctions, bounds, cell_matrix, cell_scale, potential, cell_nodes, face_nodes):
    nodes = wavefunctions.shape[0]
    cell_matrix = pltpu.with_memory_space_constraint(cell_matrix, pltpu.HBM)
    cell_scale = pltpu.with_memory_space_constraint(cell_scale, pltpu.HBM)
    held = pltpu.with_memory_space_constraint(wavefunctions, pltpu.HBM)
    faces = jnp.where(face_nodes < 0, nodes, face_nodes).reshape(-1)
    potential = potential.reshape(-1, LANES)
    at = lax.axis_index("dom").astype(jnp.int32)
    band = lax.axis_index("band").astype(jnp.int32)
    kind = jnp.arange(4, dtype=jnp.int32) ^ (2 * band)
    flip = jnp.where(kind < 2, at % 2, at // 2 % 2)
    side = kind // 2 * 2 + ((kind % 2) ^ flip)
    pairs = exchange_pairs(lax.axis_size("dom"))

    def exchanged(blocks):
        return [
            lax.ppermute(
                block,
                ("dom", "band"),
                [(2 * i + b, 2 * j + b) for b in range(2) for i, j in pairs[q ^ (2 * b)]],
            )
            for q, block in enumerate(blocks)
        ]

    cells = functools.partial(apply_cells, side, cell_nodes.reshape(-1), cell_scale, cell_matrix)
    blocks, vectors = send_faces(side, face_nodes, held)
    own, *sums = cells(vectors, exchanged(blocks))
    degree_one, *blocks = finish_first(
        side, faces, bounds, own, potential, vectors, exchanged(sums)
    )
    own, *sums = cells(degree_one, exchanged(blocks))
    degree_two = finish_second(
        side, faces, bounds, own, potential, degree_one, exchanged(sums), wavefunctions
    )
    other = swapped(degree_two)
    band = band.reshape(1)
    mine = summed_over(margin_rows(band, degree_two, other), "dom")
    inv_count = jnp.full((1,), 1.0 / (nodes * lax.axis_size("dom")), f32)
    return rotate(band, inv_count, mine, swapped(mine), degree_two, other)


def solution(mesh):
    return jax.shard_map(
        on_device,
        mesh=mesh,
        in_specs=(
            P(("kpt", "dom"), "band"),
            P("kpt"),
            P(),
            P("dom"),
            P("dom"),
            P("dom", None),
            P("dom", None),
        ),
        out_specs=P(("kpt", "dom"), "band"),
        check_vma=False,
    )
```

```python
import functools

import jax
import jax.numpy as jnp
from jax import lax
from jax.experimental import pallas as pl
from jax.experimental.pallas import tpu as pltpu
from jax.sharding import PartitionSpec as P

peer_offsets = (1, -1, 2, -2)
f32, bf16 = jnp.float32, jnp.bfloat16
LANES, GROUP, PANEL, HALF = 128, 8, 16, 8
vmem = pl.BlockSpec(memory_space=pltpu.VMEM)
smem = pl.BlockSpec(memory_space=pltpu.SMEM)
hbm = pl.BlockSpec(memory_space=pltpu.HBM)


def grant(mib):
    return pltpu.CompilerParams(vmem_limit_bytes=mib * 2**20)


def exchange_pairs(size):
    first = ([i for i in range(size) if i % 2 == 0], 1)
    second = ([i for i in range(size) if i % 2 == 1], 1)
    third = ([i for i in range(size) if i % 4 < 2], 2)
    fourth = ([i for i in range(size) if i % 4 >= 2], 2)
    return [
        [pair for i in starts if i + by < size for pair in ((i, i + by), (i + by, i))]
        for starts, by in (first, second, third, fourth)
    ]


def gather_faces(order_ref, faces_ref, table_ref, rows_ref, out_refs):
    slots = out_refs[0].shape[0]
    for q in range(4):
        offset = order_ref[q] * slots

        def body(step, _):
            base = step * 64
            for u in range(64):
                face = faces_ref[offset + base + u]
                rows_ref[pl.ds(base + u, 1), :] = table_ref[pl.ds(face, 1), :]
            return 0

        lax.fori_loop(0, slots // 64, body, 0)
        out_refs[q][...] = rows_ref[...].astype(bf16)


def face_kernel(
    order_ref, faces_ref, given_ref, o0, o1, o2, o3, vec_ref, table_ref, rows_ref, sems
):
    nodes, chunk = vec_ref.shape[0], vec_ref.shape[0] // sems.shape[0]
    copies = []
    for c in range(sems.shape[0]):
        rows = pl.ds(c * chunk, chunk)
        copies.append(pltpu.make_async_copy(given_ref.at[rows], vec_ref.at[rows], sems.at[c]))
        copies[-1].start()
    table_ref[nodes : nodes + 8, :] = jnp.zeros((8, LANES), f32)
    for c, copy in enumerate(copies):
        rows = pl.ds(c * chunk, chunk)
        copy.wait()
        table_ref[rows, :] = vec_ref[rows, :].astype(f32)
    gather_faces(order_ref, faces_ref, table_ref, rows_ref, (o0, o1, o2, o3))


def send_faces(side, faces, vectors):
    nodes, slots = vectors.shape[0], faces.shape[0] // 4
    *blocks, vectors = pl.pallas_call(
        face_kernel,
        out_shape=[jax.ShapeDtypeStruct((slots, LANES), bf16)] * 4
        + [jax.ShapeDtypeStruct((nodes, LANES), bf16)],
        in_specs=[smem, smem, hbm],
        out_specs=[vmem] * 5,
        scratch_shapes=[
            pltpu.VMEM((nodes + 8, LANES), f32),
            pltpu.VMEM((slots, LANES), f32),
            pltpu.SemaphoreType.DMA((4,)),
        ],
        compiler_params=grant(8),
    )(side, faces, vectors)
    return blocks, vectors


def cells_kernel(
    order_ref, names_ref, scales_ref, whole_ref, vec_ref, h0, h1, h2, h3,
    own_ref, g0, g1, g2, g3, maps_ref, scale_ref, matrix_ref, ext_ref, in_ref, out_ref, sems, *acc
):
    nodes, slots = vec_ref.shape[0], h0.shape[0]
    size = matrix_ref.shape[0]
    ext = nodes + 4 * slots
    fetch = pltpu.make_async_copy(whole_ref, matrix_ref, sems.at[0])
    cells = scale_ref.shape[0]
    scale = pltpu.make_async_copy(scales_ref, scale_ref, sems.at[1])
    names = []
    for batch in range(cells // GROUP):
        part = pl.ds(batch * GROUP * size, GROUP * size)
        names.append(
            pltpu.make_async_copy(names_ref.at[part], maps_ref.at[part], sems.at[2 + batch])
        )
        names[-1].start()
    scale.start()
    fetch.start()
    for q, ghost in enumerate((h0, h1, h2, h3)):
        start = pl.multiple_of(nodes + (order_ref[q] ^ 1) * slots, slots)
        ext_ref[pl.ds(start, slots), :] = ghost[...].astype(f32)
    share = ext // (size // 32)
    ext_ref[0:nodes, :] = vec_ref[...].astype(f32)
    for first in range(0, cells, GROUP):
        names[first // GROUP].wait()

        def gather(step, _):
            base = step * 32
            if first == 0:
                cleared = pl.ds(pl.multiple_of(step * share, 8), share)
                for a in acc:
                    a[cleared, :] = jnp.zeros((share, LANES), f32)
            for u in range(32):
                for k in range(GROUP):
                    row = maps_ref[(first + k) * size + base + u]
                    in_ref[k, pl.ds(base + u, 1), :] = ext_ref[pl.ds(row, 1), :]
            return 0

        lax.fori_loop(0, size // 32, gather, 0)
        if first == 0:
            fetch.wait()
            scale.wait()
        for k in range(0, GROUP, 2):
            pair = jnp.concatenate([in_ref[k].astype(bf16), in_ref[k + 1].astype(bf16)], 1)
            product = jnp.dot(matrix_ref[...], pair, preferred_element_type=f32)
            out_ref[k] = product[:, :LANES] * scale_ref[first + k]
            out_ref[k + 1] = product[:, LANES:] * scale_ref[first + k + 1]

        def scatter(step, _):
            base = step * 32
            for u in range(32):
                rows = [maps_ref[(first + k) * size + base + u] for k in range(GROUP)]
                sums = [
                    acc[k][pl.ds(rows[k], 1), :] + out_ref[k, pl.ds(base + u, 1), :]
                    for k in range(GROUP)
                ]
                for k in range(GROUP):
                    acc[k][pl.ds(rows[k], 1), :] = sums[k]
            return 0

        lax.fori_loop(0, size // 32, scatter, 0)

    def total(start):
        rows = pl.ds(start, 64)
        parts = [a[rows, :] for a in acc]
        while len(parts) > 1:
            parts = [parts[i] + parts[i + 1] for i in range(0, len(parts), 2)]
        return parts[0]

    def reduce_own(step, _):
        start = pl.multiple_of(step * 64, 64)
        own_ref[pl.ds(start, 64), :] = total(start)
        return 0

    lax.fori_loop(0, nodes // 64, reduce_own, 0)
    for q, ghost in enumerate((g0, g1, g2, g3)):
        start = pl.multiple_of(nodes + (order_ref[q] ^ 1) * slots, slots)
        for r in range(0, slots, 64):
            ghost[r : r + 64, :] = total(pl.multiple_of(start + r, 64))


def apply_cells(side, maps, scale, matrix, vectors, ghosts):
    nodes, slots, size = vectors.shape[0], ghosts[0].shape[0], matrix.shape[0]
    ext = nodes + 4 * slots
    return pl.pallas_call(
        cells_kernel,
        out_shape=[jax.ShapeDtypeStruct((nodes, LANES), f32)]
        + [jax.ShapeDtypeStruct((slots, LANES), f32)] * 4,
        in_specs=[smem, hbm, hbm, hbm] + [vmem] * 5,
        out_specs=[vmem] * 5,
        scratch_shapes=[
            pltpu.SMEM(maps.shape, jnp.int32),
            pltpu.SMEM(scale.shape, f32),
            pltpu.VMEM((size, size), bf16),
            pltpu.VMEM((ext, LANES), f32),
            pltpu.VMEM((GROUP, size, LANES), f32),
            pltpu.VMEM((GROUP, size, LANES), f32),
            pltpu.SemaphoreType.DMA((2 + scale.shape[0] // GROUP,)),
        ]
        + [pltpu.VMEM((ext, LANES), f32)] * GROUP,
        compiler_params=grant(36),
    )(side, maps, scale, matrix, vectors, *ghosts)


def add_returned(order_ref, faces_ref, at, returned, acc):
    slots = returned[0].shape[0]
    for a in acc:
        a[...] = jnp.zeros(a.shape, f32)
    offsets = [order_ref[at + q] * slots for q in range(2)]

    def body(step, _):
        base = step * 32
        for u in range(32):
            rows = [faces_ref[offsets[q] + base + u] for q in range(2)]
            sums = [
                acc[q][pl.ds(rows[q], 1), :] + returned[q][pl.ds(base + u, 1), :]
                for q in range(2)
            ]
            for q in range(2):
                acc[q][pl.ds(rows[q], 1), :] = sums[q]
        return 0

    lax.fori_loop(0, slots // 32, body, 0)


def early_kernel(order_ref, faces_ref, own_ref, r0, r1, out_ref, *acc):
    add_returned(order_ref, faces_ref, 0, (r0, r1), acc)

    def combine(step, _):
        rows = pl.ds(pl.multiple_of(step * 64, 64), 64)
        out_ref[rows, :] = own_ref[rows, :] + (acc[0][rows, :] + acc[1][rows, :])
        return 0

    lax.fori_loop(0, own_ref.shape[0] // 64, combine, 0)


def add_early(side, faces, own, returned):
    nodes = own.shape[0]
    return pl.pallas_call(
        early_kernel,
        out_shape=jax.ShapeDtypeStruct((nodes, LANES), f32),
        in_specs=[smem] * 2 + [vmem] * 3,
        out_specs=vmem,
        scratch_shapes=[pltpu.VMEM((nodes + 8, LANES), f32)] * 2,
        compiler_params=grant(12),
        cost_estimate=pl.CostEstimate(flops=10**6, bytes_accessed=4 * 10**6, transcendentals=0),
    )(side, faces, own, *returned)


def filtered(interval_ref, own_ref, pot_ref, vec_ref, acc, write):
    low = jnp.full((1, LANES), interval_ref[0])
    high = jnp.full((1, LANES), interval_ref[1])
    center, half_width = (low + high) / 2.0, (high - low) / 2.0
    inverse = 1.0 / half_width
    shifts = ((pot_ref[...] - center) * inverse).T
    for step in range(shifts.shape[1]):
        rows = slice(step * LANES, (step + 1) * LANES)
        image = own_ref[rows, :] + (acc[0][rows, :] + acc[1][rows, :])
        shift = jnp.broadcast_to(shifts[:, step : step + 1], (LANES, LANES))
        write(rows, image * inverse + shift * vec_ref[rows, :].astype(f32))


def first_kernel(
    order_ref, faces_ref, interval_ref, own_ref, pot_ref, vec_ref, r2, r3,
    out_ref, o0, o1, o2, o3, table_ref, rows_ref, *acc
):
    nodes = vec_ref.shape[0]
    add_returned(order_ref, faces_ref, 2, (r2, r3), acc)

    def write(rows, value):
        value = value.astype(bf16)
        out_ref[rows, :] = value
        table_ref[rows, :] = value.astype(f32)

    filtered(interval_ref, own_ref, pot_ref, vec_ref, acc, write)
    table_ref[nodes : nodes + 8, :] = jnp.zeros((8, LANES), f32)

    gather_faces(order_ref, faces_ref, table_ref, rows_ref, (o0, o1, o2, o3))


def second_kernel(
    order_ref, faces_ref, interval_ref, own_ref, pot_ref, vec_ref, r2, r3, old_ref,
    out_ref, *acc
):
    add_returned(order_ref, faces_ref, 2, (r2, r3), acc)

    def write(rows, value):
        out_ref[rows, :] = (2.0 * value - old_ref[rows, :].astype(f32)).astype(bf16)

    filtered(interval_ref, own_ref, pot_ref, vec_ref, acc, write)


def finish_first(side, faces, interval, own, potential, vectors, returned):
    nodes, slots = vectors.shape[0], returned[0].shape[0]
    own = add_early(side, faces, own, returned[:2])
    return pl.pallas_call(
        first_kernel,
        out_shape=[jax.ShapeDtypeStruct((nodes, LANES), bf16)]
        + [jax.ShapeDtypeStruct((slots, LANES), bf16)] * 4,
        in_specs=[smem] * 3 + [vmem] * 5,
        out_specs=[vmem] * 5,
        scratch_shapes=[
            pltpu.VMEM((nodes + 8, LANES), f32),
            pltpu.VMEM((slots, LANES), f32),
        ]
        + [pltpu.VMEM((nodes + 8, LANES), f32)] * 2,
        compiler_params=grant(20),
    )(side, faces, interval, own, potential, vectors, *returned[2:])


def finish_second(side, faces, interval, own, potential, vectors, returned, old):
    nodes = vectors.shape[0]
    own = add_early(side, faces, own, returned[:2])
    return pl.pallas_call(
        second_kernel,
        out_shape=jax.ShapeDtypeStruct((nodes, LANES), bf16),
        in_specs=[smem] * 3 + [vmem] * 6,
        out_specs=vmem,
        scratch_shapes=[pltpu.VMEM((nodes + 8, LANES), f32)] * 2,
        compiler_params=grant(20),
    )(side, faces, interval, own, potential, vectors, *returned[2:], old)


def margin_kernel(band_ref, own_ref, other_ref, out_ref):
    half = LANES // 2
    nt = functools.partial(
        lax.dot_general,
        dimension_numbers=(((0,), (0,)), ((), ())),
        preferred_element_type=f32,
    )

    def write(low, high, band):
        low_rows = low[:, band * half : (band + 1) * half]
        high_rows = high[:, band * half : (band + 1) * half]
        block = nt(low_rows, low)
        cross = nt(low_rows, high)
        tail = nt(high_rows, high)
        row = lax.broadcasted_iota(jnp.int32, (half, LANES), 0) + band * half
        col = lax.broadcasted_iota(jnp.int32, (half, LANES), 1)
        out_ref[0:half, :] = jnp.where(col >= row, block, tail)
        out_ref[half : 2 * half, :] = cross
        diag = jnp.sum(jnp.where(col == row, tail, 0.0), 0, keepdims=True)
        out_ref[2 * half : 2 * half + 8, :] = jnp.broadcast_to(diag, (8, LANES))

    @pl.when(band_ref[0] == 0)
    def _():
        write(own_ref[...], other_ref[...], 0)

    @pl.when(band_ref[0] != 0)
    def _():
        write(other_ref[...], own_ref[...], 1)


def margin_rows(band, own, other):
    return pl.pallas_call(
        margin_kernel,
        out_shape=jax.ShapeDtypeStruct((LANES + 8, LANES), f32),
        in_specs=[smem, vmem, vmem],
        out_specs=vmem,
        compiler_params=grant(12),
    )(band, own, other)


def split_three(x):
    high = x.astype(bf16)
    rest = x - high.astype(f32)
    mid = rest.astype(bf16)
    return high, mid, (rest - mid.astype(f32)).astype(bf16)


def invert_factor(work_ref, block_ref, panel_ref, lower_ref, second_ref):
    total = work_ref.shape[0]
    halves = total // LANES
    col = lax.broadcasted_iota(jnp.int32, (PANEL, total), 1)
    row = lax.broadcasted_iota(jnp.int32, (PANEL, total), 0)

    def step(p, start_row):
        first = pl.multiple_of(p * PANEL, PANEL)
        rows = work_ref[pl.ds(first, PANEL), :]
        block = rows[:, start_row : start_row + LANES]
        block = pltpu.roll(block, lax.rem(total - first, LANES), 1)
        for k in range(PANEL):
            block_ref[k] = jnp.broadcast_to(block[:, k : k + 1], (PANEL, LANES))
        panel = jnp.where((col >= first) & (col < first + PANEL), 0.0, rows)
        panel = jnp.where(col == row + first, 1.0, panel)
        for h in range(halves):
            panel_ref[h] = panel[:, h * LANES : (h + 1) * LANES]

        def repeated(ref, k, i):
            return ref[k, pl.ds(i, HALF, stride=0), :]

        def factor(entry, below):
            scales = []
            for k in range(HALF):
                scale = lax.rsqrt(entry[k, k])
                scales.append(scale)
                for i in range(k + 1, HALF):
                    entry[i, k] = entry[i, k] * scale
                for i in range(k + 1, HALF):
                    for m in range(k + 1, i + 1):
                        entry[i, m] = entry[i, m] - entry[i, k] * entry[m, k]
                if below:
                    below[k] = below[k] * scale
                    for m in range(k + 1, HALF):
                        below[m] = below[m] - below[k] * entry[m, k]
            return scales

        def corner(ref):
            return {(i, k): repeated(ref, k, i) for k in range(HALF) for i in range(k, HALF)}

        done = []

        def write_lines(k, weights, scale):
            lines = [panel_ref[h, pl.ds(k, HALF, stride=0), :] for h in range(halves)]
            for m, weight in enumerate(weights):
                lines = [line - weight * old for line, old in zip(lines, done[m])]
            lines = [line * scale for line in lines]
            done.append(lines)
            at = k % HALF
            for h in range(halves):
                panel_ref[h, k : k + 1, :] = lines[h][at : at + 1, :]

        entry = corner(block_ref)
        below = [block_ref[k, HALF:PANEL, :] for k in range(HALF)]
        scales = factor(entry, below)
        for k in range(HALF):
            write_lines(k, [entry[k, m] for m in range(k)], scales[k])
            lower_ref[k] = below[k]
        cross = {(m, k): repeated(lower_ref, k, m) for k in range(HALF) for m in range(HALF)}
        for m in range(HALF):
            column = block_ref[HALF + m, HALF:PANEL, :]
            for k in range(HALF):
                column = column - below[k] * cross[m, k]
            second_ref[m] = column
        entry = corner(second_ref)
        scales = factor(entry, None)
        for k in range(HALF):
            weights = [cross[k, m] for m in range(HALF)] + [entry[k, m] for m in range(k)]
            write_lines(HALF + k, weights, scales[k])
        panel = jnp.concatenate([panel_ref[h] for h in range(halves)], 1)
        right = jnp.where(col >= first + PANEL, panel, 0.0)
        ah, am, al = split_three(right)
        bh, bm, bl = split_three(panel)
        lhs = jnp.concatenate([ah, ah, am, am, ah, al], 0)
        rhs = jnp.concatenate([bh, bm, bh, bm, bl, bh], 0)
        update = lax.dot_general(
            lhs[:, start_row:], rhs, (((0,), (0,)), ((), ())), preferred_element_type=f32
        )
        below = work_ref[start_row:, :]
        big = lax.broadcasted_iota(jnp.int32, below.shape, 1)
        inside = (big >= first) & (big < first + PANEL)
        work_ref[start_row:, :] = jnp.where(inside, 0.0, below) - update
        work_ref[pl.ds(first, PANEL), :] = panel

    per = LANES // PANEL
    for h in range(halves):
        lax.fori_loop(h * per, (h + 1) * per, lambda p, _: (step(p, h * LANES), 0)[1], 0)


def rotate_kernel(
    band_ref, count_ref, mine_ref, theirs_ref, own_ref, other_ref, out_ref, work_ref,
    block_ref, panel_ref, lower_ref, second_ref, result_ref, sems
):
    half = LANES // 2
    band = band_ref[0]
    mine, theirs = mine_ref[...] * count_ref[0], theirs_ref[...] * count_ref[0]
    top = jnp.where(band == 0, mine, theirs)
    bottom = jnp.where(band == 0, theirs, mine)
    packed = jnp.concatenate([top[0:half], bottom[0:half]], 0)
    cross = jnp.concatenate([top[half:LANES], bottom[half:LANES]], 0)
    diag = top[LANES : LANES + 1] + bottom[LANES : LANES + 1]
    flipped = packed.T
    row = lax.broadcasted_iota(jnp.int32, (LANES, LANES), 0)
    col = lax.broadcasted_iota(jnp.int32, (LANES, LANES), 1)
    work_ref[0:LANES, 0:LANES] = jnp.where(col >= row, packed, flipped)
    work_ref[0:LANES, LANES:] = cross
    work_ref[LANES:, 0:LANES] = cross.T
    tail = jnp.where(col < row, packed, flipped)
    work_ref[LANES:, LANES:] = jnp.where(col == row, jnp.broadcast_to(diag, tail.shape), tail)
    invert_factor(work_ref, block_ref, panel_ref, lower_ref, second_ref)
    lower = jnp.where(col <= row, 1.0, 0.0)
    first = work_ref[0:LANES, 0:LANES] * lower
    last = work_ref[LANES:, LANES:] * lower
    corner = work_ref[LANES:, 0:LANES]
    from_own = jnp.where(band == 0, first, last)
    from_other = jnp.where(band == 0, jnp.zeros_like(corner), corner)
    weights = jnp.concatenate([from_own, from_other], 1)
    high = weights.astype(bf16)
    low = (weights - high.astype(f32)).astype(bf16)
    weights = jnp.concatenate([high, low], 0)
    chunk = own_ref.shape[0] // sems.shape[0]
    copies = []
    for c in range(sems.shape[0]):
        rows = pl.ds(c * chunk, chunk)
        both = jnp.concatenate([own_ref[rows, :], other_ref[rows, :]], 1)
        product = lax.dot_general(
            both, weights, (((1,), (1,)), ((), ())), preferred_element_type=f32
        )
        result_ref[rows, :] = product[:, :LANES] + product[:, LANES:]
        copies.append(pltpu.make_async_copy(result_ref.at[rows], out_ref.at[rows], sems.at[c]))
        copies[-1].start()
    for copy in copies:
        copy.wait()


def rotate(band, inv_count, mine, theirs, own, other):
    return pl.pallas_call(
        rotate_kernel,
        out_shape=jax.ShapeDtypeStruct(own.shape, f32),
        in_specs=[smem, smem] + [vmem] * 4,
        out_specs=hbm,
        scratch_shapes=[
            pltpu.VMEM((2 * LANES, 2 * LANES), f32),
            pltpu.VMEM((PANEL, PANEL, LANES), f32),
            pltpu.VMEM((2, PANEL, LANES), f32),
            pltpu.VMEM((HALF, HALF, LANES), f32),
            pltpu.VMEM((HALF, HALF, LANES), f32),
            pltpu.VMEM(own.shape, f32),
            pltpu.SemaphoreType.DMA((8,)),
        ],
        compiler_params=grant(12),
    )(band, inv_count, mine, theirs, own, other)


def summed_over(value, axis):
    size = lax.axis_size(axis)
    if size & (size - 1):
        return lax.psum(value, axis)
    stride = 1
    while stride < size:
        count = min(4, size // stride)
        parts = [
            lax.ppermute(value, axis, [(i, i ^ (k * stride)) for i in range(size)])
            for k in range(1, count)
        ]
        value = value + sum(parts[1:], parts[0])
        stride *= count
    return value


def swapped(value):
    return lax.ppermute(value, "band", [(0, 1), (1, 0)])


def on_device(wavefunctions, bounds, cell_matrix, cell_scale, potential, cell_nodes, face_nodes):
    nodes = wavefunctions.shape[0]
    cell_matrix = pltpu.with_memory_space_constraint(cell_matrix, pltpu.HBM)
    cell_scale = pltpu.with_memory_space_constraint(cell_scale, pltpu.HBM)
    held = pltpu.with_memory_space_constraint(wavefunctions, pltpu.HBM)
    faces = jnp.where(face_nodes < 0, nodes, face_nodes).reshape(-1)
    potential = potential.reshape(-1, LANES)
    at = lax.axis_index("dom").astype(jnp.int32)
    band = lax.axis_index("band").astype(jnp.int32)
    kind = jnp.arange(4, dtype=jnp.int32) ^ (2 * band)
    flip = jnp.where(kind < 2, at % 2, at // 2 % 2)
    side = kind // 2 * 2 + ((kind % 2) ^ flip)
    pairs = exchange_pairs(lax.axis_size("dom"))

    def exchanged(blocks):
        return [
            lax.ppermute(
                block,
                ("dom", "band"),
                [(2 * i + b, 2 * j + b) for b in range(2) for i, j in pairs[q ^ (2 * b)]],
            )
            for q, block in enumerate(blocks)
        ]

    cells = functools.partial(apply_cells, side, cell_nodes.reshape(-1), cell_scale, cell_matrix)
    blocks, vectors = send_faces(side, faces, held)
    own, *sums = cells(vectors, exchanged(blocks))
    degree_one, *blocks = finish_first(
        side, faces, bounds, own, potential, vectors, exchanged(sums)
    )
    own, *sums = cells(degree_one, exchanged(blocks))
    degree_two = finish_second(
        side, faces, bounds, own, potential, degree_one, exchanged(sums), wavefunctions
    )
    other = swapped(degree_two)
    band = band.reshape(1)
    mine = summed_over(margin_rows(band, degree_two, other), "dom")
    inv_count = jnp.full((1,), 1.0 / (nodes * lax.axis_size("dom")), f32)
    return rotate(band, inv_count, mine, swapped(mine), degree_two, other)


def solution(mesh):
    return jax.shard_map(
        on_device,
        mesh=mesh,
        in_specs=(
            P(("kpt", "dom"), "band"),
            P("kpt"),
            P(),
            P("dom"),
            P("dom"),
            P("dom", None),
            P("dom", None),
        ),
        out_specs=P(("kpt", "dom"), "band"),
        check_vma=False,
    )
```

```python
import functools

import jax
import jax.numpy as jnp
from jax import lax
from jax.experimental import pallas as pl
from jax.experimental.pallas import tpu as pltpu
from jax.sharding import PartitionSpec as P

peer_offsets = (1, -1, 2, -2)
f32, bf16 = jnp.float32, jnp.bfloat16
LANES, GROUP, PANEL, HALF = 128, 8, 16, 8
vmem = pl.BlockSpec(memory_space=pltpu.VMEM)
smem = pl.BlockSpec(memory_space=pltpu.SMEM)
hbm = pl.BlockSpec(memory_space=pltpu.HBM)


def grant(mib):
    return pltpu.CompilerParams(vmem_limit_bytes=mib * 2**20)


def exchange_pairs(size):
    first = ([i for i in range(size) if i % 2 == 0], 1)
    second = ([i for i in range(size) if i % 2 == 1], 1)
    third = ([i for i in range(size) if i % 4 < 2], 2)
    fourth = ([i for i in range(size) if i % 4 >= 2], 2)
    return [
        [pair for i in starts if i + by < size for pair in ((i, i + by), (i + by, i))]
        for starts, by in (first, second, third, fourth)
    ]


def gather_faces(order_ref, faces_ref, table_ref, rows_ref, out_refs):
    slots = out_refs[0].shape[0]
    for q in range(4):
        offset = order_ref[q] * slots

        def body(step, _):
            base = step * 64
            for u in range(64):
                face = faces_ref[offset + base + u]
                rows_ref[pl.ds(base + u, 1), :] = table_ref[pl.ds(face, 1), :]
            return 0

        lax.fori_loop(0, slots // 64, body, 0)
        out_refs[q][...] = rows_ref[...].astype(bf16)


def face_kernel(
    order_ref, faces_ref, given_ref, o0, o1, o2, o3, vec_ref, table_ref, rows_ref, sems
):
    nodes, chunk = vec_ref.shape[0], vec_ref.shape[0] // sems.shape[0]
    copies = []
    for c in range(sems.shape[0]):
        rows = pl.ds(c * chunk, chunk)
        copies.append(pltpu.make_async_copy(given_ref.at[rows], vec_ref.at[rows], sems.at[c]))
        copies[-1].start()
    table_ref[nodes : nodes + 8, :] = jnp.zeros((8, LANES), f32)
    for c, copy in enumerate(copies):
        rows = pl.ds(c * chunk, chunk)
        copy.wait()
        table_ref[rows, :] = vec_ref[rows, :].astype(f32)
    gather_faces(order_ref, faces_ref, table_ref, rows_ref, (o0, o1, o2, o3))


def send_faces(side, faces, vectors):
    nodes, slots = vectors.shape[0], faces.shape[0] // 4
    *blocks, vectors = pl.pallas_call(
        face_kernel,
        out_shape=[jax.ShapeDtypeStruct((slots, LANES), bf16)] * 4
        + [jax.ShapeDtypeStruct((nodes, LANES), bf16)],
        in_specs=[smem, smem, hbm],
        out_specs=[vmem] * 5,
        scratch_shapes=[
            pltpu.VMEM((nodes + 8, LANES), f32),
            pltpu.VMEM((slots, LANES), f32),
            pltpu.SemaphoreType.DMA((4,)),
        ],
        compiler_params=grant(8),
    )(side, faces, vectors)
    return blocks, vectors


def cells_kernel(
    order_ref, names_ref, scales_ref, whole_ref, vec_ref, h0, h1, h2, h3,
    own_ref, g0, g1, g2, g3, maps_ref, scale_ref, matrix_ref, ext_ref, in_ref, out_ref, sems, *acc
):
    nodes, slots = vec_ref.shape[0], h0.shape[0]
    size = matrix_ref.shape[0]
    ext = nodes + 4 * slots
    fetch = pltpu.make_async_copy(whole_ref, matrix_ref, sems.at[0])
    cells = scale_ref.shape[0]
    scale = pltpu.make_async_copy(scales_ref, scale_ref, sems.at[1])
    names = []
    for batch in range(cells // GROUP):
        part = pl.ds(batch * GROUP * size, GROUP * size)
        names.append(
            pltpu.make_async_copy(names_ref.at[part], maps_ref.at[part], sems.at[2 + batch])
        )
        names[-1].start()
    scale.start()
    fetch.start()
    for q, ghost in enumerate((h0, h1, h2, h3)):
        start = pl.multiple_of(nodes + (order_ref[q] ^ 1) * slots, slots)
        ext_ref[pl.ds(start, slots), :] = ghost[...].astype(f32)
    share = ext // (size // 32)
    ext_ref[0:nodes, :] = vec_ref[...].astype(f32)
    for first in range(0, cells, GROUP):
        names[first // GROUP].wait()

        def gather(step, _):
            base = step * 32
            if first == 0:
                cleared = pl.ds(pl.multiple_of(step * share, 8), share)
                for a in acc:
                    a[cleared, :] = jnp.zeros((share, LANES), f32)
            for u in range(32):
                for k in range(GROUP):
                    row = maps_ref[(first + k) * size + base + u]
                    in_ref[k, pl.ds(base + u, 1), :] = ext_ref[pl.ds(row, 1), :]
            return 0

        lax.fori_loop(0, size // 32, gather, 0)
        if first == 0:
            fetch.wait()
            scale.wait()
        for k in range(0, GROUP, 2):
            pair = jnp.concatenate([in_ref[k].astype(bf16), in_ref[k + 1].astype(bf16)], 1)
            product = jnp.dot(matrix_ref[...], pair, preferred_element_type=f32)
            out_ref[k] = product[:, :LANES] * scale_ref[first + k]
            out_ref[k + 1] = product[:, LANES:] * scale_ref[first + k + 1]

        def scatter(step, _):
            base = step * 32
            for u in range(32):
                rows = [maps_ref[(first + k) * size + base + u] for k in range(GROUP)]
                sums = [
                    acc[k][pl.ds(rows[k], 1), :] + out_ref[k, pl.ds(base + u, 1), :]
                    for k in range(GROUP)
                ]
                for k in range(GROUP):
                    acc[k][pl.ds(rows[k], 1), :] = sums[k]
            return 0

        lax.fori_loop(0, size // 32, scatter, 0)

    def total(start):
        rows = pl.ds(start, 64)
        parts = [a[rows, :] for a in acc]
        while len(parts) > 1:
            parts = [parts[i] + parts[i + 1] for i in range(0, len(parts), 2)]
        return parts[0]

    def reduce_own(step, _):
        start = pl.multiple_of(step * 64, 64)
        own_ref[pl.ds(start, 64), :] = total(start)
        return 0

    lax.fori_loop(0, nodes // 64, reduce_own, 0)
    for q, ghost in enumerate((g0, g1, g2, g3)):
        start = pl.multiple_of(nodes + (order_ref[q] ^ 1) * slots, slots)
        for r in range(0, slots, 64):
            ghost[r : r + 64, :] = total(pl.multiple_of(start + r, 64))


def apply_cells(side, maps, scale, matrix, vectors, ghosts):
    nodes, slots, size = vectors.shape[0], ghosts[0].shape[0], matrix.shape[0]
    ext = nodes + 4 * slots
    return pl.pallas_call(
        cells_kernel,
        out_shape=[jax.ShapeDtypeStruct((nodes, LANES), f32)]
        + [jax.ShapeDtypeStruct((slots, LANES), f32)] * 4,
        in_specs=[smem, hbm, hbm, hbm] + [vmem] * 5,
        out_specs=[vmem] * 5,
        scratch_shapes=[
            pltpu.SMEM(maps.shape, jnp.int32),
            pltpu.SMEM(scale.shape, f32),
            pltpu.VMEM((size, size), bf16),
            pltpu.VMEM((ext, LANES), f32),
            pltpu.VMEM((GROUP, size, LANES), f32),
            pltpu.VMEM((GROUP, size, LANES), f32),
            pltpu.SemaphoreType.DMA((2 + scale.shape[0] // GROUP,)),
        ]
        + [pltpu.VMEM((ext, LANES), f32)] * GROUP,
        compiler_params=grant(36),
    )(side, maps, scale, matrix, vectors, *ghosts)


def add_returned(order_ref, faces_ref, pieces, count, acc):
    for a in acc:
        a[...] = jnp.zeros(a.shape, f32)
    lists = [order_ref[q] * block.shape[0] + first for q, first, block in pieces]

    def body(step, _):
        base = step * 16
        for u in range(16):
            rows = [faces_ref[start + base + u] for start in lists]
            sums = [
                a[pl.ds(row, 1), :] + block[pl.ds(first + base + u, 1), :]
                for a, row, (_, first, block) in zip(acc, rows, pieces)
            ]
            for a, row, value in zip(acc, rows, sums):
                a[pl.ds(row, 1), :] = value
        return 0

    lax.fori_loop(0, count // 16, body, 0)


def early_kernel(order_ref, faces_ref, own_ref, r0, out_ref, *acc):
    half = r0.shape[0] // 2
    add_returned(order_ref, faces_ref, [(0, 0, r0), (0, half, r0)], half, acc)

    def combine(step, _):
        rows = pl.ds(pl.multiple_of(step * 64, 64), 64)
        out_ref[rows, :] = own_ref[rows, :] + (acc[0][rows, :] + acc[1][rows, :])
        return 0

    lax.fori_loop(0, own_ref.shape[0] // 64, combine, 0)


def add_early(side, faces, own, returned):
    nodes = own.shape[0]
    return pl.pallas_call(
        early_kernel,
        out_shape=jax.ShapeDtypeStruct((nodes, LANES), f32),
        in_specs=[smem] * 2 + [vmem] * 2,
        out_specs=vmem,
        scratch_shapes=[pltpu.VMEM((nodes + 8, LANES), f32)] * 2,
        compiler_params=grant(12),
        cost_estimate=pl.CostEstimate(flops=10**6, bytes_accessed=4 * 10**6, transcendentals=0),
    )(side, faces, own, returned)


def filtered(interval_ref, own_ref, pot_ref, vec_ref, acc, write):
    low = jnp.full((1, LANES), interval_ref[0])
    high = jnp.full((1, LANES), interval_ref[1])
    center, half_width = (low + high) / 2.0, (high - low) / 2.0
    inverse = 1.0 / half_width
    shifts = ((pot_ref[...] - center) * inverse).T
    for step in range(shifts.shape[1]):
        rows = slice(step * LANES, (step + 1) * LANES)
        image = (own_ref[rows, :] + acc[0][rows, :]) + (acc[1][rows, :] + acc[2][rows, :])
        shift = jnp.broadcast_to(shifts[:, step : step + 1], (LANES, LANES))
        write(rows, image * inverse + shift * vec_ref[rows, :].astype(f32))


def first_kernel(
    order_ref, faces_ref, interval_ref, own_ref, pot_ref, vec_ref, r1, r2, r3,
    out_ref, o0, o1, o2, o3, table_ref, rows_ref, *acc
):
    nodes = vec_ref.shape[0]
    late = [(1, 0, r1), (2, 0, r2), (3, 0, r3)]
    add_returned(order_ref, faces_ref, late, r1.shape[0], acc)

    def write(rows, value):
        value = value.astype(bf16)
        out_ref[rows, :] = value
        table_ref[rows, :] = value.astype(f32)

    filtered(interval_ref, own_ref, pot_ref, vec_ref, acc, write)
    table_ref[nodes : nodes + 8, :] = jnp.zeros((8, LANES), f32)

    gather_faces(order_ref, faces_ref, table_ref, rows_ref, (o0, o1, o2, o3))


def second_kernel(
    order_ref, faces_ref, interval_ref, own_ref, pot_ref, vec_ref, r1, r2, r3, old_ref,
    out_ref, *acc
):
    late = [(1, 0, r1), (2, 0, r2), (3, 0, r3)]
    add_returned(order_ref, faces_ref, late, r1.shape[0], acc)

    def write(rows, value):
        out_ref[rows, :] = (2.0 * value - old_ref[rows, :].astype(f32)).astype(bf16)

    filtered(interval_ref, own_ref, pot_ref, vec_ref, acc, write)


def finish_first(side, faces, interval, own, potential, vectors, returned):
    nodes, slots = vectors.shape[0], returned[0].shape[0]
    own = add_early(side, faces, own, returned[0])
    return pl.pallas_call(
        first_kernel,
        out_shape=[jax.ShapeDtypeStruct((nodes, LANES), bf16)]
        + [jax.ShapeDtypeStruct((slots, LANES), bf16)] * 4,
        in_specs=[smem] * 3 + [vmem] * 6,
        out_specs=[vmem] * 5,
        scratch_shapes=[
            pltpu.VMEM((nodes + 8, LANES), f32),
            pltpu.VMEM((slots, LANES), f32),
        ]
        + [pltpu.VMEM((nodes + 8, LANES), f32)] * 3,
        compiler_params=grant(20),
    )(side, faces, interval, own, potential, vectors, *returned[1:])


def finish_second(side, faces, interval, own, potential, vectors, returned, old):
    nodes = vectors.shape[0]
    own = add_early(side, faces, own, returned[0])
    return pl.pallas_call(
        second_kernel,
        out_shape=jax.ShapeDtypeStruct((nodes, LANES), bf16),
        in_specs=[smem] * 3 + [vmem] * 7,
        out_specs=vmem,
        scratch_shapes=[pltpu.VMEM((nodes + 8, LANES), f32)] * 3,
        compiler_params=grant(20),
    )(side, faces, interval, own, potential, vectors, *returned[1:], old)


def margin_kernel(band_ref, own_ref, other_ref, out_ref):
    half = LANES // 2
    nt = functools.partial(
        lax.dot_general,
        dimension_numbers=(((0,), (0,)), ((), ())),
        preferred_element_type=f32,
    )

    def write(low, high, band):
        low_rows = low[:, band * half : (band + 1) * half]
        high_rows = high[:, band * half : (band + 1) * half]
        block = nt(low_rows, low)
        cross = nt(low_rows, high)
        tail = nt(high_rows, high)
        row = lax.broadcasted_iota(jnp.int32, (half, LANES), 0) + band * half
        col = lax.broadcasted_iota(jnp.int32, (half, LANES), 1)
        out_ref[0:half, :] = jnp.where(col >= row, block, tail)
        out_ref[half : 2 * half, :] = cross
        diag = jnp.sum(jnp.where(col == row, tail, 0.0), 0, keepdims=True)
        out_ref[2 * half : 2 * half + 8, :] = jnp.broadcast_to(diag, (8, LANES))

    @pl.when(band_ref[0] == 0)
    def _():
        write(own_ref[...], other_ref[...], 0)

    @pl.when(band_ref[0] != 0)
    def _():
        write(other_ref[...], own_ref[...], 1)


def margin_rows(band, own, other):
    return pl.pallas_call(
        margin_kernel,
        out_shape=jax.ShapeDtypeStruct((LANES + 8, LANES), f32),
        in_specs=[smem, vmem, vmem],
        out_specs=vmem,
        compiler_params=grant(12),
    )(band, own, other)


def split_three(x):
    high = x.astype(bf16)
    rest = x - high.astype(f32)
    mid = rest.astype(bf16)
    return high, mid, (rest - mid.astype(f32)).astype(bf16)


def invert_factor(work_ref, block_ref, panel_ref, lower_ref, second_ref):
    total = work_ref.shape[0]
    halves = total // LANES
    col = lax.broadcasted_iota(jnp.int32, (PANEL, total), 1)
    row = lax.broadcasted_iota(jnp.int32, (PANEL, total), 0)

    def step(p, start_row):
        first = pl.multiple_of(p * PANEL, PANEL)
        rows = work_ref[pl.ds(first, PANEL), :]
        block = rows[:, start_row : start_row + LANES]
        block = pltpu.roll(block, lax.rem(total - first, LANES), 1)
        for k in range(PANEL):
            block_ref[k] = jnp.broadcast_to(block[:, k : k + 1], (PANEL, LANES))
        panel = jnp.where((col >= first) & (col < first + PANEL), 0.0, rows)
        panel = jnp.where(col == row + first, 1.0, panel)
        for h in range(halves):
            panel_ref[h] = panel[:, h * LANES : (h + 1) * LANES]

        def repeated(ref, k, i):
            return ref[k, pl.ds(i, HALF, stride=0), :]

        def factor(entry, below):
            scales = []
            for k in range(HALF):
                scale = lax.rsqrt(entry[k, k])
                scales.append(scale)
                for i in range(k + 1, HALF):
                    entry[i, k] = entry[i, k] * scale
                for i in range(k + 1, HALF):
                    for m in range(k + 1, i + 1):
                        entry[i, m] = entry[i, m] - entry[i, k] * entry[m, k]
                if below:
                    below[k] = below[k] * scale
                    for m in range(k + 1, HALF):
                        below[m] = below[m] - below[k] * entry[m, k]
            return scales

        def corner(ref):
            return {(i, k): repeated(ref, k, i) for k in range(HALF) for i in range(k, HALF)}

        done = []

        def write_lines(k, weights, scale):
            lines = [panel_ref[h, pl.ds(k, HALF, stride=0), :] for h in range(halves)]
            for m, weight in enumerate(weights):
                lines = [line - weight * old for line, old in zip(lines, done[m])]
            lines = [line * scale for line in lines]
            done.append(lines)
            at = k % HALF
            for h in range(halves):
                panel_ref[h, k : k + 1, :] = lines[h][at : at + 1, :]

        entry = corner(block_ref)
        below = [block_ref[k, HALF:PANEL, :] for k in range(HALF)]
        scales = factor(entry, below)
        for k in range(HALF):
            write_lines(k, [entry[k, m] for m in range(k)], scales[k])
            lower_ref[k] = below[k]
        cross = {(m, k): repeated(lower_ref, k, m) for k in range(HALF) for m in range(HALF)}
        for m in range(HALF):
            column = block_ref[HALF + m, HALF:PANEL, :]
            for k in range(HALF):
                column = column - below[k] * cross[m, k]
            second_ref[m] = column
        entry = corner(second_ref)
        scales = factor(entry, None)
        for k in range(HALF):
            weights = [cross[k, m] for m in range(HALF)] + [entry[k, m] for m in range(k)]
            write_lines(HALF + k, weights, scales[k])
        panel = jnp.concatenate([panel_ref[h] for h in range(halves)], 1)
        right = jnp.where(col >= first + PANEL, panel, 0.0)
        ah, am, al = split_three(right)
        bh, bm, bl = split_three(panel)
        lhs = jnp.concatenate([ah, ah, am, am, ah, al], 0)
        rhs = jnp.concatenate([bh, bm, bh, bm, bl, bh], 0)
        update = lax.dot_general(
            lhs[:, start_row:], rhs, (((0,), (0,)), ((), ())), preferred_element_type=f32
        )
        below = work_ref[start_row:, :]
        big = lax.broadcasted_iota(jnp.int32, below.shape, 1)
        inside = (big >= first) & (big < first + PANEL)
        work_ref[start_row:, :] = jnp.where(inside, 0.0, below) - update
        work_ref[pl.ds(first, PANEL), :] = panel

    per = LANES // PANEL
    for h in range(halves):
        lax.fori_loop(h * per, (h + 1) * per, lambda p, _: (step(p, h * LANES), 0)[1], 0)


def rotate_kernel(
    band_ref, count_ref, mine_ref, theirs_ref, own_ref, other_ref, out_ref, work_ref,
    block_ref, panel_ref, lower_ref, second_ref, result_ref, sems
):
    half = LANES // 2
    band = band_ref[0]
    mine, theirs = mine_ref[...] * count_ref[0], theirs_ref[...] * count_ref[0]
    top = jnp.where(band == 0, mine, theirs)
    bottom = jnp.where(band == 0, theirs, mine)
    packed = jnp.concatenate([top[0:half], bottom[0:half]], 0)
    cross = jnp.concatenate([top[half:LANES], bottom[half:LANES]], 0)
    diag = top[LANES : LANES + 1] + bottom[LANES : LANES + 1]
    flipped = packed.T
    row = lax.broadcasted_iota(jnp.int32, (LANES, LANES), 0)
    col = lax.broadcasted_iota(jnp.int32, (LANES, LANES), 1)
    work_ref[0:LANES, 0:LANES] = jnp.where(col >= row, packed, flipped)
    work_ref[0:LANES, LANES:] = cross
    work_ref[LANES:, 0:LANES] = cross.T
    tail = jnp.where(col < row, packed, flipped)
    work_ref[LANES:, LANES:] = jnp.where(col == row, jnp.broadcast_to(diag, tail.shape), tail)
    invert_factor(work_ref, block_ref, panel_ref, lower_ref, second_ref)
    lower = jnp.where(col <= row, 1.0, 0.0)
    first = work_ref[0:LANES, 0:LANES] * lower
    last = work_ref[LANES:, LANES:] * lower
    corner = work_ref[LANES:, 0:LANES]
    from_own = jnp.where(band == 0, first, last)
    from_other = jnp.where(band == 0, jnp.zeros_like(corner), corner)
    weights = jnp.concatenate([from_own, from_other], 1)
    high = weights.astype(bf16)
    low = (weights - high.astype(f32)).astype(bf16)
    weights = jnp.concatenate([high, low], 0)
    chunk = own_ref.shape[0] // sems.shape[0]
    copies = []
    for c in range(sems.shape[0]):
        rows = pl.ds(c * chunk, chunk)
        both = jnp.concatenate([own_ref[rows, :], other_ref[rows, :]], 1)
        product = lax.dot_general(
            both, weights, (((1,), (1,)), ((), ())), preferred_element_type=f32
        )
        result_ref[rows, :] = product[:, :LANES] + product[:, LANES:]
        copies.append(pltpu.make_async_copy(result_ref.at[rows], out_ref.at[rows], sems.at[c]))
        copies[-1].start()
    for copy in copies:
        copy.wait()


def rotate(band, inv_count, mine, theirs, own, other):
    return pl.pallas_call(
        rotate_kernel,
        out_shape=jax.ShapeDtypeStruct(own.shape, f32),
        in_specs=[smem, smem] + [vmem] * 4,
        out_specs=hbm,
        scratch_shapes=[
            pltpu.VMEM((2 * LANES, 2 * LANES), f32),
            pltpu.VMEM((PANEL, PANEL, LANES), f32),
            pltpu.VMEM((2, PANEL, LANES), f32),
            pltpu.VMEM((HALF, HALF, LANES), f32),
            pltpu.VMEM((HALF, HALF, LANES), f32),
            pltpu.VMEM(own.shape, f32),
            pltpu.SemaphoreType.DMA((8,)),
        ],
        compiler_params=grant(12),
    )(band, inv_count, mine, theirs, own, other)


def summed_over(value, axis):
    size = lax.axis_size(axis)
    if size & (size - 1):
        return lax.psum(value, axis)
    stride = 1
    while stride < size:
        count = min(4, size // stride)
        parts = [
            lax.ppermute(value, axis, [(i, i ^ (k * stride)) for i in range(size)])
            for k in range(1, count)
        ]
        value = value + sum(parts[1:], parts[0])
        stride *= count
    return value


def swapped(value):
    return lax.ppermute(value, "band", [(0, 1), (1, 0)])


def on_device(wavefunctions, bounds, cell_matrix, cell_scale, potential, cell_nodes, face_nodes):
    nodes = wavefunctions.shape[0]
    cell_matrix = pltpu.with_memory_space_constraint(cell_matrix, pltpu.HBM)
    cell_scale = pltpu.with_memory_space_constraint(cell_scale, pltpu.HBM)
    held = pltpu.with_memory_space_constraint(wavefunctions, pltpu.HBM)
    faces = jnp.where(face_nodes < 0, nodes, face_nodes).reshape(-1)
    potential = potential.reshape(-1, LANES)
    at = lax.axis_index("dom").astype(jnp.int32)
    band = lax.axis_index("band").astype(jnp.int32)
    kind = jnp.arange(4, dtype=jnp.int32) ^ (2 * band)
    flip = jnp.where(kind < 2, at % 2, at // 2 % 2)
    side = kind // 2 * 2 + ((kind % 2) ^ flip)
    pairs = exchange_pairs(lax.axis_size("dom"))

    def exchanged(blocks):
        return [
            lax.ppermute(
                block,
                ("dom", "band"),
                [(2 * i + b, 2 * j + b) for b in range(2) for i, j in pairs[q ^ (2 * b)]],
            )
            for q, block in enumerate(blocks)
        ]

    cells = functools.partial(apply_cells, side, cell_nodes.reshape(-1), cell_scale, cell_matrix)
    blocks, vectors = send_faces(side, faces, held)
    own, *sums = cells(vectors, exchanged(blocks))
    degree_one, *blocks = finish_first(
        side, faces, bounds, own, potential, vectors, exchanged(sums)
    )
    own, *sums = cells(degree_one, exchanged(blocks))
    degree_two = finish_second(
        side, faces, bounds, own, potential, degree_one, exchanged(sums), wavefunctions
    )
    other = swapped(degree_two)
    band = band.reshape(1)
    mine = summed_over(margin_rows(band, degree_two, other), "dom")
    inv_count = jnp.full((1,), 1.0 / (nodes * lax.axis_size("dom")), f32)
    return rotate(band, inv_count, mine, swapped(mine), degree_two, other)


def solution(mesh):
    return jax.shard_map(
        on_device,
        mesh=mesh,
        in_specs=(
            P(("kpt", "dom"), "band"),
            P("kpt"),
            P(),
            P("dom"),
            P("dom"),
            P("dom", None),
            P("dom", None),
        ),
        out_specs=P(("kpt", "dom"), "band"),
        check_vma=False,
    )
```

```python
import functools

import jax
import jax.numpy as jnp
from jax import lax
from jax.experimental import pallas as pl
from jax.experimental.pallas import tpu as pltpu
from jax.sharding import PartitionSpec as P

peer_offsets = (1, -1, 2, -2)
f32, bf16 = jnp.float32, jnp.bfloat16
LANES, GROUP, PANEL, HALF = 128, 8, 16, 8
vmem = pl.BlockSpec(memory_space=pltpu.VMEM)
smem = pl.BlockSpec(memory_space=pltpu.SMEM)
hbm = pl.BlockSpec(memory_space=pltpu.HBM)


def grant(mib):
    return pltpu.CompilerParams(vmem_limit_bytes=mib * 2**20)


def exchange_pairs(size):
    first = ([i for i in range(size) if i % 2 == 0], 1)
    second = ([i for i in range(size) if i % 2 == 1], 1)
    third = ([i for i in range(size) if i % 4 < 2], 2)
    fourth = ([i for i in range(size) if i % 4 >= 2], 2)
    return [
        [pair for i in starts if i + by < size for pair in ((i, i + by), (i + by, i))]
        for starts, by in (first, second, third, fourth)
    ]


def gather_faces(order_ref, faces_ref, table_ref, rows_ref, out_refs):
    slots = out_refs[0].shape[0]
    for q in range(4):
        offset = order_ref[q] * slots

        def body(step, _):
            base = step * 64
            for u in range(64):
                face = faces_ref[offset + base + u]
                rows_ref[pl.ds(base + u, 1), :] = table_ref[pl.ds(face, 1), :]
            return 0

        lax.fori_loop(0, slots // 64, body, 0)
        out_refs[q][...] = rows_ref[...].astype(bf16)


def face_kernel(
    order_ref, lists_ref, given_ref, o0, o1, o2, o3, vec_ref, faces_ref, table_ref, rows_ref, sems
):
    nodes, chunks = vec_ref.shape[0], sems.shape[0] - 1
    chunk = nodes // chunks
    names = pltpu.make_async_copy(lists_ref, faces_ref, sems.at[chunks])
    names.start()
    copies = []
    for c in range(chunks):
        rows = pl.ds(c * chunk, chunk)
        copies.append(pltpu.make_async_copy(given_ref.at[rows], vec_ref.at[rows], sems.at[c]))
        copies[-1].start()
    table_ref[0:8, :] = jnp.zeros((8, LANES), f32)
    for c, copy in enumerate(copies):
        copy.wait()
        rows = pl.ds(c * chunk, chunk)
        table_ref[pl.ds(8 + c * chunk, chunk), :] = vec_ref[rows, :].astype(f32)
    names.wait()
    for q, out_ref in enumerate((o0, o1, o2, o3)):
        face = order_ref[q]
        for slot in range(rows_ref.shape[0]):
            row = faces_ref[face, slot] + 8
            rows_ref[slot : slot + 1, :] = table_ref[pl.ds(row, 1), :]
        out_ref[...] = rows_ref[...].astype(bf16)


def send_faces(side, face_nodes, vectors):
    nodes, slots = vectors.shape[0], face_nodes.shape[1]
    *blocks, vectors = pl.pallas_call(
        face_kernel,
        out_shape=[jax.ShapeDtypeStruct((slots, LANES), bf16)] * 4
        + [jax.ShapeDtypeStruct((nodes, LANES), bf16)],
        in_specs=[smem, hbm, hbm],
        out_specs=[vmem] * 5,
        scratch_shapes=[
            pltpu.SMEM(face_nodes.shape, jnp.int32),
            pltpu.VMEM((nodes + 8, LANES), f32),
            pltpu.VMEM((slots, LANES), f32),
            pltpu.SemaphoreType.DMA((5,)),
        ],
        compiler_params=grant(8),
    )(side, face_nodes, vectors)
    return blocks, vectors


def cells_kernel(
    order_ref, names_ref, scales_ref, whole_ref, vec_ref, h0, h1, h2, h3,
    own_ref, g0, g1, g2, g3, maps_ref, scale_ref, matrix_ref, ext_ref, in_ref, out_ref, sems, *acc
):
    nodes, slots = vec_ref.shape[0], h0.shape[0]
    size = matrix_ref.shape[0]
    ext = nodes + 4 * slots
    fetch = pltpu.make_async_copy(whole_ref, matrix_ref, sems.at[0])
    cells = scale_ref.shape[0]
    scale = pltpu.make_async_copy(scales_ref, scale_ref, sems.at[1])
    names = []
    for batch in range(cells // GROUP):
        part = pl.ds(batch * GROUP * size, GROUP * size)
        names.append(
            pltpu.make_async_copy(names_ref.at[part], maps_ref.at[part], sems.at[2 + batch])
        )
        names[-1].start()
    scale.start()
    fetch.start()
    for q, ghost in enumerate((h0, h1, h2, h3)):
        start = pl.multiple_of(nodes + (order_ref[q] ^ 1) * slots, slots)
        ext_ref[pl.ds(start, slots), :] = ghost[...].astype(f32)
    share = ext // (size // 32)
    ext_ref[0:nodes, :] = vec_ref[...].astype(f32)
    for first in range(0, cells, GROUP):
        names[first // GROUP].wait()

        def gather(step, _):
            base = step * 32
            if first == 0:
                cleared = pl.ds(pl.multiple_of(step * share, 8), share)
                for a in acc:
                    a[cleared, :] = jnp.zeros((share, LANES), f32)
            for u in range(32):
                for k in range(GROUP):
                    row = maps_ref[(first + k) * size + base + u]
                    in_ref[k, pl.ds(base + u, 1), :] = ext_ref[pl.ds(row, 1), :]
            return 0

        lax.fori_loop(0, size // 32, gather, 0)
        if first == 0:
            fetch.wait()
            scale.wait()
        for k in range(0, GROUP, 2):
            pair = jnp.concatenate([in_ref[k].astype(bf16), in_ref[k + 1].astype(bf16)], 1)
            product = jnp.dot(matrix_ref[...], pair, preferred_element_type=f32)
            out_ref[k] = product[:, :LANES] * scale_ref[first + k]
            out_ref[k + 1] = product[:, LANES:] * scale_ref[first + k + 1]

        def scatter(step, _):
            base = step * 32
            for u in range(32):
                rows = [maps_ref[(first + k) * size + base + u] for k in range(GROUP)]
                sums = [
                    acc[k][pl.ds(rows[k], 1), :] + out_ref[k, pl.ds(base + u, 1), :]
                    for k in range(GROUP)
                ]
                for k in range(GROUP):
                    acc[k][pl.ds(rows[k], 1), :] = sums[k]
            return 0

        lax.fori_loop(0, size // 32, scatter, 0)

    def total(start):
        rows = pl.ds(start, 64)
        parts = [a[rows, :] for a in acc]
        while len(parts) > 1:
            parts = [parts[i] + parts[i + 1] for i in range(0, len(parts), 2)]
        return parts[0]

    def reduce_own(step, _):
        start = pl.multiple_of(step * 64, 64)
        own_ref[pl.ds(start, 64), :] = total(start)
        return 0

    lax.fori_loop(0, nodes // 64, reduce_own, 0)
    for q, ghost in enumerate((g0, g1, g2, g3)):
        start = pl.multiple_of(nodes + (order_ref[q] ^ 1) * slots, slots)
        for r in range(0, slots, 64):
            ghost[r : r + 64, :] = total(pl.multiple_of(start + r, 64))


def apply_cells(side, maps, scale, matrix, vectors, ghosts):
    nodes, slots, size = vectors.shape[0], ghosts[0].shape[0], matrix.shape[0]
    ext = nodes + 4 * slots
    return pl.pallas_call(
        cells_kernel,
        out_shape=[jax.ShapeDtypeStruct((nodes, LANES), f32)]
        + [jax.ShapeDtypeStruct((slots, LANES), f32)] * 4,
        in_specs=[smem, hbm, hbm, hbm] + [vmem] * 5,
        out_specs=[vmem] * 5,
        scratch_shapes=[
            pltpu.SMEM(maps.shape, jnp.int32),
            pltpu.SMEM(scale.shape, f32),
            pltpu.VMEM((size, size), bf16),
            pltpu.VMEM((ext, LANES), f32),
            pltpu.VMEM((GROUP, size, LANES), f32),
            pltpu.VMEM((GROUP, size, LANES), f32),
            pltpu.SemaphoreType.DMA((2 + scale.shape[0] // GROUP,)),
        ]
        + [pltpu.VMEM((ext, LANES), f32)] * GROUP,
        compiler_params=grant(36),
    )(side, maps, scale, matrix, vectors, *ghosts)


def add_returned(order_ref, faces_ref, pieces, count, acc):
    for a in acc:
        a[...] = jnp.zeros(a.shape, f32)
    lists = [order_ref[q] * block.shape[0] + first for q, first, block in pieces]

    def body(step, _):
        base = step * 16
        for u in range(16):
            rows = [faces_ref[start + base + u] for start in lists]
            sums = [
                a[pl.ds(row, 1), :] + block[pl.ds(first + base + u, 1), :]
                for a, row, (_, first, block) in zip(acc, rows, pieces)
            ]
            for a, row, value in zip(acc, rows, sums):
                a[pl.ds(row, 1), :] = value
        return 0

    lax.fori_loop(0, count // 16, body, 0)


def early_kernel(order_ref, faces_ref, own_ref, r0, out_ref, *acc):
    half = r0.shape[0] // 2
    add_returned(order_ref, faces_ref, [(0, 0, r0), (0, half, r0)], half, acc)

    def combine(step, _):
        rows = pl.ds(pl.multiple_of(step * 64, 64), 64)
        out_ref[rows, :] = own_ref[rows, :] + (acc[0][rows, :] + acc[1][rows, :])
        return 0

    lax.fori_loop(0, own_ref.shape[0] // 64, combine, 0)


def add_early(side, faces, own, returned):
    nodes = own.shape[0]
    return pl.pallas_call(
        early_kernel,
        out_shape=jax.ShapeDtypeStruct((nodes, LANES), f32),
        in_specs=[smem] * 2 + [vmem] * 2,
        out_specs=vmem,
        scratch_shapes=[pltpu.VMEM((nodes + 8, LANES), f32)] * 2,
        compiler_params=grant(12),
        cost_estimate=pl.CostEstimate(flops=10**6, bytes_accessed=4 * 10**6, transcendentals=0),
    )(side, faces, own, returned)


def filtered(interval_ref, own_ref, pot_ref, vec_ref, acc, write):
    low = jnp.full((1, LANES), interval_ref[0])
    high = jnp.full((1, LANES), interval_ref[1])
    center, half_width = (low + high) / 2.0, (high - low) / 2.0
    inverse = 1.0 / half_width
    shifts = ((pot_ref[...] - center) * inverse).T
    for step in range(shifts.shape[1]):
        rows = slice(step * LANES, (step + 1) * LANES)
        image = (own_ref[rows, :] + acc[0][rows, :]) + (acc[1][rows, :] + acc[2][rows, :])
        shift = jnp.broadcast_to(shifts[:, step : step + 1], (LANES, LANES))
        write(rows, image * inverse + shift * vec_ref[rows, :].astype(f32))


def first_kernel(
    order_ref, faces_ref, interval_ref, own_ref, pot_ref, vec_ref, r1, r2, r3,
    out_ref, o0, o1, o2, o3, table_ref, rows_ref, *acc
):
    nodes = vec_ref.shape[0]
    late = [(1, 0, r1), (2, 0, r2), (3, 0, r3)]
    add_returned(order_ref, faces_ref, late, r1.shape[0], acc)

    def write(rows, value):
        value = value.astype(bf16)
        out_ref[rows, :] = value
        table_ref[rows, :] = value.astype(f32)

    filtered(interval_ref, own_ref, pot_ref, vec_ref, acc, write)
    table_ref[nodes : nodes + 8, :] = jnp.zeros((8, LANES), f32)

    gather_faces(order_ref, faces_ref, table_ref, rows_ref, (o0, o1, o2, o3))


def second_kernel(
    order_ref, faces_ref, interval_ref, own_ref, pot_ref, vec_ref, r1, r2, r3, old_ref,
    out_ref, *acc
):
    late = [(1, 0, r1), (2, 0, r2), (3, 0, r3)]
    add_returned(order_ref, faces_ref, late, r1.shape[0], acc)

    def write(rows, value):
        out_ref[rows, :] = (2.0 * value - old_ref[rows, :].astype(f32)).astype(bf16)

    filtered(interval_ref, own_ref, pot_ref, vec_ref, acc, write)


def finish_first(side, faces, interval, own, potential, vectors, returned):
    nodes, slots = vectors.shape[0], returned[0].shape[0]
    own = add_early(side, faces, own, returned[0])
    return pl.pallas_call(
        first_kernel,
        out_shape=[jax.ShapeDtypeStruct((nodes, LANES), bf16)]
        + [jax.ShapeDtypeStruct((slots, LANES), bf16)] * 4,
        in_specs=[smem] * 3 + [vmem] * 6,
        out_specs=[vmem] * 5,
        scratch_shapes=[
            pltpu.VMEM((nodes + 8, LANES), f32),
            pltpu.VMEM((slots, LANES), f32),
        ]
        + [pltpu.VMEM((nodes + 8, LANES), f32)] * 3,
        compiler_params=grant(20),
    )(side, faces, interval, own, potential, vectors, *returned[1:])


def finish_second(side, faces, interval, own, potential, vectors, returned, old):
    nodes = vectors.shape[0]
    own = add_early(side, faces, own, returned[0])
    return pl.pallas_call(
        second_kernel,
        out_shape=jax.ShapeDtypeStruct((nodes, LANES), bf16),
        in_specs=[smem] * 3 + [vmem] * 7,
        out_specs=vmem,
        scratch_shapes=[pltpu.VMEM((nodes + 8, LANES), f32)] * 3,
        compiler_params=grant(20),
    )(side, faces, interval, own, potential, vectors, *returned[1:], old)


def margin_kernel(band_ref, own_ref, other_ref, out_ref):
    half = LANES // 2
    nt = functools.partial(
        lax.dot_general,
        dimension_numbers=(((0,), (0,)), ((), ())),
        preferred_element_type=f32,
    )

    def write(low, high, band):
        low_rows = low[:, band * half : (band + 1) * half]
        high_rows = high[:, band * half : (band + 1) * half]
        block = nt(low_rows, low)
        cross = nt(low_rows, high)
        tail = nt(high_rows, high)
        row = lax.broadcasted_iota(jnp.int32, (half, LANES), 0) + band * half
        col = lax.broadcasted_iota(jnp.int32, (half, LANES), 1)
        out_ref[0:half, :] = jnp.where(col >= row, block, tail)
        out_ref[half : 2 * half, :] = cross
        diag = jnp.sum(jnp.where(col == row, tail, 0.0), 0, keepdims=True)
        out_ref[2 * half : 2 * half + 8, :] = jnp.broadcast_to(diag, (8, LANES))

    @pl.when(band_ref[0] == 0)
    def _():
        write(own_ref[...], other_ref[...], 0)

    @pl.when(band_ref[0] != 0)
    def _():
        write(other_ref[...], own_ref[...], 1)


def margin_rows(band, own, other):
    return pl.pallas_call(
        margin_kernel,
        out_shape=jax.ShapeDtypeStruct((LANES + 8, LANES), f32),
        in_specs=[smem, vmem, vmem],
        out_specs=vmem,
        compiler_params=grant(12),
    )(band, own, other)


def split_three(x):
    high = x.astype(bf16)
    rest = x - high.astype(f32)
    mid = rest.astype(bf16)
    return high, mid, (rest - mid.astype(f32)).astype(bf16)


def invert_factor(work_ref, block_ref, panel_ref, lower_ref, second_ref):
    total = work_ref.shape[0]
    halves = total // LANES
    col = lax.broadcasted_iota(jnp.int32, (PANEL, total), 1)
    row = lax.broadcasted_iota(jnp.int32, (PANEL, total), 0)

    def step(p, start_row):
        first = pl.multiple_of(p * PANEL, PANEL)
        rows = work_ref[pl.ds(first, PANEL), :]
        block = rows[:, start_row : start_row + LANES]
        block = pltpu.roll(block, lax.rem(total - first, LANES), 1)
        for k in range(PANEL):
            block_ref[k] = jnp.broadcast_to(block[:, k : k + 1], (PANEL, LANES))
        panel = jnp.where((col >= first) & (col < first + PANEL), 0.0, rows)
        panel = jnp.where(col == row + first, 1.0, panel)
        for h in range(halves):
            panel_ref[h] = panel[:, h * LANES : (h + 1) * LANES]

        def repeated(ref, k, i):
            return ref[k, pl.ds(i, HALF, stride=0), :]

        def factor(entry, below):
            scales = []
            for k in range(HALF):
                scale = lax.rsqrt(entry[k, k])
                scales.append(scale)
                for i in range(k + 1, HALF):
                    entry[i, k] = entry[i, k] * scale
                for i in range(k + 1, HALF):
                    for m in range(k + 1, i + 1):
                        entry[i, m] = entry[i, m] - entry[i, k] * entry[m, k]
                if below:
                    below[k] = below[k] * scale
                    for m in range(k + 1, HALF):
                        below[m] = below[m] - below[k] * entry[m, k]
            return scales

        def corner(ref):
            return {(i, k): repeated(ref, k, i) for k in range(HALF) for i in range(k, HALF)}

        done = []

        def write_lines(k, weights, scale):
            lines = [panel_ref[h, pl.ds(k, HALF, stride=0), :] for h in range(halves)]
            for m, weight in enumerate(weights):
                lines = [line - weight * old for line, old in zip(lines, done[m])]
            lines = [line * scale for line in lines]
            done.append(lines)
            at = k % HALF
            for h in range(halves):
                panel_ref[h, k : k + 1, :] = lines[h][at : at + 1, :]

        entry = corner(block_ref)
        below = [block_ref[k, HALF:PANEL, :] for k in range(HALF)]
        scales = factor(entry, below)
        for k in range(HALF):
            write_lines(k, [entry[k, m] for m in range(k)], scales[k])
            lower_ref[k] = below[k]
        cross = {(m, k): repeated(lower_ref, k, m) for k in range(HALF) for m in range(HALF)}
        for m in range(HALF):
            column = block_ref[HALF + m, HALF:PANEL, :]
            for k in range(HALF):
                column = column - below[k] * cross[m, k]
            second_ref[m] = column
        entry = corner(second_ref)
        scales = factor(entry, None)
        for k in range(HALF):
            weights = [cross[k, m] for m in range(HALF)] + [entry[k, m] for m in range(k)]
            write_lines(HALF + k, weights, scales[k])
        panel = jnp.concatenate([panel_ref[h] for h in range(halves)], 1)
        right = jnp.where(col >= first + PANEL, panel, 0.0)
        ah, am, al = split_three(right)
        bh, bm, bl = split_three(panel)
        lhs = jnp.concatenate([ah, ah, am, am, ah, al], 0)
        rhs = jnp.concatenate([bh, bm, bh, bm, bl, bh], 0)
        update = lax.dot_general(
            lhs[:, start_row:], rhs, (((0,), (0,)), ((), ())), preferred_element_type=f32
        )
        below = work_ref[start_row:, :]
        big = lax.broadcasted_iota(jnp.int32, below.shape, 1)
        inside = (big >= first) & (big < first + PANEL)
        work_ref[start_row:, :] = jnp.where(inside, 0.0, below) - update
        work_ref[pl.ds(first, PANEL), :] = panel

    per = LANES // PANEL
    for h in range(halves):
        lax.fori_loop(h * per, (h + 1) * per, lambda p, _: (step(p, h * LANES), 0)[1], 0)


def rotate_kernel(
    band_ref, count_ref, mine_ref, theirs_ref, own_ref, other_ref, out_ref, work_ref,
    block_ref, panel_ref, lower_ref, second_ref, result_ref, sems
):
    half = LANES // 2
    band = band_ref[0]
    mine, theirs = mine_ref[...] * count_ref[0], theirs_ref[...] * count_ref[0]
    top = jnp.where(band == 0, mine, theirs)
    bottom = jnp.where(band == 0, theirs, mine)
    packed = jnp.concatenate([top[0:half], bottom[0:half]], 0)
    cross = jnp.concatenate([top[half:LANES], bottom[half:LANES]], 0)
    diag = top[LANES : LANES + 1] + bottom[LANES : LANES + 1]
    flipped = packed.T
    row = lax.broadcasted_iota(jnp.int32, (LANES, LANES), 0)
    col = lax.broadcasted_iota(jnp.int32, (LANES, LANES), 1)
    work_ref[0:LANES, 0:LANES] = jnp.where(col >= row, packed, flipped)
    work_ref[0:LANES, LANES:] = cross
    work_ref[LANES:, 0:LANES] = cross.T
    tail = jnp.where(col < row, packed, flipped)
    work_ref[LANES:, LANES:] = jnp.where(col == row, jnp.broadcast_to(diag, tail.shape), tail)
    invert_factor(work_ref, block_ref, panel_ref, lower_ref, second_ref)
    lower = jnp.where(col <= row, 1.0, 0.0)
    first = work_ref[0:LANES, 0:LANES] * lower
    last = work_ref[LANES:, LANES:] * lower
    corner = work_ref[LANES:, 0:LANES]
    from_own = jnp.where(band == 0, first, last)
    from_other = jnp.where(band == 0, jnp.zeros_like(corner), corner)
    weights = jnp.concatenate([from_own, from_other], 1)
    high = weights.astype(bf16)
    low = (weights - high.astype(f32)).astype(bf16)
    weights = jnp.concatenate([high, low], 0)
    chunk = own_ref.shape[0] // sems.shape[0]
    copies = []
    for c in range(sems.shape[0]):
        rows = pl.ds(c * chunk, chunk)
        both = jnp.concatenate([own_ref[rows, :], other_ref[rows, :]], 1)
        product = lax.dot_general(
            both, weights, (((1,), (1,)), ((), ())), preferred_element_type=f32
        )
        result_ref[rows, :] = product[:, :LANES] + product[:, LANES:]
        copies.append(pltpu.make_async_copy(result_ref.at[rows], out_ref.at[rows], sems.at[c]))
        copies[-1].start()
    for copy in copies:
        copy.wait()


def rotate(band, inv_count, mine, theirs, own, other):
    return pl.pallas_call(
        rotate_kernel,
        out_shape=jax.ShapeDtypeStruct(own.shape, f32),
        in_specs=[smem, smem] + [vmem] * 4,
        out_specs=hbm,
        scratch_shapes=[
            pltpu.VMEM((2 * LANES, 2 * LANES), f32),
            pltpu.VMEM((PANEL, PANEL, LANES), f32),
            pltpu.VMEM((2, PANEL, LANES), f32),
            pltpu.VMEM((HALF, HALF, LANES), f32),
            pltpu.VMEM((HALF, HALF, LANES), f32),
            pltpu.VMEM(own.shape, f32),
            pltpu.SemaphoreType.DMA((8,)),
        ],
        compiler_params=grant(12),
    )(band, inv_count, mine, theirs, own, other)


def summed_over(value, axis):
    size = lax.axis_size(axis)
    if size & (size - 1):
        return lax.psum(value, axis)
    stride = 1
    while stride < size:
        count = min(4, size // stride)
        parts = [
            lax.ppermute(value, axis, [(i, i ^ (k * stride)) for i in range(size)])
            for k in range(1, count)
        ]
        value = value + sum(parts[1:], parts[0])
        stride *= count
    return value


def swapped(value):
    return lax.ppermute(value, "band", [(0, 1), (1, 0)])


def on_device(wavefunctions, bounds, cell_matrix, cell_scale, potential, cell_nodes, face_nodes):
    nodes = wavefunctions.shape[0]
    cell_matrix = pltpu.with_memory_space_constraint(cell_matrix, pltpu.HBM)
    cell_scale = pltpu.with_memory_space_constraint(cell_scale, pltpu.HBM)
    lists = pltpu.with_memory_space_constraint(face_nodes, pltpu.HBM)
    held = pltpu.with_memory_space_constraint(wavefunctions, pltpu.HBM)
    faces = jnp.where(face_nodes < 0, nodes, face_nodes).reshape(-1)
    potential = potential.reshape(-1, LANES)
    at = lax.axis_index("dom").astype(jnp.int32)
    band = lax.axis_index("band").astype(jnp.int32)
    kind = jnp.arange(4, dtype=jnp.int32) ^ (2 * band)
    flip = jnp.where(kind < 2, at % 2, at // 2 % 2)
    side = kind // 2 * 2 + ((kind % 2) ^ flip)
    pairs = exchange_pairs(lax.axis_size("dom"))

    def exchanged(blocks):
        return [
            lax.ppermute(
                block,
                ("dom", "band"),
                [(2 * i + b, 2 * j + b) for b in range(2) for i, j in pairs[q ^ (2 * b)]],
            )
            for q, block in enumerate(blocks)
        ]

    cells = functools.partial(apply_cells, side, cell_nodes.reshape(-1), cell_scale, cell_matrix)
    blocks, vectors = send_faces(side, lists, held)
    own, *sums = cells(vectors, exchanged(blocks))
    degree_one, *blocks = finish_first(
        side, faces, bounds, own, potential, vectors, exchanged(sums)
    )
    own, *sums = cells(degree_one, exchanged(blocks))
    degree_two = finish_second(
        side, faces, bounds, own, potential, degree_one, exchanged(sums), wavefunctions
    )
    other = swapped(degree_two)
    band = band.reshape(1)
    mine = summed_over(margin_rows(band, degree_two, other), "dom")
    inv_count = jnp.full((1,), 1.0 / (nodes * lax.axis_size("dom")), f32)
    return rotate(band, inv_count, mine, swapped(mine), degree_two, other)


def solution(mesh):
    return jax.shard_map(
        on_device,
        mesh=mesh,
        in_specs=(
            P(("kpt", "dom"), "band"),
            P("kpt"),
            P(),
            P("dom"),
            P("dom"),
            P("dom", None),
            P("dom", None),
        ),
        out_specs=P(("kpt", "dom"), "band"),
        check_vma=False,
    )
```

```python
import functools

import jax
import jax.numpy as jnp
from jax import lax
from jax.experimental import pallas as pl
from jax.experimental.pallas import tpu as pltpu
from jax.sharding import PartitionSpec as P

peer_offsets = (1, -1, 2, -2)
f32, bf16 = jnp.float32, jnp.bfloat16
LANES, GROUP, PANEL, HALF = 128, 8, 16, 8
vmem = pl.BlockSpec(memory_space=pltpu.VMEM)
smem = pl.BlockSpec(memory_space=pltpu.SMEM)
hbm = pl.BlockSpec(memory_space=pltpu.HBM)


def grant(mib):
    return pltpu.CompilerParams(vmem_limit_bytes=mib * 2**20)


def exchange_pairs(size):
    first = ([i for i in range(size) if i % 2 == 0], 1)
    second = ([i for i in range(size) if i % 2 == 1], 1)
    third = ([i for i in range(size) if i % 4 < 2], 2)
    fourth = ([i for i in range(size) if i % 4 >= 2], 2)
    return [
        [pair for i in starts if i + by < size for pair in ((i, i + by), (i + by, i))]
        for starts, by in (first, second, third, fourth)
    ]


def gather_faces(order_ref, faces_ref, table_ref, rows_ref, out_refs):
    slots = out_refs[0].shape[0]
    for q in range(4):
        offset = order_ref[q] * slots

        def body(step, _):
            base = step * 64
            for u in range(64):
                face = faces_ref[offset + base + u]
                rows_ref[pl.ds(base + u, 1), :] = table_ref[pl.ds(face, 1), :]
            return 0

        lax.fori_loop(0, slots // 64, body, 0)
        out_refs[q][...] = rows_ref[...].astype(bf16)


def face_kernel(
    order_ref, lists_ref, given_ref, o0, o1, o2, o3, vec_ref, faces_ref, table_ref, rows_ref, sems
):
    nodes, chunks = vec_ref.shape[0], sems.shape[0] - 1
    chunk = nodes // chunks
    names = pltpu.make_async_copy(lists_ref, faces_ref, sems.at[chunks])
    names.start()
    copies = []
    for c in range(chunks):
        rows = pl.ds(c * chunk, chunk)
        copies.append(pltpu.make_async_copy(given_ref.at[rows], vec_ref.at[rows], sems.at[c]))
        copies[-1].start()
    table_ref[0:8, :] = jnp.zeros((8, LANES), f32)
    for c, copy in enumerate(copies):
        copy.wait()
        rows = pl.ds(c * chunk, chunk)
        table_ref[pl.ds(8 + c * chunk, chunk), :] = vec_ref[rows, :].astype(f32)
    names.wait()
    for q, out_ref in enumerate((o0, o1, o2, o3)):
        face = order_ref[q]
        for slot in range(rows_ref.shape[0]):
            row = faces_ref[face, slot] + 8
            rows_ref[slot : slot + 1, :] = table_ref[pl.ds(row, 1), :]
        out_ref[...] = rows_ref[...].astype(bf16)


def send_faces(side, face_nodes, vectors):
    nodes, slots = vectors.shape[0], face_nodes.shape[1]
    *blocks, vectors = pl.pallas_call(
        face_kernel,
        out_shape=[jax.ShapeDtypeStruct((slots, LANES), bf16)] * 4
        + [jax.ShapeDtypeStruct((nodes, LANES), bf16)],
        in_specs=[smem, hbm, hbm],
        out_specs=[vmem] * 5,
        scratch_shapes=[
            pltpu.SMEM(face_nodes.shape, jnp.int32),
            pltpu.VMEM((nodes + 8, LANES), f32),
            pltpu.VMEM((slots, LANES), f32),
            pltpu.SemaphoreType.DMA((5,)),
        ],
        compiler_params=grant(8),
    )(side, face_nodes, vectors)
    return blocks, vectors


def cells_kernel(
    order_ref, names_ref, scales_ref, whole_ref, vec_ref, h0, h1, h2, h3,
    own_ref, g0, g1, g2, g3, maps_ref, scale_ref, matrix_ref, ext_ref, in_ref, out_ref, sems, *acc
):
    nodes, slots = vec_ref.shape[0], h0.shape[0]
    size = matrix_ref.shape[0]
    ext = nodes + 4 * slots
    fetch = pltpu.make_async_copy(whole_ref, matrix_ref, sems.at[0])
    cells = scale_ref.shape[0]
    scale = pltpu.make_async_copy(scales_ref, scale_ref, sems.at[1])
    names = []
    for batch in range(cells // GROUP):
        part = pl.ds(batch * GROUP * size, GROUP * size)
        names.append(
            pltpu.make_async_copy(names_ref.at[part], maps_ref.at[part], sems.at[2 + batch])
        )
        names[-1].start()
    scale.start()
    fetch.start()
    for q, ghost in enumerate((h0, h1, h2, h3)):
        start = pl.multiple_of(nodes + (order_ref[q] ^ 1) * slots, slots)
        ext_ref[pl.ds(start, slots), :] = ghost[...].astype(f32)
    share = ext // (size // 32)
    ext_ref[0:nodes, :] = vec_ref[...].astype(f32)
    for first in range(0, cells, GROUP):
        names[first // GROUP].wait()

        def gather(step, _):
            base = step * 32
            if first == 0:
                cleared = pl.ds(pl.multiple_of(step * share, 8), share)
                for a in acc:
                    a[cleared, :] = jnp.zeros((share, LANES), f32)
            for u in range(32):
                for k in range(GROUP):
                    row = maps_ref[(first + k) * size + base + u]
                    in_ref[k, pl.ds(base + u, 1), :] = ext_ref[pl.ds(row, 1), :]
            return 0

        lax.fori_loop(0, size // 32, gather, 0)
        if first == 0:
            fetch.wait()
            scale.wait()
        for k in range(0, GROUP, 2):
            pair = jnp.concatenate([in_ref[k].astype(bf16), in_ref[k + 1].astype(bf16)], 1)
            product = jnp.dot(matrix_ref[...], pair, preferred_element_type=f32)
            out_ref[k] = product[:, :LANES] * scale_ref[first + k]
            out_ref[k + 1] = product[:, LANES:] * scale_ref[first + k + 1]

        def scatter(step, _):
            base = step * 32
            for u in range(32):
                rows = [maps_ref[(first + k) * size + base + u] for k in range(GROUP)]
                sums = [
                    acc[k][pl.ds(rows[k], 1), :] + out_ref[k, pl.ds(base + u, 1), :]
                    for k in range(GROUP)
                ]
                for k in range(GROUP):
                    acc[k][pl.ds(rows[k], 1), :] = sums[k]
            return 0

        lax.fori_loop(0, size // 32, scatter, 0)

    def total(start):
        rows = pl.ds(start, 64)
        parts = [a[rows, :] for a in acc]
        while len(parts) > 1:
            parts = [parts[i] + parts[i + 1] for i in range(0, len(parts), 2)]
        return parts[0]

    def reduce_own(step, _):
        start = pl.multiple_of(step * 64, 64)
        own_ref[pl.ds(start, 64), :] = total(start)
        return 0

    lax.fori_loop(0, nodes // 64, reduce_own, 0)
    for q, ghost in enumerate((g0, g1, g2, g3)):
        start = pl.multiple_of(nodes + (order_ref[q] ^ 1) * slots, slots)
        for r in range(0, slots, 64):
            ghost[r : r + 64, :] = total(pl.multiple_of(start + r, 64))


def apply_cells(side, maps, scale, matrix, vectors, ghosts):
    nodes, slots, size = vectors.shape[0], ghosts[0].shape[0], matrix.shape[0]
    ext = nodes + 4 * slots
    return pl.pallas_call(
        cells_kernel,
        out_shape=[jax.ShapeDtypeStruct((nodes, LANES), f32)]
        + [jax.ShapeDtypeStruct((slots, LANES), f32)] * 4,
        in_specs=[smem, hbm, hbm, hbm] + [vmem] * 5,
        out_specs=[vmem] * 5,
        scratch_shapes=[
            pltpu.SMEM(maps.shape, jnp.int32),
            pltpu.SMEM(scale.shape, f32),
            pltpu.VMEM((size, size), bf16),
            pltpu.VMEM((ext, LANES), f32),
            pltpu.VMEM((GROUP, size, LANES), f32),
            pltpu.VMEM((GROUP, size, LANES), f32),
            pltpu.SemaphoreType.DMA((2 + scale.shape[0] // GROUP,)),
        ]
        + [pltpu.VMEM((ext, LANES), f32)] * GROUP,
        compiler_params=grant(36),
    )(side, maps, scale, matrix, vectors, *ghosts)


def add_returned(order_ref, faces_ref, pieces, count, acc):
    for a in acc:
        a[...] = jnp.zeros(a.shape, f32)
    lists = [order_ref[q] * block.shape[0] + first for q, first, block in pieces]

    def body(step, _):
        base = step * 16
        for u in range(16):
            rows = [faces_ref[start + base + u] for start in lists]
            sums = [
                a[pl.ds(row, 1), :] + block[pl.ds(first + base + u, 1), :]
                for a, row, (_, first, block) in zip(acc, rows, pieces)
            ]
            for a, row, value in zip(acc, rows, sums):
                a[pl.ds(row, 1), :] = value
        return 0

    lax.fori_loop(0, count // 16, body, 0)


def early_kernel(order_ref, faces_ref, own_ref, r0, out_ref, *acc):
    half = r0.shape[0] // 2
    add_returned(order_ref, faces_ref, [(0, 0, r0), (0, half, r0)], half, acc)

    def combine(step, _):
        rows = pl.ds(pl.multiple_of(step * 64, 64), 64)
        out_ref[rows, :] = own_ref[rows, :] + (acc[0][rows, :] + acc[1][rows, :])
        return 0

    lax.fori_loop(0, own_ref.shape[0] // 64, combine, 0)


def add_early(side, faces, own, returned):
    nodes = own.shape[0]
    return pl.pallas_call(
        early_kernel,
        out_shape=jax.ShapeDtypeStruct((nodes, LANES), f32),
        in_specs=[smem] * 2 + [vmem] * 2,
        out_specs=vmem,
        scratch_shapes=[pltpu.VMEM((nodes + 8, LANES), f32)] * 2,
        compiler_params=grant(12),
        cost_estimate=pl.CostEstimate(flops=10**6, bytes_accessed=4 * 10**6, transcendentals=0),
    )(side, faces, own, returned)


def filtered(interval_ref, own_ref, pot_ref, vec_ref, acc, write):
    low = jnp.full((1, LANES), interval_ref[0])
    high = jnp.full((1, LANES), interval_ref[1])
    center, half_width = (low + high) / 2.0, (high - low) / 2.0
    inverse = 1.0 / half_width
    shifts = ((pot_ref[...] - center) * inverse).T
    for step in range(shifts.shape[1]):
        rows = slice(step * LANES, (step + 1) * LANES)
        image = (own_ref[rows, :] + acc[0][rows, :]) + (acc[1][rows, :] + acc[2][rows, :])
        shift = jnp.broadcast_to(shifts[:, step : step + 1], (LANES, LANES))
        write(rows, image * inverse + shift * vec_ref[rows, :].astype(f32))


def first_kernel(
    order_ref, faces_ref, interval_ref, own_ref, pot_ref, vec_ref, r1, r2, r3,
    out_ref, o0, o1, o2, o3, table_ref, rows_ref, *acc
):
    nodes = vec_ref.shape[0]
    late = [(1, 0, r1), (2, 0, r2), (3, 0, r3)]
    add_returned(order_ref, faces_ref, late, r1.shape[0], acc)

    def write(rows, value):
        value = value.astype(bf16)
        out_ref[rows, :] = value
        table_ref[rows, :] = value.astype(f32)

    filtered(interval_ref, own_ref, pot_ref, vec_ref, acc, write)
    table_ref[nodes : nodes + 8, :] = jnp.zeros((8, LANES), f32)

    gather_faces(order_ref, faces_ref, table_ref, rows_ref, (o0, o1, o2, o3))


def second_kernel(
    order_ref, faces_ref, interval_ref, own_ref, pot_ref, vec_ref, r1, r2, r3, old_ref,
    out_ref, *acc
):
    late = [(1, 0, r1), (2, 0, r2), (3, 0, r3)]
    add_returned(order_ref, faces_ref, late, r1.shape[0], acc)

    def write(rows, value):
        out_ref[rows, :] = (2.0 * value - old_ref[rows, :].astype(f32)).astype(bf16)

    filtered(interval_ref, own_ref, pot_ref, vec_ref, acc, write)


def finish_first(side, faces, interval, own, potential, vectors, returned):
    nodes, slots = vectors.shape[0], returned[0].shape[0]
    own = add_early(side, faces, own, returned[0])
    return pl.pallas_call(
        first_kernel,
        out_shape=[jax.ShapeDtypeStruct((nodes, LANES), bf16)]
        + [jax.ShapeDtypeStruct((slots, LANES), bf16)] * 4,
        in_specs=[smem] * 3 + [vmem] * 6,
        out_specs=[vmem] * 5,
        scratch_shapes=[
            pltpu.VMEM((nodes + 8, LANES), f32),
            pltpu.VMEM((slots, LANES), f32),
        ]
        + [pltpu.VMEM((nodes + 8, LANES), f32)] * 3,
        compiler_params=grant(20),
    )(side, faces, interval, own, potential, vectors, *returned[1:])


def finish_second(side, faces, interval, own, potential, vectors, returned, old):
    nodes = vectors.shape[0]
    own = add_early(side, faces, own, returned[0])
    return pl.pallas_call(
        second_kernel,
        out_shape=jax.ShapeDtypeStruct((nodes, LANES), bf16),
        in_specs=[smem] * 3 + [vmem] * 7,
        out_specs=vmem,
        scratch_shapes=[pltpu.VMEM((nodes + 8, LANES), f32)] * 3,
        compiler_params=grant(20),
    )(side, faces, interval, own, potential, vectors, *returned[1:], old)


def margin_kernel(band_ref, own_ref, other_ref, out_ref):
    half = LANES // 2
    nt = functools.partial(
        lax.dot_general,
        dimension_numbers=(((0,), (0,)), ((), ())),
        preferred_element_type=f32,
    )

    def write(low, high, band):
        low_rows = low[:, band * half : (band + 1) * half]
        high_rows = high[:, band * half : (band + 1) * half]
        block = nt(low_rows, low)
        cross = nt(low_rows, high)
        tail = nt(high_rows, high)
        row = lax.broadcasted_iota(jnp.int32, (half, LANES), 0) + band * half
        col = lax.broadcasted_iota(jnp.int32, (half, LANES), 1)
        out_ref[0:half, :] = jnp.where(col >= row, block, tail)
        out_ref[half : 2 * half, :] = cross
        diag = jnp.sum(jnp.where(col == row, tail, 0.0), 0, keepdims=True)
        out_ref[2 * half : 2 * half + 8, :] = jnp.broadcast_to(diag, (8, LANES))

    @pl.when(band_ref[0] == 0)
    def _():
        write(own_ref[...], other_ref[...], 0)

    @pl.when(band_ref[0] != 0)
    def _():
        write(other_ref[...], own_ref[...], 1)


def margin_rows(band, own, other):
    return pl.pallas_call(
        margin_kernel,
        out_shape=jax.ShapeDtypeStruct((LANES + 8, LANES), f32),
        in_specs=[smem, vmem, vmem],
        out_specs=vmem,
        compiler_params=grant(12),
    )(band, own, other)


def split_three(x):
    high = x.astype(bf16)
    rest = x - high.astype(f32)
    mid = rest.astype(bf16)
    return high, mid, (rest - mid.astype(f32)).astype(bf16)


def invert_factor(work_ref, block_ref, panel_ref, lower_ref, second_ref):
    total = work_ref.shape[0]
    halves = total // LANES
    col = lax.broadcasted_iota(jnp.int32, (PANEL, total), 1)
    row = lax.broadcasted_iota(jnp.int32, (PANEL, total), 0)

    def step(p, start_row):
        first = pl.multiple_of(p * PANEL, PANEL)
        rows = work_ref[pl.ds(first, PANEL), :]
        block = rows[:, start_row : start_row + LANES]
        block = pltpu.roll(block, lax.rem(total - first, LANES), 1)
        for k in range(PANEL):
            block_ref[k, 0:PANEL, :] = jnp.broadcast_to(block[:, k : k + 1], (PANEL, LANES))
        panel = jnp.where((col >= first) & (col < first + PANEL), 0.0, rows)
        panel = jnp.where(col == row + first, 1.0, panel)
        for h in range(halves):
            panel_ref[h, 0:PANEL, :] = panel[:, h * LANES : (h + 1) * LANES]

        def repeated(ref, k, i):
            return ref[k, pl.ds(i, HALF, stride=0), :]

        def factor(entry, below):
            scales = []
            for k in range(HALF):
                scale = lax.rsqrt(entry[k, k])
                scales.append(scale)
                for i in range(k + 1, HALF):
                    entry[i, k] = entry[i, k] * scale
                for i in range(k + 1, HALF):
                    for m in range(k + 1, i + 1):
                        entry[i, m] = entry[i, m] - entry[i, k] * entry[m, k]
                if below:
                    below[k] = below[k] * scale
                    for m in range(k + 1, HALF):
                        below[m] = below[m] - below[k] * entry[m, k]
            return scales

        def corner(ref):
            return {(i, k): repeated(ref, k, i) for k in range(HALF) for i in range(k, HALF)}

        done = []

        def write_lines(k, weights, scale):
            lines = [panel_ref[h, pl.ds(k, HALF, stride=0), :] for h in range(halves)]
            for m, weight in enumerate(weights):
                lines = [line - weight * old for line, old in zip(lines, done[m])]
            lines = [line * scale for line in lines]
            done.append(lines)
            at = k % HALF
            for h in range(halves):
                panel_ref[h, k : k + 1, :] = lines[h][at : at + 1, :]

        entry = corner(block_ref)
        below = [block_ref[k, HALF:PANEL, :] for k in range(HALF)]
        scales = factor(entry, below)
        for k in range(HALF):
            write_lines(k, [entry[k, m] for m in range(k)], scales[k])
            lower_ref[k, 0:HALF, :] = below[k]
        cross = {(m, k): repeated(lower_ref, k, m) for k in range(HALF) for m in range(HALF)}
        for m in range(HALF):
            column = block_ref[HALF + m, HALF:PANEL, :]
            for k in range(HALF):
                column = column - below[k] * cross[m, k]
            second_ref[m, 0:HALF, :] = column
        entry = corner(second_ref)
        scales = factor(entry, None)
        for k in range(HALF):
            weights = [cross[k, m] for m in range(HALF)] + [entry[k, m] for m in range(k)]
            write_lines(HALF + k, weights, scales[k])
        panel = jnp.concatenate([panel_ref[h, 0:PANEL, :] for h in range(halves)], 1)
        right = jnp.where(col >= first + PANEL, panel, 0.0)
        ah, am, al = split_three(right)
        bh, bm, bl = split_three(panel)
        lhs = jnp.concatenate([ah, ah, am, am, ah, al], 0)
        rhs = jnp.concatenate([bh, bm, bh, bm, bl, bh], 0)
        update = lax.dot_general(
            lhs[:, start_row:], rhs, (((0,), (0,)), ((), ())), preferred_element_type=f32
        )
        below = work_ref[start_row:, :]
        big = lax.broadcasted_iota(jnp.int32, below.shape, 1)
        inside = (big >= first) & (big < first + PANEL)
        work_ref[start_row:, :] = jnp.where(inside, 0.0, below) - update
        work_ref[pl.ds(first, PANEL), :] = panel

    per = LANES // PANEL
    for h in range(halves):
        lax.fori_loop(h * per, (h + 1) * per, lambda p, _: (step(p, h * LANES), 0)[1], 0)


def rotate_kernel(
    band_ref, count_ref, mine_ref, theirs_ref, own_ref, other_ref, out_ref, work_ref,
    block_ref, panel_ref, lower_ref, second_ref, result_ref, sems
):
    half = LANES // 2
    band = band_ref[0]
    mine, theirs = mine_ref[...] * count_ref[0], theirs_ref[...] * count_ref[0]
    top = jnp.where(band == 0, mine, theirs)
    bottom = jnp.where(band == 0, theirs, mine)
    packed = jnp.concatenate([top[0:half], bottom[0:half]], 0)
    cross = jnp.concatenate([top[half:LANES], bottom[half:LANES]], 0)
    diag = top[LANES : LANES + 1] + bottom[LANES : LANES + 1]
    flipped = packed.T
    row = lax.broadcasted_iota(jnp.int32, (LANES, LANES), 0)
    col = lax.broadcasted_iota(jnp.int32, (LANES, LANES), 1)
    work_ref[0:LANES, 0:LANES] = jnp.where(col >= row, packed, flipped)
    work_ref[0:LANES, LANES:] = cross
    work_ref[LANES:, 0:LANES] = cross.T
    tail = jnp.where(col < row, packed, flipped)
    work_ref[LANES:, LANES:] = jnp.where(col == row, jnp.broadcast_to(diag, tail.shape), tail)
    invert_factor(work_ref, block_ref, panel_ref, lower_ref, second_ref)
    lower = jnp.where(col <= row, 1.0, 0.0)
    first = work_ref[0:LANES, 0:LANES] * lower
    last = work_ref[LANES:, LANES:] * lower
    corner = work_ref[LANES:, 0:LANES]
    from_own = jnp.where(band == 0, first, last)
    from_other = jnp.where(band == 0, jnp.zeros_like(corner), corner)
    weights = jnp.concatenate([from_own, from_other], 1)
    high = weights.astype(bf16)
    low = (weights - high.astype(f32)).astype(bf16)
    weights = jnp.concatenate([high, low], 0)
    chunk = own_ref.shape[0] // sems.shape[0]
    copies = []
    for c in range(sems.shape[0]):
        rows = pl.ds(c * chunk, chunk)
        both = jnp.concatenate([own_ref[rows, :], other_ref[rows, :]], 1)
        product = lax.dot_general(
            both, weights, (((1,), (1,)), ((), ())), preferred_element_type=f32
        )
        result_ref[rows, :] = product[:, :LANES] + product[:, LANES:]
        copies.append(pltpu.make_async_copy(result_ref.at[rows], out_ref.at[rows], sems.at[c]))
        copies[-1].start()
    for copy in copies:
        copy.wait()


def rotate(band, inv_count, mine, theirs, own, other):
    return pl.pallas_call(
        rotate_kernel,
        out_shape=jax.ShapeDtypeStruct(own.shape, f32),
        in_specs=[smem, smem] + [vmem] * 4,
        out_specs=hbm,
        scratch_shapes=[
            pltpu.VMEM((2 * LANES, 2 * LANES), f32),
            pltpu.VMEM((PANEL, PANEL + HALF, LANES), f32),
            pltpu.VMEM((2, PANEL + HALF, LANES), f32),
            pltpu.VMEM((HALF, 2 * HALF, LANES), f32),
            pltpu.VMEM((HALF, 2 * HALF, LANES), f32),
            pltpu.VMEM(own.shape, f32),
            pltpu.SemaphoreType.DMA((8,)),
        ],
        compiler_params=grant(12),
    )(band, inv_count, mine, theirs, own, other)


def summed_over(value, axis):
    size = lax.axis_size(axis)
    if size & (size - 1):
        return lax.psum(value, axis)
    stride = 1
    while stride < size:
        count = min(4, size // stride)
        parts = [
            lax.ppermute(value, axis, [(i, i ^ (k * stride)) for i in range(size)])
            for k in range(1, count)
        ]
        value = value + sum(parts[1:], parts[0])
        stride *= count
    return value


def swapped(value):
    return lax.ppermute(value, "band", [(0, 1), (1, 0)])


def on_device(wavefunctions, bounds, cell_matrix, cell_scale, potential, cell_nodes, face_nodes):
    nodes = wavefunctions.shape[0]
    cell_matrix = pltpu.with_memory_space_constraint(cell_matrix, pltpu.HBM)
    cell_scale = pltpu.with_memory_space_constraint(cell_scale, pltpu.HBM)
    lists = pltpu.with_memory_space_constraint(face_nodes, pltpu.HBM)
    held = pltpu.with_memory_space_constraint(wavefunctions, pltpu.HBM)
    faces = jnp.where(face_nodes < 0, nodes, face_nodes).reshape(-1)
    potential = potential.reshape(-1, LANES)
    at = lax.axis_index("dom").astype(jnp.int32)
    band = lax.axis_index("band").astype(jnp.int32)
    kind = jnp.arange(4, dtype=jnp.int32) ^ (2 * band)
    flip = jnp.where(kind < 2, at % 2, at // 2 % 2)
    side = kind // 2 * 2 + ((kind % 2) ^ flip)
    pairs = exchange_pairs(lax.axis_size("dom"))

    def exchanged(blocks):
        return [
            lax.ppermute(
                block,
                ("dom", "band"),
                [(2 * i + b, 2 * j + b) for b in range(2) for i, j in pairs[q ^ (2 * b)]],
            )
            for q, block in enumerate(blocks)
        ]

    cells = functools.partial(apply_cells, side, cell_nodes.reshape(-1), cell_scale, cell_matrix)
    blocks, vectors = send_faces(side, lists, held)
    own, *sums = cells(vectors, exchanged(blocks))
    degree_one, *blocks = finish_first(
        side, faces, bounds, own, potential, vectors, exchanged(sums)
    )
    own, *sums = cells(degree_one, exchanged(blocks))
    degree_two = finish_second(
        side, faces, bounds, own, potential, degree_one, exchanged(sums), wavefunctions
    )
    other = swapped(degree_two)
    band = band.reshape(1)
    mine = summed_over(margin_rows(band, degree_two, other), "dom")
    inv_count = jnp.full((1,), 1.0 / (nodes * lax.axis_size("dom")), f32)
    return rotate(band, inv_count, mine, swapped(mine), degree_two, other)


def solution(mesh):
    return jax.shard_map(
        on_device,
        mesh=mesh,
        in_specs=(
            P(("kpt", "dom"), "band"),
            P("kpt"),
            P(),
            P("dom"),
            P("dom"),
            P("dom", None),
            P("dom", None),
        ),
        out_specs=P(("kpt", "dom"), "band"),
        check_vma=False,
    )
```

```python
import functools

import jax
import jax.numpy as jnp
from jax import lax
from jax.experimental import pallas as pl
from jax.experimental.pallas import tpu as pltpu
from jax.sharding import PartitionSpec as P

peer_offsets = (1, -1, 2, -2)
f32, bf16 = jnp.float32, jnp.bfloat16
LANES, GROUP, PANEL, HALF = 128, 8, 16, 8
vmem = pl.BlockSpec(memory_space=pltpu.VMEM)
smem = pl.BlockSpec(memory_space=pltpu.SMEM)
hbm = pl.BlockSpec(memory_space=pltpu.HBM)


def grant(mib):
    return pltpu.CompilerParams(vmem_limit_bytes=mib * 2**20)


def exchange_pairs(size):
    first = ([i for i in range(size) if i % 2 == 0], 1)
    second = ([i for i in range(size) if i % 2 == 1], 1)
    third = ([i for i in range(size) if i % 4 < 2], 2)
    fourth = ([i for i in range(size) if i % 4 >= 2], 2)
    return [
        [pair for i in starts if i + by < size for pair in ((i, i + by), (i + by, i))]
        for starts, by in (first, second, third, fourth)
    ]


def gather_faces(order_ref, faces_ref, table_ref, rows_ref, out_refs):
    slots = out_refs[0].shape[0]
    for q in range(4):
        offset = order_ref[q] * slots

        def body(step, _):
            base = step * 64
            for u in range(64):
                face = faces_ref[offset + base + u]
                rows_ref[pl.ds(base + u, 1), :] = table_ref[pl.ds(face, 1), :]
            return 0

        lax.fori_loop(0, slots // 64, body, 0)
        out_refs[q][...] = rows_ref[...].astype(bf16)


def face_kernel(
    order_ref, lists_ref, given_ref, o0, o1, o2, o3, vec_ref, faces_ref, table_ref, rows_ref, sems
):
    nodes, chunks = vec_ref.shape[0], sems.shape[0] - 1
    chunk = nodes // chunks
    names = pltpu.make_async_copy(lists_ref, faces_ref, sems.at[chunks])
    names.start()
    copies = []
    for c in range(chunks):
        rows = pl.ds(c * chunk, chunk)
        copies.append(pltpu.make_async_copy(given_ref.at[rows], vec_ref.at[rows], sems.at[c]))
        copies[-1].start()
    table_ref[0:8, :] = jnp.zeros((8, LANES), f32)
    for c, copy in enumerate(copies):
        copy.wait()
        rows = pl.ds(c * chunk, chunk)
        table_ref[pl.ds(8 + c * chunk, chunk), :] = vec_ref[rows, :].astype(f32)
    names.wait()
    for q, out_ref in enumerate((o0, o1, o2, o3)):
        face = order_ref[q]
        for slot in range(rows_ref.shape[0]):
            row = faces_ref[face, slot] + 8
            rows_ref[slot : slot + 1, :] = table_ref[pl.ds(row, 1), :]
        out_ref[...] = rows_ref[...].astype(bf16)


def send_faces(side, face_nodes, vectors):
    nodes, slots = vectors.shape[0], face_nodes.shape[1]
    *blocks, vectors = pl.pallas_call(
        face_kernel,
        out_shape=[jax.ShapeDtypeStruct((slots, LANES), bf16)] * 4
        + [jax.ShapeDtypeStruct((nodes, LANES), bf16)],
        in_specs=[smem, hbm, hbm],
        out_specs=[vmem] * 5,
        scratch_shapes=[
            pltpu.SMEM(face_nodes.shape, jnp.int32),
            pltpu.VMEM((nodes + 8, LANES), f32),
            pltpu.VMEM((slots, LANES), f32),
            pltpu.SemaphoreType.DMA((9,)),
        ],
        compiler_params=grant(8),
    )(side, face_nodes, vectors)
    return blocks, vectors


def cells_kernel(
    order_ref, names_ref, scales_ref, whole_ref, vec_ref, h0, h1, h2, h3,
    own_ref, g0, g1, g2, g3, maps_ref, scale_ref, matrix_ref, ext_ref, in_ref, out_ref, sems, *acc
):
    nodes, slots = vec_ref.shape[0], h0.shape[0]
    size = matrix_ref.shape[0]
    ext = nodes + 4 * slots
    fetch = pltpu.make_async_copy(whole_ref, matrix_ref, sems.at[0])
    cells = scale_ref.shape[0]
    scale = pltpu.make_async_copy(scales_ref, scale_ref, sems.at[1])
    names = []
    for batch in range(cells // GROUP):
        part = pl.ds(batch * GROUP * size, GROUP * size)
        names.append(
            pltpu.make_async_copy(names_ref.at[part], maps_ref.at[part], sems.at[2 + batch])
        )
        names[-1].start()
    scale.start()
    fetch.start()
    for q, ghost in enumerate((h0, h1, h2, h3)):
        start = pl.multiple_of(nodes + (order_ref[q] ^ 1) * slots, slots)
        ext_ref[pl.ds(start, slots), :] = ghost[...].astype(f32)
    share = ext // (size // 32)
    ext_ref[0:nodes, :] = vec_ref[...].astype(f32)
    for first in range(0, cells, GROUP):
        names[first // GROUP].wait()

        def gather(step, _):
            base = step * 32
            if first == 0:
                cleared = pl.ds(pl.multiple_of(step * share, 8), share)
                for a in acc:
                    a[cleared, :] = jnp.zeros((share, LANES), f32)
            for u in range(32):
                for k in range(GROUP):
                    row = maps_ref[(first + k) * size + base + u]
                    in_ref[k, pl.ds(base + u, 1), :] = ext_ref[pl.ds(row, 1), :]
            return 0

        lax.fori_loop(0, size // 32, gather, 0)
        if first == 0:
            fetch.wait()
            scale.wait()
        for k in range(0, GROUP, 2):
            pair = jnp.concatenate([in_ref[k].astype(bf16), in_ref[k + 1].astype(bf16)], 1)
            product = jnp.dot(matrix_ref[...], pair, preferred_element_type=f32)
            out_ref[k] = product[:, :LANES] * scale_ref[first + k]
            out_ref[k + 1] = product[:, LANES:] * scale_ref[first + k + 1]

        def scatter(step, _):
            base = step * 32
            for u in range(32):
                rows = [maps_ref[(first + k) * size + base + u] for k in range(GROUP)]
                sums = [
                    acc[k][pl.ds(rows[k], 1), :] + out_ref[k, pl.ds(base + u, 1), :]
                    for k in range(GROUP)
                ]
                for k in range(GROUP):
                    acc[k][pl.ds(rows[k], 1), :] = sums[k]
            return 0

        lax.fori_loop(0, size // 32, scatter, 0)

    def total(start):
        rows = pl.ds(start, 64)
        parts = [a[rows, :] for a in acc]
        while len(parts) > 1:
            parts = [parts[i] + parts[i + 1] for i in range(0, len(parts), 2)]
        return parts[0]

    def reduce_own(step, _):
        start = pl.multiple_of(step * 64, 64)
        own_ref[pl.ds(start, 64), :] = total(start)
        return 0

    lax.fori_loop(0, nodes // 64, reduce_own, 0)
    for q, ghost in enumerate((g0, g1, g2, g3)):
        start = pl.multiple_of(nodes + (order_ref[q] ^ 1) * slots, slots)
        for r in range(0, slots, 64):
            ghost[r : r + 64, :] = total(pl.multiple_of(start + r, 64))


def apply_cells(side, maps, scale, matrix, vectors, ghosts):
    nodes, slots, size = vectors.shape[0], ghosts[0].shape[0], matrix.shape[0]
    ext = nodes + 4 * slots
    return pl.pallas_call(
        cells_kernel,
        out_shape=[jax.ShapeDtypeStruct((nodes, LANES), f32)]
        + [jax.ShapeDtypeStruct((slots, LANES), f32)] * 4,
        in_specs=[smem, hbm, hbm, hbm] + [vmem] * 5,
        out_specs=[vmem] * 5,
        scratch_shapes=[
            pltpu.SMEM(maps.shape, jnp.int32),
            pltpu.SMEM(scale.shape, f32),
            pltpu.VMEM((size, size), bf16),
            pltpu.VMEM((ext, LANES), f32),
            pltpu.VMEM((GROUP, size, LANES), f32),
            pltpu.VMEM((GROUP, size, LANES), f32),
            pltpu.SemaphoreType.DMA((2 + scale.shape[0] // GROUP,)),
        ]
        + [pltpu.VMEM((ext, LANES), f32)] * GROUP,
        compiler_params=grant(36),
    )(side, maps, scale, matrix, vectors, *ghosts)


def add_returned(order_ref, faces_ref, pieces, count, acc):
    for a in acc:
        a[...] = jnp.zeros(a.shape, f32)
    lists = [order_ref[q] * block.shape[0] + first for q, first, block in pieces]

    def body(step, _):
        base = step * 16
        for u in range(16):
            rows = [faces_ref[start + base + u] for start in lists]
            sums = [
                a[pl.ds(row, 1), :] + block[pl.ds(first + base + u, 1), :]
                for a, row, (_, first, block) in zip(acc, rows, pieces)
            ]
            for a, row, value in zip(acc, rows, sums):
                a[pl.ds(row, 1), :] = value
        return 0

    lax.fori_loop(0, count // 16, body, 0)


def early_kernel(order_ref, faces_ref, own_ref, r0, out_ref, *acc):
    half = r0.shape[0] // 2
    add_returned(order_ref, faces_ref, [(0, 0, r0), (0, half, r0)], half, acc)

    def combine(step, _):
        rows = pl.ds(pl.multiple_of(step * 64, 64), 64)
        out_ref[rows, :] = own_ref[rows, :] + (acc[0][rows, :] + acc[1][rows, :])
        return 0

    lax.fori_loop(0, own_ref.shape[0] // 64, combine, 0)


def add_early(side, faces, own, returned):
    nodes = own.shape[0]
    return pl.pallas_call(
        early_kernel,
        out_shape=jax.ShapeDtypeStruct((nodes, LANES), f32),
        in_specs=[smem] * 2 + [vmem] * 2,
        out_specs=vmem,
        scratch_shapes=[pltpu.VMEM((nodes + 8, LANES), f32)] * 2,
        compiler_params=grant(12),
        cost_estimate=pl.CostEstimate(flops=10**6, bytes_accessed=4 * 10**6, transcendentals=0),
    )(side, faces, own, returned)


def filtered(interval_ref, own_ref, pot_ref, vec_ref, acc, write):
    low = jnp.full((1, LANES), interval_ref[0])
    high = jnp.full((1, LANES), interval_ref[1])
    center, half_width = (low + high) / 2.0, (high - low) / 2.0
    inverse = 1.0 / half_width
    shifts = ((pot_ref[...] - center) * inverse).T
    for step in range(shifts.shape[1]):
        rows = slice(step * LANES, (step + 1) * LANES)
        image = (own_ref[rows, :] + acc[0][rows, :]) + (acc[1][rows, :] + acc[2][rows, :])
        shift = jnp.broadcast_to(shifts[:, step : step + 1], (LANES, LANES))
        write(rows, image * inverse + shift * vec_ref[rows, :].astype(f32))


def first_kernel(
    order_ref, faces_ref, interval_ref, own_ref, pot_ref, vec_ref, r1, r2, r3,
    out_ref, o0, o1, o2, o3, table_ref, rows_ref, *acc
):
    nodes = vec_ref.shape[0]
    late = [(1, 0, r1), (2, 0, r2), (3, 0, r3)]
    add_returned(order_ref, faces_ref, late, r1.shape[0], acc)

    def write(rows, value):
        value = value.astype(bf16)
        out_ref[rows, :] = value
        table_ref[rows, :] = value.astype(f32)

    filtered(interval_ref, own_ref, pot_ref, vec_ref, acc, write)
    table_ref[nodes : nodes + 8, :] = jnp.zeros((8, LANES), f32)

    gather_faces(order_ref, faces_ref, table_ref, rows_ref, (o0, o1, o2, o3))


def second_kernel(
    order_ref, faces_ref, interval_ref, own_ref, pot_ref, vec_ref, r1, r2, r3, old_ref,
    out_ref, *acc
):
    late = [(1, 0, r1), (2, 0, r2), (3, 0, r3)]
    add_returned(order_ref, faces_ref, late, r1.shape[0], acc)

    def write(rows, value):
        out_ref[rows, :] = (2.0 * value - old_ref[rows, :].astype(f32)).astype(bf16)

    filtered(interval_ref, own_ref, pot_ref, vec_ref, acc, write)


def finish_first(side, faces, interval, own, potential, vectors, returned):
    nodes, slots = vectors.shape[0], returned[0].shape[0]
    own = add_early(side, faces, own, returned[0])
    return pl.pallas_call(
        first_kernel,
        out_shape=[jax.ShapeDtypeStruct((nodes, LANES), bf16)]
        + [jax.ShapeDtypeStruct((slots, LANES), bf16)] * 4,
        in_specs=[smem] * 3 + [vmem] * 6,
        out_specs=[vmem] * 5,
        scratch_shapes=[
            pltpu.VMEM((nodes + 8, LANES), f32),
            pltpu.VMEM((slots, LANES), f32),
        ]
        + [pltpu.VMEM((nodes + 8, LANES), f32)] * 3,
        compiler_params=grant(20),
    )(side, faces, interval, own, potential, vectors, *returned[1:])


def finish_second(side, faces, interval, own, potential, vectors, returned, old):
    nodes = vectors.shape[0]
    own = add_early(side, faces, own, returned[0])
    return pl.pallas_call(
        second_kernel,
        out_shape=jax.ShapeDtypeStruct((nodes, LANES), bf16),
        in_specs=[smem] * 3 + [vmem] * 7,
        out_specs=vmem,
        scratch_shapes=[pltpu.VMEM((nodes + 8, LANES), f32)] * 3,
        compiler_params=grant(20),
    )(side, faces, interval, own, potential, vectors, *returned[1:], old)


def margin_kernel(band_ref, own_ref, other_ref, out_ref):
    half = LANES // 2
    nt = functools.partial(
        lax.dot_general,
        dimension_numbers=(((0,), (0,)), ((), ())),
        preferred_element_type=f32,
    )

    def write(low, high, band):
        low_rows = low[:, band * half : (band + 1) * half]
        high_rows = high[:, band * half : (band + 1) * half]
        block = nt(low_rows, low)
        cross = nt(low_rows, high)
        tail = nt(high_rows, high)
        row = lax.broadcasted_iota(jnp.int32, (half, LANES), 0) + band * half
        col = lax.broadcasted_iota(jnp.int32, (half, LANES), 1)
        out_ref[0:half, :] = jnp.where(col >= row, block, tail)
        out_ref[half : 2 * half, :] = cross
        diag = jnp.sum(jnp.where(col == row, tail, 0.0), 0, keepdims=True)
        out_ref[2 * half : 2 * half + 8, :] = jnp.broadcast_to(diag, (8, LANES))

    @pl.when(band_ref[0] == 0)
    def _():
        write(own_ref[...], other_ref[...], 0)

    @pl.when(band_ref[0] != 0)
    def _():
        write(other_ref[...], own_ref[...], 1)


def margin_rows(band, own, other):
    return pl.pallas_call(
        margin_kernel,
        out_shape=jax.ShapeDtypeStruct((LANES + 8, LANES), f32),
        in_specs=[smem, vmem, vmem],
        out_specs=vmem,
        compiler_params=grant(12),
    )(band, own, other)


def split_three(x):
    high = x.astype(bf16)
    rest = x - high.astype(f32)
    mid = rest.astype(bf16)
    return high, mid, (rest - mid.astype(f32)).astype(bf16)


def invert_factor(work_ref, block_ref, panel_ref, lower_ref, second_ref):
    total = work_ref.shape[0]
    halves = total // LANES
    col = lax.broadcasted_iota(jnp.int32, (PANEL, total), 1)
    row = lax.broadcasted_iota(jnp.int32, (PANEL, total), 0)

    def step(p, start_row):
        first = pl.multiple_of(p * PANEL, PANEL)
        rows = work_ref[pl.ds(first, PANEL), :]
        block = rows[:, start_row : start_row + LANES]
        block = pltpu.roll(block, lax.rem(total - first, LANES), 1)
        for k in range(PANEL):
            block_ref[k, 0:PANEL, :] = jnp.broadcast_to(block[:, k : k + 1], (PANEL, LANES))
        panel = jnp.where((col >= first) & (col < first + PANEL), 0.0, rows)
        panel = jnp.where(col == row + first, 1.0, panel)
        for h in range(halves):
            panel_ref[h, 0:PANEL, :] = panel[:, h * LANES : (h + 1) * LANES]

        def repeated(ref, k, i):
            return ref[k, pl.ds(i, HALF, stride=0), :]

        def factor(entry, below):
            scales = []
            for k in range(HALF):
                scale = lax.rsqrt(entry[k, k])
                scales.append(scale)
                for i in range(k + 1, HALF):
                    entry[i, k] = entry[i, k] * scale
                for i in range(k + 1, HALF):
                    for m in range(k + 1, i + 1):
                        entry[i, m] = entry[i, m] - entry[i, k] * entry[m, k]
                if below:
                    below[k] = below[k] * scale
                    for m in range(k + 1, HALF):
                        below[m] = below[m] - below[k] * entry[m, k]
            return scales

        def corner(ref):
            return {(i, k): repeated(ref, k, i) for k in range(HALF) for i in range(k, HALF)}

        done = []

        def write_lines(k, weights, scale):
            lines = [panel_ref[h, pl.ds(k, HALF, stride=0), :] for h in range(halves)]
            for m, weight in enumerate(weights):
                lines = [line - weight * old for line, old in zip(lines, done[m])]
            lines = [line * scale for line in lines]
            done.append(lines)
            at = k % HALF
            for h in range(halves):
                panel_ref[h, k : k + 1, :] = lines[h][at : at + 1, :]

        entry = corner(block_ref)
        below = [block_ref[k, HALF:PANEL, :] for k in range(HALF)]
        scales = factor(entry, below)
        for k in range(HALF):
            write_lines(k, [entry[k, m] for m in range(k)], scales[k])
            lower_ref[k, 0:HALF, :] = below[k]
        cross = {(m, k): repeated(lower_ref, k, m) for k in range(HALF) for m in range(HALF)}
        for m in range(HALF):
            column = block_ref[HALF + m, HALF:PANEL, :]
            for k in range(HALF):
                column = column - below[k] * cross[m, k]
            second_ref[m, 0:HALF, :] = column
        entry = corner(second_ref)
        scales = factor(entry, None)
        for k in range(HALF):
            weights = [cross[k, m] for m in range(HALF)] + [entry[k, m] for m in range(k)]
            write_lines(HALF + k, weights, scales[k])
        panel = jnp.concatenate([panel_ref[h, 0:PANEL, :] for h in range(halves)], 1)
        right = jnp.where(col >= first + PANEL, panel, 0.0)
        ah, am, al = split_three(right)
        bh, bm, bl = split_three(panel)
        lhs = jnp.concatenate([ah, ah, am, am, ah, al], 0)
        rhs = jnp.concatenate([bh, bm, bh, bm, bl, bh], 0)
        update = lax.dot_general(
            lhs[:, start_row:], rhs, (((0,), (0,)), ((), ())), preferred_element_type=f32
        )
        below = work_ref[start_row:, :]
        big = lax.broadcasted_iota(jnp.int32, below.shape, 1)
        inside = (big >= first) & (big < first + PANEL)
        work_ref[start_row:, :] = jnp.where(inside, 0.0, below) - update
        work_ref[pl.ds(first, PANEL), :] = panel

    per = LANES // PANEL
    for h in range(halves):
        lax.fori_loop(h * per, (h + 1) * per, lambda p, _: (step(p, h * LANES), 0)[1], 0)


def rotate_kernel(
    band_ref, count_ref, mine_ref, theirs_ref, own_ref, other_ref, out_ref, work_ref,
    block_ref, panel_ref, lower_ref, second_ref, result_ref, sems
):
    half = LANES // 2
    band = band_ref[0]
    mine, theirs = mine_ref[...] * count_ref[0], theirs_ref[...] * count_ref[0]
    top = jnp.where(band == 0, mine, theirs)
    bottom = jnp.where(band == 0, theirs, mine)
    packed = jnp.concatenate([top[0:half], bottom[0:half]], 0)
    cross = jnp.concatenate([top[half:LANES], bottom[half:LANES]], 0)
    diag = top[LANES : LANES + 1] + bottom[LANES : LANES + 1]
    flipped = packed.T
    row = lax.broadcasted_iota(jnp.int32, (LANES, LANES), 0)
    col = lax.broadcasted_iota(jnp.int32, (LANES, LANES), 1)
    work_ref[0:LANES, 0:LANES] = jnp.where(col >= row, packed, flipped)
    work_ref[0:LANES, LANES:] = cross
    work_ref[LANES:, 0:LANES] = cross.T
    tail = jnp.where(col < row, packed, flipped)
    work_ref[LANES:, LANES:] = jnp.where(col == row, jnp.broadcast_to(diag, tail.shape), tail)
    invert_factor(work_ref, block_ref, panel_ref, lower_ref, second_ref)
    lower = jnp.where(col <= row, 1.0, 0.0)
    first = work_ref[0:LANES, 0:LANES] * lower
    last = work_ref[LANES:, LANES:] * lower
    corner = work_ref[LANES:, 0:LANES]
    from_own = jnp.where(band == 0, first, last)
    from_other = jnp.where(band == 0, jnp.zeros_like(corner), corner)
    weights = jnp.concatenate([from_own, from_other], 1)
    high = weights.astype(bf16)
    low = (weights - high.astype(f32)).astype(bf16)
    weights = jnp.concatenate([high, low], 0)
    chunk = own_ref.shape[0] // sems.shape[0]
    copies = []
    for c in range(sems.shape[0]):
        rows = pl.ds(c * chunk, chunk)
        both = jnp.concatenate([own_ref[rows, :], other_ref[rows, :]], 1)
        product = lax.dot_general(
            both, weights, (((1,), (1,)), ((), ())), preferred_element_type=f32
        )
        result_ref[rows, :] = product[:, :LANES] + product[:, LANES:]
        copies.append(pltpu.make_async_copy(result_ref.at[rows], out_ref.at[rows], sems.at[c]))
        copies[-1].start()
    for copy in copies:
        copy.wait()


def rotate(band, inv_count, mine, theirs, own, other):
    return pl.pallas_call(
        rotate_kernel,
        out_shape=jax.ShapeDtypeStruct(own.shape, f32),
        in_specs=[smem, smem] + [vmem] * 4,
        out_specs=hbm,
        scratch_shapes=[
            pltpu.VMEM((2 * LANES, 2 * LANES), f32),
            pltpu.VMEM((PANEL, PANEL + HALF, LANES), f32),
            pltpu.VMEM((2, PANEL + HALF, LANES), f32),
            pltpu.VMEM((HALF, 2 * HALF, LANES), f32),
            pltpu.VMEM((HALF, 2 * HALF, LANES), f32),
            pltpu.VMEM(own.shape, f32),
            pltpu.SemaphoreType.DMA((8,)),
        ],
        compiler_params=grant(12),
    )(band, inv_count, mine, theirs, own, other)


def summed_over(value, axis):
    size = lax.axis_size(axis)
    if size & (size - 1):
        return lax.psum(value, axis)
    stride = 1
    while stride < size:
        count = min(4, size // stride)
        parts = [
            lax.ppermute(value, axis, [(i, i ^ (k * stride)) for i in range(size)])
            for k in range(1, count)
        ]
        value = value + sum(parts[1:], parts[0])
        stride *= count
    return value


def swapped(value):
    return lax.ppermute(value, "band", [(0, 1), (1, 0)])


def on_device(wavefunctions, bounds, cell_matrix, cell_scale, potential, cell_nodes, face_nodes):
    nodes = wavefunctions.shape[0]
    cell_matrix = pltpu.with_memory_space_constraint(cell_matrix, pltpu.HBM)
    cell_scale = pltpu.with_memory_space_constraint(cell_scale, pltpu.HBM)
    lists = pltpu.with_memory_space_constraint(face_nodes, pltpu.HBM)
    held = pltpu.with_memory_space_constraint(wavefunctions, pltpu.HBM)
    faces = jnp.where(face_nodes < 0, nodes, face_nodes).reshape(-1)
    potential = potential.reshape(-1, LANES)
    at = lax.axis_index("dom").astype(jnp.int32)
    band = lax.axis_index("band").astype(jnp.int32)
    kind = jnp.arange(4, dtype=jnp.int32) ^ (2 * band)
    flip = jnp.where(kind < 2, at % 2, at // 2 % 2)
    side = kind // 2 * 2 + ((kind % 2) ^ flip)
    pairs = exchange_pairs(lax.axis_size("dom"))

    def exchanged(blocks):
        return [
            lax.ppermute(
                block,
                ("dom", "band"),
                [(2 * i + b, 2 * j + b) for b in range(2) for i, j in pairs[q ^ (2 * b)]],
            )
            for q, block in enumerate(blocks)
        ]

    cells = functools.partial(apply_cells, side, cell_nodes.reshape(-1), cell_scale, cell_matrix)
    blocks, vectors = send_faces(side, lists, held)
    own, *sums = cells(vectors, exchanged(blocks))
    degree_one, *blocks = finish_first(
        side, faces, bounds, own, potential, vectors, exchanged(sums)
    )
    own, *sums = cells(degree_one, exchanged(blocks))
    degree_two = finish_second(
        side, faces, bounds, own, potential, degree_one, exchanged(sums), wavefunctions
    )
    other = swapped(degree_two)
    band = band.reshape(1)
    mine = summed_over(margin_rows(band, degree_two, other), "dom")
    inv_count = jnp.full((1,), 1.0 / (nodes * lax.axis_size("dom")), f32)
    return rotate(band, inv_count, mine, swapped(mine), degree_two, other)


def solution(mesh):
    return jax.shard_map(
        on_device,
        mesh=mesh,
        in_specs=(
            P(("kpt", "dom"), "band"),
            P("kpt"),
            P(),
            P("dom"),
            P("dom"),
            P("dom", None),
            P("dom", None),
        ),
        out_specs=P(("kpt", "dom"), "band"),
        check_vma=False,
    )
```
